128 devices in a mesh: gx: 16 (over z, y), gy: 8 (over x, core).
Axes of the slice: x: 4, y: 4, z: 4, core: 2. Of those that a mesh axis runs over, the one named last changes fastest.
Arguments:
- state: float32 [512, 512, 128], P('gx', 'gy'), may hold values from -6 to 6
- syndromes: int32 [2, 512, 512], P(None, 'gx', 'gy'), may hold values from 0 to 1
- erased: int32 [2, 128, 128], P(None, 'gx', 'gy'), may hold values 0 or 1
- readers: int32 [16384, 1], P(('gx', 'gy')), may hold values from 0 to 127; in each aligned block of 128 rows (0 to 127, 128 to 255, ...) at most 2 rows name the same one
- conv_weight: float32 [9, 128, 128], replicated, may hold values from -0.1875 to 0.1875
- syndrome_table: float32 [2, 128], replicated, may hold values from -6 to 6
- erasure_vector: float32 [128], replicated, may hold values from -6 to 6
- read_weight: float32 [16384, 128], P(('gx', 'gy')), may hold values from -0.5 to 0.5
- erasure_offset: float32 [128], replicated, may hold values from -6 to 6
Outputs:
- final_state: float32 [512, 512, 128], P('gx', 'gy')
The draws below stay inside these ranges and needn't reach their ends.
Inputs may be any that keep to these rules, and one draw needn't show every extreme that they name: `readers`: among the 128 blocks of one device no reader is named more than 2 times, a bound that some block reaches.
All inputs are finite; a program needn't handle non-finite values. No bound on the sum of `erased` on one device may be relied on, other than what follows from the above.
Results may differ from the reference program's by a relative error of at most 0.0003.
Values sent between devices are 32-bit elements; how exact they have to be, the bound alone decides.
No kernel may reach another device: no remote copies, remote signals or barrier semaphores. Data moves between devices by JAX's collectives and lax.ppermute only.
A program may use at most 64 MiB of HBM per device.

```python
import math
import jax
import jax.numpy as jnp
import numpy as np
from jax import lax

C = 128
TR = 32
TC = 64
BS = 4
ROUNDS = 2
NR = 512
NC = 512
NBR = 128
NBC = 128
BLK_DEV = 128
CAP = 2
N_GX = 16
N_GY = 8
DEVICES = 128


def with_ends(values, own_key, least, largest):
    extent = values.shape
    index_at = [jax.random.randint(jax.random.fold_in(own_key, axis), (), 0, extent[axis]) for axis in range(len(extent))]
    values = values.at[tuple(index_at)].set(least)
    longest = extent.index(max(extent))
    index_at[longest] = (index_at[longest] + 1) % extent[longest]
    return values.at[tuple(index_at)].set(largest)


def steps_of(stream_key, dims, split, least, high):
    loudness = 1.0
    for axis_at, blocks in split:
        steps = jax.random.uniform(jax.random.fold_in(jax.random.fold_in(stream_key, 6), axis_at), (blocks,), jnp.float32, least / len(split), high / len(split))
        loudness = loudness * jnp.repeat(jnp.exp(steps), dims[axis_at] // blocks).reshape((-1,) + (1,) * (len(dims) - 1 - axis_at))
    return loudness


def shared_out(key, own, number, rows, number_of, top, limit, lean):
    ranking = jax.random.permutation(key, number_of)
    heavy_load, usual = load_shares(number_of, rows * top, limit, lean, True), load_shares(number_of, rows * top, limit, lean, False)
    places = jnp.arange(number_of)

    def named(lengths, offset_by):
        used = int((lengths > 0).sum())
        fixed = max(1, used // 4)
        moved = fixed + (places - fixed + offset_by * (used - fixed)) % max(1, number_of - fixed)
        return jnp.zeros((number_of,), jnp.int32).at[ranking[jnp.where(places < fixed, places, moved)]].set(jnp.asarray(lengths, jnp.int32))

    lengths = jnp.where(number % 4 == 0, named(heavy_load, number // 4), named(usual, number - number // 4 - 1))
    mixed = jax.random.permutation(jax.random.fold_in(own, 3), number_of)
    giver, sink = mixed[0:number_of // 2 * 2:2], mixed[1:number_of // 2 * 2:2]
    slack = jnp.minimum(lengths[giver] - 1, limit - lengths[sink]) // 2
    slack = jnp.where((giver == ranking[0]) | (sink == ranking[0]) | (lengths[sink] == 0), 0, jnp.maximum(slack, 0))
    moved = jax.random.randint(jax.random.fold_in(own, 4), (number_of // 2,), 0, 1 << 20) % (slack + 1)
    lengths = lengths.at[giver].add(-moved).at[sink].add(moved)
    labels = jnp.searchsorted(jnp.cumsum(lengths), jnp.arange(rows * top), side="right").astype(jnp.int32)
    grid = labels.reshape(top, rows).T
    grid = grid[jax.random.permutation(jax.random.fold_in(own, 1), rows)]
    offset_by = jax.random.randint(jax.random.fold_in(own, 2), (rows, 1), 0, top)
    return jnp.take_along_axis(grid, (jnp.arange(top)[None, :] + offset_by) % top, axis=1)


def load_shares(number_of, total, most, lean, full):
    portions = [(1 << 20) // math.isqrt(standing ** lean) + 1 for standing in range(1, number_of + 1)]
    largest = most if full else min(most, max(-(-total // number_of), total * portions[0] // sum(portions)))
    least = 1 if total - largest >= number_of - 1 else 0
    counts, rest = [largest] + [least] * (number_of - 1), total - largest - least * (number_of - 1)
    while rest > 0:
        free = [i for i in range(1, number_of) if counts[i] < largest] or [i for i in range(1, number_of) if counts[i] < most]
        whole, budget = sum([portions[i] for i in free]), rest
        for i in free:
            more = min(most - counts[i], max(1, budget * portions[i] // whole), rest)
            counts[i] = counts[i] + more
            rest = rest - more
    return np.array(counts)


def scatter_about(key, dims, deviation, limit, shards=(), held_as=jnp.bfloat16):
    gain = steps_of(key, dims, shards, -0.22, 0.18) if shards else 1.0
    array = jax.random.normal(key, dims, jnp.float32) * deviation * gain
    return jnp.minimum(jnp.maximum(array, -limit), limit).astype(held_as)


def setup_inputs(seed: int = 0) -> dict:
    streams_of = jax.random.split(jax.random.key(seed), 10)
    state = scatter_about(streams_of[0], (NR, NC, C), 1.0, 6.0, ((0, 16), (1, 8)), jnp.float32)
    syndromes = with_ends(jax.random.randint(streams_of[1], (ROUNDS, NR, NC), 0, 2), jax.random.fold_in(streams_of[1], 1), 0, 1).astype(jnp.int32)
    erased = with_ends((jax.random.randint(streams_of[2], (ROUNDS, NBR, NBC), 0, 4) < 1).astype(jnp.int32), jax.random.fold_in(streams_of[2], 1), 0, 1)
    readers_keys = jax.random.split(jax.random.fold_in(streams_of[3], 1), (DEVICES * BLK_DEV) // BLK_DEV)
    readers_turns = jax.random.permutation(jax.random.fold_in(streams_of[3], 3), (DEVICES * BLK_DEV) // BLK_DEV)
    readers = jax.vmap(lambda own, number: shared_out(jax.random.fold_in(streams_of[3], 2), own, number, BLK_DEV, DEVICES, 1, CAP, 2))(readers_keys, readers_turns).reshape((DEVICES * BLK_DEV, 1))
    conv_weight = scatter_about(streams_of[4], (9, C, C), (9 * C) ** -0.5, 0.1875, (), jnp.float32)
    syndrome_table = scatter_about(streams_of[5], (2, C), 1.0, 6.0, (), jnp.float32)
    erasure_vector = scatter_about(streams_of[6], (C,), 1.0, 6.0, (), jnp.float32)
    read_weight = scatter_about(streams_of[7], (DEVICES * C, C), C ** -0.5, 0.5, ((0, 128),), jnp.float32)
    erasure_offset = scatter_about(streams_of[8], (C,), 1.0, 6.0, (), jnp.float32)
    return {"state": state, "syndromes": syndromes, "erased": erased, "readers": readers, "conv_weight": conv_weight, "syndrome_table": syndrome_table, "erasure_vector": erasure_vector, "read_weight": read_weight, "erasure_offset": erasure_offset}


precise = lax.Precision.HIGHEST


def convolve(field, conv_weight):
    row_count, col_count, channels = field.shape
    padded = jnp.pad(field, ((1, 1), (1, 1), (0, 0)))

    def one_slab(slab_index):
        slab = lax.dynamic_slice_in_dim(padded, slab_index * TR, TR + 2, 0)
        conv_sum = jnp.zeros((TR * col_count, channels), jnp.float32)
        for tap_index in range(9):
            row_off = tap_index // 3
            col_off = tap_index % 3
            shifted = slab[row_off:row_off + TR, col_off:col_off + col_count].reshape(-1, channels)
            conv_sum = conv_sum + jnp.dot(shifted, conv_weight[tap_index], precision=precise, preferred_element_type=jnp.float32)
        return conv_sum.reshape(TR, col_count, channels)

    slabs = lax.map(one_slab, jnp.arange(row_count // TR, dtype=jnp.int32))
    return slabs.reshape(row_count, col_count, channels)


def device_order(values):
    per_rows = TR // BS
    per_cols = TC // BS
    width = values.shape[-1]
    shaped = values.reshape(N_GX, per_rows, N_GY, per_cols, width)
    return shaped.transpose(0, 2, 1, 3, 4).reshape(N_GX * N_GY * per_rows * per_cols, width)


def grid_order(values):
    per_rows = TR // BS
    per_cols = TC // BS
    width = values.shape[-1]
    shaped = values.reshape(N_GX, N_GY, per_rows, per_cols, width)
    return shaped.transpose(0, 2, 1, 3, 4).reshape(NBR, NBC, width)


def spread_cells(values):
    width = values.shape[-1]
    block_grid = values.reshape(NBR, 1, NBC, 1, width)
    return jnp.broadcast_to(block_grid, (NBR, BS, NBC, BS, width)).reshape(NBR * BS, NBC * BS, width)


def reference(state, syndromes, erased, readers, conv_weight, syndrome_table, erasure_vector, read_weight, erasure_offset):
    field = state
    all_weights = read_weight.reshape(DEVICES, C, C)
    reader_rows = readers[:, 0].reshape(DEVICES, BLK_DEV)
    for round_index in range(ROUNDS):
        block_grid = field.reshape(NBR, BS, NBC, BS, C).transpose(0, 2, 1, 3, 4).reshape(NBR, NBC, BS * BS * C)
        block_states = device_order(block_grid).reshape(DEVICES, BLK_DEV, BS * BS * C)
        flag_grid = erased[round_index].astype(jnp.float32)[:, :, None]
        block_flags = device_order(flag_grid).reshape(DEVICES, BLK_DEV, 1)

        def one_device(items):
            states_part, flags_part, readers_part = items
            weights_part = all_weights[readers_part]
            cell_vals = states_part.reshape(BLK_DEV, BS * BS, C)
            mixed_vals = jnp.tanh(jnp.einsum("bpc,bcd->bpd", cell_vals, weights_part, precision=precise))
            return jnp.tanh(jnp.mean(mixed_vals, axis=1) + flags_part * erasure_offset)

        corrections = lax.map(one_device, (block_states, block_flags, reader_rows))
        correction_cells = spread_cells(grid_order(corrections.reshape(DEVICES * BLK_DEV, C)))
        conv_sum = convolve(field, conv_weight)
        erased_cells = spread_cells(erased[round_index][:, :, None])
        bits = syndromes[round_index][:, :, None]
        inputs = jnp.where(erased_cells > 0, erasure_vector, jnp.where(bits == 1, syndrome_table[1], syndrome_table[0]))
        field = 0.5 * field + jnp.tanh(conv_sum + inputs + correction_cells)
    return field
```

```python
import jax
import jax.numpy as jnp
from jax import lax
from jax.experimental import pallas as pl
from jax.experimental.pallas import tpu as pltpu
from jax.sharding import PartitionSpec as P

BS = 4
C = 128
TR = 32
TC = 64
HALO = 4
WIDE = TC + 2 * HALO
TALL = TR + 2 * HALO
BROWS = TALL // BS
BCOLS = WIDE // BS
GROUPS = WIDE // 8
CONV_ROWS = TR + 4
AX = ("gx", "gy")


def flat_id(z, y, x, c):
    return ((z % 4 * 4 + y % 4) * 4 + x % 4) * 2 + c


SITES = [
    (z, y, x, c) for z in range(4) for y in range(4) for x in range(4) for c in range(2)
]


def class_groups():
    groups = {}
    for z, y, x, c in SITES:
        groups.setdefault(((x + z) % 2, (y + z) % 2, c), []).append(flat_id(z, y, x, c))
    return [groups[k] for k in sorted(groups)]


def moved(dz, dy, dx):
    return [
        (flat_id(z, y, x, c), flat_id(z + dz, y + dy, x + dx, c)) for z, y, x, c in SITES
    ]


PARTNER = [(flat_id(z, y, x, c), flat_id(z, y, x, 1 - c)) for z, y, x, c in SITES]


def gather_weights(shard):
    copies = jnp.broadcast_to(shard[None], (16, C, C))
    own = lax.all_to_all(copies, AX, 0, 0, tiled=True, axis_index_groups=class_groups())
    low, high = own[:8], own[8:]
    pieces = [own]
    for step in ((0, 0, 1), (0, 1, 0), (1, 0, 0)):
        back = tuple(-s for s in step)
        pieces.append(lax.ppermute(low, AX, moved(*step)))
        pieces.append(lax.ppermute(high, AX, moved(*back)))
    return pieces + [lax.ppermute(piece, AX, PARTNER) for piece in pieces]


def slots_of(ids):
    me = lax.axis_index("gx") * 8 + lax.axis_index("gy")

    def place(n):
        return n // 32, n // 8 % 4, n // 2 % 4, n % 2

    z, y, x, c = place(ids)
    mz, my, mx, mc = place(me)
    side = (x + z + mx + mz) % 2 + 2 * ((y + z + my + mz) % 2)
    return (((c + mc) % 2) * 4 + side) * 16 + z * 4 + y // 2 * 2 + x // 2


def split(value):
    high = value.astype(jnp.bfloat16)
    return high, (value - high.astype(jnp.float32)).astype(jnp.bfloat16)


def conv_chunk(read, weights, rows):
    highs, lows = [], []
    for a in range(3):
        high, low = split(read(a).reshape(rows * WIDE, C))
        highs.append(high)
        lows.append(low)
    left = jnp.concatenate(highs + highs + lows, axis=1)
    sums = jnp.dot(left, weights, preferred_element_type=jnp.float32)
    sums = sums.reshape(rows, WIDE, 3 * C)
    return (
        pltpu.roll(sums[:, :, :C], 1, 1)
        + sums[:, :, C : 2 * C]
        + pltpu.roll(sums[:, :, 2 * C :], WIDE - 1, 1)
    )


def first_kernel(
    state, top, bottom, right, left, taps, inputs, ext_out, pre_out, weights_out
):
    ext_out[HALO : HALO + TR, :TC] = state[...]
    ext_out[:HALO, :TC] = top[: HALO * TC].reshape(HALO, TC, C)
    ext_out[HALO + TR :, :TC] = bottom[: HALO * TC].reshape(HALO, TC, C)
    both = jnp.concatenate(
        [
            right[: TALL * HALO].reshape(TALL, HALO, C),
            left[: TALL * HALO].reshape(TALL, HALO, C),
        ],
        axis=1,
    )
    ext_out[:, TC:] = both
    for a in range(3):
        for b in range(3):
            high, low = split(taps[3 * a + b])
            cols = slice(b * C, (b + 1) * C)
            weights_out[a * C : (a + 1) * C, cols] = high
            weights_out[(3 + a) * C : (4 + a) * C, cols] = low
            weights_out[(6 + a) * C : (7 + a) * C, cols] = high
    rows = 12

    def step(i, carry):
        start = i * rows
        pre_out[pl.ds(start, rows)] = (
            conv_chunk(
                lambda a: ext_out[pl.ds(start + 1 + a, rows)], weights_out[...], rows
            )
            + inputs[pl.ds(start, rows)]
        )
        return carry

    lax.fori_loop(0, CONV_ROWS // rows, step, 0)


def group_sum(total, sub):
    near = jnp.where(sub % 2 == 0, pltpu.roll(total, 7, 0), pltpu.roll(total, 1, 0))
    total = total + near
    far = jnp.where(sub % 4 < 2, pltpu.roll(total, 6, 0), pltpu.roll(total, 2, 0))
    return total + far


def readout(sites, right, flag_a, flag_b, offset, sub):
    high, low = split(sites.reshape(32, C))
    left = jnp.concatenate(
        [jnp.concatenate([high, high], axis=1), jnp.concatenate([low, low], axis=1)],
        axis=0,
    )
    mixed = jnp.dot(left, right, preferred_element_type=jnp.float32)
    mixed = (mixed[:32] + mixed[32:]).reshape(4, 8, 2 * C)
    mixed = jnp.tanh(jnp.where(sub[None] < 4, mixed[:, :, :C], mixed[:, :, C:]))
    total = mixed[0] + mixed[1] + mixed[2] + mixed[3]
    flags = jnp.where(sub < 4, flag_a, flag_b)
    return jnp.tanh(group_sum(total, sub) * 0.0625 + flags * offset)


PIECES = (16, 8, 8, 8, 8, 8, 8) * 2


def second_kernel(
    slots, flags, inside, ext, pre, inputs, weights, offset, *rest
):
    pieces, (out, table, pairs, first, field, second, sems) = rest[:14], rest[14:]
    copies = []
    at = 0
    for i, (piece, count) in enumerate(zip(pieces, PIECES)):
        copies.append(
            pltpu.make_async_copy(piece, table.at[pl.ds(at, count)], sems.at[i])
        )
        at += count
    for copy in copies:
        copy.start()
    for copy in copies:
        copy.wait()
    sub = lax.broadcasted_iota(jnp.int32, (8, C), 0)
    shift = offset[...]

    def read_first(br, carry):
        for g in range(GROUPS):
            b = br * BCOLS + 2 * g
            high_a, low_a = split(table[slots[b]])
            high_b, low_b = split(table[slots[b + 1]])
            right = jnp.concatenate(
                [
                    jnp.concatenate([high_a, high_b], axis=1),
                    jnp.concatenate([low_a, low_b], axis=1),
                ],
                axis=0,
            )
            pairs[br * GROUPS + g] = right
            first[br, 8 * g : 8 * g + 8] = readout(
                ext[pl.ds(br * BS, BS), 8 * g : 8 * g + 8],
                right,
                flags[b].astype(jnp.float32),
                flags[b + 1].astype(jnp.float32),
                shift,
                sub,
            )
        return carry

    lax.fori_loop(0, BROWS, read_first, 0)

    def update(row, br):
        field[row + 1] = 0.5 * ext[row + HALO] + jnp.tanh(pre[row + 2] + first[br])

    column = lax.broadcasted_iota(jnp.int32, (WIDE, C), 0)

    update(-1, 0)
    update(TR, BROWS - 1)

    def update_block(br, carry):
        for r in range(BS):
            update(br * BS + r, br + 1)
        return carry

    lax.fori_loop(0, TR // BS, update_block, 0)
    field[0] = field[0] * inside[0].astype(jnp.float32)
    field[TR + 1] = field[TR + 1] * inside[1].astype(jnp.float32)
    edge = lax.broadcasted_iota(jnp.int32, (TR + 2, 8, C), 1)
    kept = jnp.where(edge < 4, inside[2].astype(jnp.float32), inside[3].astype(jnp.float32))
    field[:, TC:] = field[:, TC:] * kept

    def read_second(br, carry):
        for g in range(TC // 8):
            b = (br + 1) * BCOLS + 2 * g
            second[br, 8 * g : 8 * g + 8] = readout(
                field[pl.ds(br * BS + 1, BS), 8 * g : 8 * g + 8],
                pairs[(br + 1) * GROUPS + g],
                flags[BROWS * BCOLS + b].astype(jnp.float32),
                flags[BROWS * BCOLS + b + 1].astype(jnp.float32),
                shift,
                sub,
            )
        return carry

    lax.fori_loop(0, TR // BS, read_second, 0)
    rows = 8

    def finish(i, carry):
        start = i * rows
        sums = conv_chunk(
            lambda a: field[pl.ds(start + a, rows)], weights[...], rows
        )[:, :TC]
        for half in range(rows // BS):
            at = start + half * BS
            out[pl.ds(at, BS)] = 0.5 * field[pl.ds(at + 1, BS), :TC] + jnp.tanh(
                sums[half * BS : (half + 1) * BS]
                + inputs[pl.ds(at, BS)]
                + second[i * (rows // BS) + half][None]
            )
        return carry

    lax.fori_loop(0, TR // rows, finish, 0)


def meta_row(*parts):
    joined = jnp.concatenate([p.reshape(-1).astype(jnp.float32) for p in parts])
    return jnp.pad(joined[None], ((0, 7), (0, C - joined.shape[0])))


def per_device(
    state,
    syndromes,
    erased,
    readers,
    conv_weight,
    syndrome_table,
    erasure_vector,
    read_weight,
    erasure_offset,
):
    f32 = jnp.float32
    pieces = gather_weights(read_weight)
    gx, gy = lax.axis_index("gx"), lax.axis_index("gy")
    gx_count, gy_count = lax.axis_size("gx"), lax.axis_size("gy")
    block_rows, block_cols = TR // BS, TC // BS
    ids = readers.reshape(block_rows, block_cols)
    bits, lost = syndromes[0], erased[0]

    def row_pay(row, block_row):
        cells = lax.slice_in_dim(state, row, row + HALO, axis=0).reshape(HALO * TC, C)
        edge = 0 if row == 0 else TR - 1
        return jnp.concatenate(
            [cells, meta_row(bits[edge], lost[block_row], ids[block_row])], axis=0
        )

    up = [(i, i - 1) for i in range(1, gx_count)]
    down = [(i, i + 1) for i in range(gx_count - 1)]
    top = lax.ppermute(row_pay(TR - HALO, block_rows - 1), "gx", down)
    bottom = lax.ppermute(row_pay(0, 0), "gx", up)

    def meta(pay, start, count):
        return pay[-8, start : start + count].astype(jnp.int32)

    def stack(mid, start, count):
        return jnp.concatenate(
            [meta(top, start, count)[None], mid, meta(bottom, start, count)[None]], axis=0
        )

    bits_tall = stack(bits, 0, TC)
    lost_tall = stack(lost, TC, block_cols)
    ids_tall = stack(ids, TC + block_cols, block_cols)

    def col_pay(col):
        def cut(cells):
            return lax.slice_in_dim(cells, col, col + HALO, axis=1)

        cells = jnp.concatenate(
            [
                cut(top[: HALO * TC].reshape(HALO, TC, C)),
                cut(state),
                cut(bottom[: HALO * TC].reshape(HALO, TC, C)),
            ],
            axis=0,
        ).reshape(TALL * HALO, C)
        edge = 0 if col == 0 else -1
        return jnp.concatenate(
            [cells, meta_row(bits_tall[:, edge], lost_tall[:, edge], ids_tall[:, edge])],
            axis=0,
        )

    west = [(i, i - 1) for i in range(1, gy_count)]
    east = [(i, i + 1) for i in range(gy_count - 1)]
    left = lax.ppermute(col_pay(TC - HALO), "gy", east)
    right = lax.ppermute(col_pay(0), "gy", west)

    tall = TR + 2
    bits_wide = jnp.concatenate(
        [
            bits_tall,
            meta(right, 0, tall)[:, None],
            jnp.zeros((tall, 6), jnp.int32),
            meta(left, 0, tall)[:, None],
        ],
        axis=1,
    )
    bits_wide = jnp.pad(bits_wide, ((1, 1), (0, 0)))

    def widen(mid, start):
        return jnp.concatenate(
            [mid, meta(right, start, BROWS)[:, None], meta(left, start, BROWS)[:, None]],
            axis=1,
        )

    lost_wide = widen(lost_tall, tall)
    ids_wide = widen(ids_tall, tall + BROWS)

    def embed(bits_at, lost_at):
        return jnp.where(
            lost_at[:, :, None] > 0,
            erasure_vector,
            jnp.where(bits_at[:, :, None] == 1, syndrome_table[1], syndrome_table[0]),
        )

    def sites(blocks):
        return jnp.repeat(jnp.repeat(blocks, BS, axis=0), BS, axis=1)

    inputs_first = embed(bits_wide, sites(lost_wide)[2 : 2 + CONV_ROWS])
    inputs_second = embed(syndromes[1], sites(erased[1]))

    vmem = pl.BlockSpec(memory_space=pltpu.VMEM)
    smem = pl.BlockSpec(memory_space=pltpu.SMEM)
    anywhere = pl.BlockSpec(memory_space=pl.ANY)
    ext, pre, weights = pl.pallas_call(
        first_kernel,
        name="conv_first",
        out_shape=(
            jax.ShapeDtypeStruct((TALL, WIDE, C), f32),
            jax.ShapeDtypeStruct((CONV_ROWS, WIDE, C), f32),
            jax.ShapeDtypeStruct((9 * C, 3 * C), jnp.bfloat16),
        ),
        in_specs=[vmem] * 7,
        out_specs=(vmem, vmem, vmem),
        cost_estimate=pl.CostEstimate(
            flops=2_000_000_000, bytes_accessed=6_000_000, transcendentals=0
        ),
    )(state, top, bottom, right, left, conv_weight, inputs_first)

    slots = slots_of(ids_wide).reshape(-1)
    lost_second = jnp.pad(erased[1], ((1, 1), (0, 2))).reshape(-1)
    flags = jnp.concatenate([lost_wide.reshape(-1), lost_second])
    inside = jnp.stack(
        [gx > 0, gx < gx_count - 1, gy < gy_count - 1, gy > 0]
    ).astype(jnp.int32)
    return pl.pallas_call(
        second_kernel,
        name="read_and_finish",
        out_shape=jax.ShapeDtypeStruct((TR, TC, C), f32),
        in_specs=[smem] * 3 + [vmem] * 5 + [anywhere] * 14,
        out_specs=vmem,
        scratch_shapes=[
            pltpu.VMEM((128, C, C), f32),
            pltpu.VMEM((BROWS * GROUPS, 2 * C, 2 * C), jnp.bfloat16),
            pltpu.VMEM((BROWS, WIDE, C), f32),
            pltpu.VMEM((TR + 2, WIDE, C), f32),
            pltpu.VMEM((TR // BS, TC, C), f32),
            pltpu.SemaphoreType.DMA((14,)),
        ],
        cost_estimate=pl.CostEstimate(
            flops=4_000_000_000, bytes_accessed=12_000_000, transcendentals=1_000_000
        ),
    )(
        slots,
        flags,
        inside,
        ext,
        pre,
        inputs_second,
        weights,
        erasure_offset[None],
        *pieces,
    )


def solution(mesh):
    placed = (
        P("gx", "gy", None),
        P(None, "gx", "gy"),
        P(None, "gx", "gy"),
        P(("gx", "gy"), None),
        P(),
        P(),
        P(),
        P(("gx", "gy"), None),
        P(),
    )
    return jax.shard_map(
        per_device, mesh=mesh, in_specs=placed, out_specs=P("gx", "gy", None), check_vma=False
    )
```

```python
import jax
import jax.numpy as jnp
from jax import lax
from jax.experimental import pallas as pl
from jax.experimental.pallas import tpu as pltpu
from jax.sharding import PartitionSpec as P


BS = 4
C = 128
TR = 32
TC = 64
HALO = 4
WIDE = TC + 2 * HALO
TALL = TR + 2 * HALO
BROWS = TALL // BS
BCOLS = WIDE // BS
GROUPS = WIDE // 8
CONV_ROWS = TR + 4
AX = ("gx", "gy")


def flat_id(z, y, x, c):
    return ((z % 4 * 4 + y % 4) * 4 + x % 4) * 2 + c


SITES = [
    (z, y, x, c) for z in range(4) for y in range(4) for x in range(4) for c in range(2)
]


def class_groups():
    groups = {}
    for z, y, x, c in SITES:
        groups.setdefault(((x + z) % 2, (y + z) % 2, c), []).append(flat_id(z, y, x, c))
    return [groups[k] for k in sorted(groups)]


def moved(dz, dy, dx):
    return [
        (flat_id(z, y, x, c), flat_id(z + dz, y + dy, x + dx, c)) for z, y, x, c in SITES
    ]


PARTNER = [(flat_id(z, y, x, c), flat_id(z, y, x, 1 - c)) for z, y, x, c in SITES]


def gather_weights(shard):
    copies = jnp.broadcast_to(shard[None], (16, C, C))
    own = lax.all_to_all(copies, AX, 0, 0, tiled=True, axis_index_groups=class_groups())
    low, high = own[:8], own[8:]
    pieces = [own]
    for step in ((0, 0, 1), (0, 1, 0), (1, 0, 0)):
        back = tuple(-s for s in step)
        pieces.append(lax.ppermute(low, AX, moved(*step)))
        pieces.append(lax.ppermute(high, AX, moved(*back)))
    pieces += [lax.ppermute(piece, AX, PARTNER) for piece in pieces]
    return pieces


def slots_of(ids):
    me = lax.axis_index("gx") * 8 + lax.axis_index("gy")

    def place(n):
        return n // 32, n // 8 % 4, n // 2 % 4, n % 2

    z, y, x, c = place(ids)
    mz, my, mx, mc = place(me)
    side = (x + z + mx + mz) % 2 + 2 * ((y + z + my + mz) % 2)
    return (((c + mc) % 2) * 4 + side) * 16 + z * 4 + y // 2 * 2 + x // 2


def split(value):
    high = value.astype(jnp.bfloat16)
    return high, (value - high.astype(jnp.float32)).astype(jnp.bfloat16)


def conv_chunk(read, weights, rows):
    highs, lows = [], []
    for a in range(3):
        high, low = split(read(a).reshape(rows * WIDE, C))
        highs.append(high)
        lows.append(low)
    left = jnp.concatenate(highs + highs + lows, axis=1)
    sums = jnp.dot(left, weights, preferred_element_type=jnp.float32)
    sums = sums.reshape(rows, WIDE, 3 * C)
    return (
        pltpu.roll(sums[:, :, :C], 1, 1)
        + sums[:, :, C : 2 * C]
        + pltpu.roll(sums[:, :, 2 * C :], WIDE - 1, 1)
    )


def first_kernel(
    state, top, bottom, right, left, taps, inputs, ext_out, pre_out, weights_out
):
    ext_out[HALO : HALO + TR, :TC] = state[...]
    ext_out[:HALO, :TC] = top[: HALO * TC].reshape(HALO, TC, C)
    ext_out[HALO + TR :, :TC] = bottom[: HALO * TC].reshape(HALO, TC, C)
    both = jnp.concatenate(
        [
            right[: TALL * HALO].reshape(TALL, HALO, C),
            left[: TALL * HALO].reshape(TALL, HALO, C),
        ],
        axis=1,
    )
    ext_out[:, TC:] = both
    for a in range(3):
        for b in range(3):
            high, low = split(taps[3 * a + b])
            cols = slice(b * C, (b + 1) * C)
            weights_out[a * C : (a + 1) * C, cols] = high
            weights_out[(3 + a) * C : (4 + a) * C, cols] = low
            weights_out[(6 + a) * C : (7 + a) * C, cols] = high
    rows = 12

    def step(i, carry):
        start = i * rows
        pre_out[pl.ds(start, rows)] = (
            conv_chunk(
                lambda a: ext_out[pl.ds(start + 1 + a, rows)], weights_out[...], rows
            )
            + inputs[pl.ds(start, rows)]
        )
        return carry

    lax.fori_loop(0, CONV_ROWS // rows, step, 0)


def group_sum(total, sub):
    near = jnp.where(sub % 2 == 0, pltpu.roll(total, 7, 0), pltpu.roll(total, 1, 0))
    total = total + near
    far = jnp.where(sub % 4 < 2, pltpu.roll(total, 6, 0), pltpu.roll(total, 2, 0))
    return total + far


def readout(sites, right, flag_a, flag_b, offset, sub):
    high, low = split(sites.reshape(32, C))
    left = jnp.concatenate(
        [jnp.concatenate([high, high], axis=1), jnp.concatenate([low, low], axis=1)],
        axis=0,
    )
    mixed = jnp.dot(left, right, preferred_element_type=jnp.float32)
    mixed = (mixed[:32] + mixed[32:]).reshape(4, 8, 2 * C)
    mixed = jnp.tanh(jnp.where(sub[None] < 4, mixed[:, :, :C], mixed[:, :, C:]))
    total = mixed[0] + mixed[1] + mixed[2] + mixed[3]
    flags = jnp.where(sub < 4, flag_a, flag_b)
    return jnp.tanh(group_sum(total, sub) * 0.0625 + flags * offset)


PIECES = (16, 8, 8, 8, 8, 8, 8) * 2


def second_kernel(
    slots, flags, inside, ext, pre, inputs, weights, offset, *rest
):
    pieces, (out, table, pairs, first, field, second, sems) = rest[:14], rest[14:]
    copies = []
    at = 0
    for i, (piece, count) in enumerate(zip(pieces, PIECES)):
        copies.append(
            pltpu.make_async_copy(piece, table.at[pl.ds(at, count)], sems.at[i])
        )
        at += count
    for copy in copies:
        copy.start()
    for copy in copies:
        copy.wait()
    sub = lax.broadcasted_iota(jnp.int32, (8, C), 0)
    shift = offset[...]

    def read_first(br, carry):
        for g in range(GROUPS):
            b = br * BCOLS + 2 * g
            high_a, low_a = split(table[slots[b]])
            high_b, low_b = split(table[slots[b + 1]])
            right = jnp.concatenate(
                [
                    jnp.concatenate([high_a, high_b], axis=1),
                    jnp.concatenate([low_a, low_b], axis=1),
                ],
                axis=0,
            )
            pairs[br * GROUPS + g] = right
            first[br, 8 * g : 8 * g + 8] = readout(
                ext[pl.ds(br * BS, BS), 8 * g : 8 * g + 8],
                right,
                flags[b].astype(jnp.float32),
                flags[b + 1].astype(jnp.float32),
                shift,
                sub,
            )
        return carry

    lax.fori_loop(0, BROWS, read_first, 0)

    def update(row, br):
        field[row + 1] = 0.5 * ext[row + HALO] + jnp.tanh(pre[row + 2] + first[br])

    column = lax.broadcasted_iota(jnp.int32, (WIDE, C), 0)

    update(-1, 0)
    update(TR, BROWS - 1)

    def update_block(br, carry):
        for r in range(BS):
            update(br * BS + r, br + 1)
        return carry

    lax.fori_loop(0, TR // BS, update_block, 0)
    field[0] = field[0] * inside[0].astype(jnp.float32)
    field[TR + 1] = field[TR + 1] * inside[1].astype(jnp.float32)
    edge = lax.broadcasted_iota(jnp.int32, (TR + 2, 8, C), 1)
    kept = jnp.where(edge < 4, inside[2].astype(jnp.float32), inside[3].astype(jnp.float32))
    field[:, TC:] = field[:, TC:] * kept

    def read_second(br, carry):
        for g in range(TC // 8):
            b = (br + 1) * BCOLS + 2 * g
            second[br, 8 * g : 8 * g + 8] = readout(
                field[pl.ds(br * BS + 1, BS), 8 * g : 8 * g + 8],
                pairs[(br + 1) * GROUPS + g],
                flags[BROWS * BCOLS + b].astype(jnp.float32),
                flags[BROWS * BCOLS + b + 1].astype(jnp.float32),
                shift,
                sub,
            )
        return carry

    lax.fori_loop(0, TR // BS, read_second, 0)
    rows = 8

    def finish(i, carry):
        start = i * rows
        sums = conv_chunk(
            lambda a: field[pl.ds(start + a, rows)], weights[...], rows
        )[:, :TC]
        for half in range(rows // BS):
            at = start + half * BS
            out[pl.ds(at, BS)] = 0.5 * field[pl.ds(at + 1, BS), :TC] + jnp.tanh(
                sums[half * BS : (half + 1) * BS]
                + inputs[pl.ds(at, BS)]
                + second[i * (rows // BS) + half][None]
            )
        return carry

    lax.fori_loop(0, TR // rows, finish, 0)


def meta_row(*parts):
    joined = jnp.concatenate([p.reshape(-1).astype(jnp.float32) for p in parts])
    return jnp.pad(joined[None], ((0, 7), (0, C - joined.shape[0])))


def decode(
    state,
    syndromes,
    erased,
    readers,
    conv_weight,
    syndrome_table,
    erasure_vector,
    read_weight,
    erasure_offset,
):
    f32 = jnp.float32
    pieces = gather_weights(read_weight)
    gx, gy = lax.axis_index("gx"), lax.axis_index("gy")
    gx_count, gy_count = lax.axis_size("gx"), lax.axis_size("gy")
    block_rows, block_cols = TR // BS, TC // BS
    ids = readers.reshape(block_rows, block_cols)
    bits, lost = syndromes[0], erased[0]

    def row_pay(row, block_row):
        cells = lax.slice_in_dim(state, row, row + HALO, axis=0).reshape(HALO * TC, C)
        edge = 0 if row == 0 else TR - 1
        return jnp.concatenate(
            [cells, meta_row(bits[edge], lost[block_row], ids[block_row])], axis=0
        )

    up = [(i, i - 1) for i in range(1, gx_count)]
    down = [(i, i + 1) for i in range(gx_count - 1)]
    top = lax.ppermute(row_pay(TR - HALO, block_rows - 1), "gx", down)
    bottom = lax.ppermute(row_pay(0, 0), "gx", up)

    def meta(pay, start, count):
        return pay[-8, start : start + count].astype(jnp.int32)

    def stack(mid, start, count):
        return jnp.concatenate(
            [meta(top, start, count)[None], mid, meta(bottom, start, count)[None]], axis=0
        )

    bits_tall = stack(bits, 0, TC)
    lost_tall = stack(lost, TC, block_cols)
    ids_tall = stack(ids, TC + block_cols, block_cols)

    def col_pay(col):
        def cut(cells):
            return lax.slice_in_dim(cells, col, col + HALO, axis=1)

        cells = jnp.concatenate(
            [
                cut(top[: HALO * TC].reshape(HALO, TC, C)),
                cut(state),
                cut(bottom[: HALO * TC].reshape(HALO, TC, C)),
            ],
            axis=0,
        ).reshape(TALL * HALO, C)
        edge = 0 if col == 0 else -1
        return jnp.concatenate(
            [cells, meta_row(bits_tall[:, edge], lost_tall[:, edge], ids_tall[:, edge])],
            axis=0,
        )

    west = [(i, i - 1) for i in range(1, gy_count)]
    east = [(i, i + 1) for i in range(gy_count - 1)]
    left = lax.ppermute(col_pay(TC - HALO), "gy", east)
    right = lax.ppermute(col_pay(0), "gy", west)

    tall = TR + 2
    bits_wide = jnp.concatenate(
        [
            bits_tall,
            meta(right, 0, tall)[:, None],
            jnp.zeros((tall, 6), jnp.int32),
            meta(left, 0, tall)[:, None],
        ],
        axis=1,
    )
    bits_wide = jnp.pad(bits_wide, ((1, 1), (0, 0)))

    def widen(mid, start):
        return jnp.concatenate(
            [mid, meta(right, start, BROWS)[:, None], meta(left, start, BROWS)[:, None]],
            axis=1,
        )

    lost_wide = widen(lost_tall, tall)
    ids_wide = widen(ids_tall, tall + BROWS)

    def embed(bits_at, lost_at):
        return jnp.where(
            lost_at[:, :, None] > 0,
            erasure_vector,
            jnp.where(bits_at[:, :, None] == 1, syndrome_table[1], syndrome_table[0]),
        )

    def sites(blocks):
        return jnp.repeat(jnp.repeat(blocks, BS, axis=0), BS, axis=1)

    inputs_first = embed(bits_wide, sites(lost_wide)[2 : 2 + CONV_ROWS])
    inputs_second = embed(syndromes[1], sites(erased[1]))

    vmem = pl.BlockSpec(memory_space=pltpu.VMEM)
    smem = pl.BlockSpec(memory_space=pltpu.SMEM)
    anywhere = pl.BlockSpec(memory_space=pl.ANY)
    ext, pre, weights = pl.pallas_call(
        first_kernel,
        name="conv_first",
        out_shape=(
            jax.ShapeDtypeStruct((TALL, WIDE, C), f32),
            jax.ShapeDtypeStruct((CONV_ROWS, WIDE, C), f32),
            jax.ShapeDtypeStruct((9 * C, 3 * C), jnp.bfloat16),
        ),
        in_specs=[vmem] * 7,
        out_specs=(vmem, vmem, vmem),
        cost_estimate=pl.CostEstimate(
            flops=2_000_000_000, bytes_accessed=6_000_000, transcendentals=0
        ),
    )(state, top, bottom, right, left, conv_weight, inputs_first)

    slots = slots_of(ids_wide).reshape(-1)
    lost_second = jnp.pad(erased[1], ((1, 1), (0, 2))).reshape(-1)
    flags = jnp.concatenate([lost_wide.reshape(-1), lost_second])
    inside = jnp.stack(
        [gx > 0, gx < gx_count - 1, gy < gy_count - 1, gy > 0]
    ).astype(jnp.int32)
    return pl.pallas_call(
        second_kernel,
        name="read_and_finish",
        out_shape=jax.ShapeDtypeStruct((TR, TC, C), f32),
        in_specs=[smem] * 3 + [vmem] * 5 + [anywhere] * 14,
        out_specs=vmem,
        scratch_shapes=[
            pltpu.VMEM((128, C, C), f32),
            pltpu.VMEM((BROWS * GROUPS, 2 * C, 2 * C), jnp.bfloat16),
            pltpu.VMEM((BROWS, WIDE, C), f32),
            pltpu.VMEM((TR + 2, WIDE, C), f32),
            pltpu.VMEM((TR // BS, TC, C), f32),
            pltpu.SemaphoreType.DMA((14,)),
        ],
        cost_estimate=pl.CostEstimate(
            flops=4_000_000_000, bytes_accessed=12_000_000, transcendentals=1_000_000
        ),
    )(
        slots,
        flags,
        inside,
        ext,
        pre,
        inputs_second,
        weights,
        erasure_offset[None],
        *pieces,
    )


def solution(mesh):
    placed = (
        P("gx", "gy", None),
        P(None, "gx", "gy"),
        P(None, "gx", "gy"),
        P(("gx", "gy"), None),
        P(),
        P(),
        P(),
        P(("gx", "gy"), None),
        P(),
    )
    return jax.shard_map(
        decode, mesh=mesh, in_specs=placed, out_specs=P("gx", "gy", None), check_vma=False
    )
```

```python
import jax
import jax.numpy as jnp
from jax import lax
from jax.experimental import pallas as pl
from jax.experimental.pallas import tpu as pltpu
from jax.sharding import PartitionSpec as P


BS = 4
C = 128
TR = 32
TC = 64
HALO = 4
WIDE = TC + 2 * HALO
TALL = TR + 2 * HALO
BROWS = TALL // BS
GROUPS = WIDE // 8
CONV_ROWS = TR + 4
AX = ("gx", "gy")


def flat_id(z, y, x, c):
    return ((z % 4 * 4 + y % 4) * 4 + x % 4) * 2 + c


SITES = [
    (z, y, x, c) for z in range(4) for y in range(4) for x in range(4) for c in range(2)
]


def class_groups():
    groups = {}
    for z, y, x, c in SITES:
        groups.setdefault(((x + z) % 2, (y + z) % 2, c), []).append(flat_id(z, y, x, c))
    return [groups[k] for k in sorted(groups)]


def moved(dz, dy, dx):
    return [
        (flat_id(z, y, x, c), flat_id(z + dz, y + dy, x + dx, c)) for z, y, x, c in SITES
    ]


PARTNER = [(flat_id(z, y, x, c), flat_id(z, y, x, 1 - c)) for z, y, x, c in SITES]


def gather_weights(copies):
    own = lax.all_to_all(copies, AX, 0, 0, tiled=True, axis_index_groups=class_groups())
    low, high = own[:8], own[8:]
    pieces = [own]
    for step in ((0, 0, 1), (0, 1, 0), (1, 0, 0)):
        back = tuple(-s for s in step)
        pieces.append(lax.ppermute(low, AX, moved(*step)))
        pieces.append(lax.ppermute(high, AX, moved(*back)))
    pieces += [lax.ppermute(piece, AX, PARTNER) for piece in pieces]
    return pieces


def split(value):
    high = value.astype(jnp.bfloat16)
    return high, (value - high.astype(jnp.float32)).astype(jnp.bfloat16)


def conv_chunk(read, weights, rows):
    highs, lows = [], []
    for a in range(3):
        high, low = split(read(a).reshape(rows * WIDE, C))
        highs.append(high)
        lows.append(low)
    left = jnp.concatenate(highs + highs + lows, axis=1)
    sums = jnp.dot(left, weights, preferred_element_type=jnp.float32)
    sums = sums.reshape(rows, WIDE, 3 * C)
    return (
        pltpu.roll(sums[:, :, :C], 1, 1)
        + sums[:, :, C : 2 * C]
        + pltpu.roll(sums[:, :, 2 * C :], WIDE - 1, 1)
    )


def rows_kernel(
    state, weight, syndromes, erased, readers, up, down, copies, rows_sem, copies_sem
):
    moves = [
        pltpu.make_async_copy(state.at[pl.ds(0, HALO)], up.at[pl.ds(0, HALO)], rows_sem.at[0]),
        pltpu.make_async_copy(
            state.at[pl.ds(TR - HALO, HALO)], down.at[pl.ds(0, HALO)], rows_sem.at[1]
        ),
    ]
    moves += [
        pltpu.make_async_copy(weight, copies.at[i], copies_sem.at[i]) for i in range(16)
    ]
    for move in moves:
        move.start()
    ids = readers[...].astype(jnp.float32)
    for pay, row, block_row in ((up, 0, 0), (down, TR - 1, TR // BS - 1)):
        pay[HALO] = jnp.zeros((TC, C), jnp.float32)
        pay[HALO, 0:1, :TC] = syndromes[0, row : row + 1, :].astype(jnp.float32)
        pay[HALO, 1:2, : TC // BS] = erased[0, block_row : block_row + 1, :].astype(
            jnp.float32
        )
        first = block_row * (TC // BS)
        pay[HALO, 2:3, :] = pltpu.roll(ids, (C - first) % C, 1)
    for move in moves:
        move.wait()


def repeat_blocks(blocks, rows):
    count = blocks.shape[0]
    row = lax.broadcasted_iota(jnp.int32, (rows, count), 0)
    tall = (row // BS == lax.broadcasted_iota(jnp.int32, (rows, count), 1)).astype(jnp.bfloat16)
    col = lax.broadcasted_iota(jnp.int32, (TC // BS, TC), 1)
    wide = (col // BS == lax.broadcasted_iota(jnp.int32, (TC // BS, TC), 0)).astype(jnp.bfloat16)
    half = jnp.dot(tall, blocks.astype(jnp.bfloat16), preferred_element_type=jnp.float32)
    return jnp.dot(half.astype(jnp.bfloat16), wide, preferred_element_type=jnp.float32)


def embed(code, table, lost_vector):
    return jnp.where(
        code > 1.5, lost_vector, jnp.where(code > 0.5, table[1:2], table[0:1])
    )


def cols_kernel(
    state,
    top,
    bottom,
    syndromes,
    erased,
    readers,
    table,
    lost_vector,
    west,
    east,
    code_out,
    lost_out,
    ids_out,
    vectors,
):
    f32 = jnp.float32
    block_rows, block_cols = TR // BS, TC // BS
    lost_out[...] = jnp.zeros((16, C), f32)
    ids_out[...] = jnp.zeros((16, C), f32)
    code_out[...] = jnp.zeros((TALL, TC), f32)
    lost_out[0:1, :block_cols] = top[HALO, 1:2, :block_cols]
    lost_out[BROWS - 1 : BROWS, :block_cols] = bottom[HALO, 1:2, :block_cols]
    lost_out[1 : 1 + block_rows, :block_cols] = erased[0].astype(f32)
    lane = lax.broadcasted_iota(jnp.int32, (1, C), 1)
    ids_out[0:1, :] = jnp.where(lane < block_cols, top[HALO, 2:3, :], 0.0)
    ids_out[BROWS - 1 : BROWS, :] = jnp.where(lane < block_cols, bottom[HALO, 2:3, :], 0.0)
    ids = readers[...].astype(f32)
    for k in range(block_rows):
        turned = pltpu.roll(ids, (C - k * block_cols) % C, 1)
        ids_out[k + 1 : k + 2, :] = jnp.where(lane < block_cols, turned, 0.0)
    code_out[HALO - 1 : HALO, :] = top[HALO, 0:1, :TC]
    code_out[HALO : HALO + TR, :] = syndromes[0].astype(f32)
    code_out[HALO + TR : HALO + TR + 1, :] = bottom[HALO, 0:1, :TC]
    sites = repeat_blocks(lost_out[:, :block_cols], TALL)
    code_out[...] = jnp.where(sites > 0.5, 2.0, code_out[...])
    sub = lax.broadcasted_iota(jnp.int32, (8, C), 0)
    for pay, edge, keep, at in ((west, 0, sub < 4, 4), (east, TC - 1, sub >= 4, 0)):
        block = edge // BS
        group = edge // 8 * 8
        code = jnp.broadcast_to(code_out[:, edge : edge + 1], (TALL, C))
        vectors[:TALL] = embed(code, table, lost_vector[...])
        vectors[TALL : TALL + 16] = jnp.broadcast_to(lost_out[:, block : block + 1], (16, C))
        vectors[TALL + 16 :] = jnp.broadcast_to(ids_out[:, block : block + 1], (16, C))
        _, second, third = (4, 5, 6) if at == 4 else (3, 2, 1)
        for r in range(TALL):
            if r < HALO:
                cells = top[r, group : group + 8]
            elif r < HALO + TR:
                cells = state[r - HALO, group : group + 8]
            else:
                cells = bottom[r - HALO - TR, group : group + 8]
            extra = jnp.broadcast_to(vectors[r : r + 1], (8, C))
            if r < BROWS:
                flag = jnp.broadcast_to(vectors[TALL + r : TALL + r + 1], (8, C))
                name = jnp.broadcast_to(vectors[TALL + 16 + r : TALL + 17 + r], (8, C))
                extra = jnp.where(sub == second, flag, jnp.where(sub == third, name, extra))
            pay[r] = jnp.where(keep, cells, extra)


def slots_of(ids, gx, gy):
    mz, my, mx, mc = gx >> 2, gx & 3, gy >> 1, gy & 1
    z, y, x, c = ids >> 5, (ids >> 3) & 3, (ids >> 1) & 3, ids & 1
    side = ((x + z + mx + mz) & 1) + 2 * ((y + z + my + mz) & 1)
    return (((c + mc) & 1) * 4 + side) * 16 + z * 4 + (y >> 1) * 2 + (x >> 1)


def first_kernel(
    me,
    state,
    top,
    bottom,
    right,
    left,
    taps,
    code,
    lost,
    ids,
    syndromes,
    erased,
    table,
    lost_vector,
    ext_out,
    pre_out,
    inputs_out,
    weights_out,
    slots_out,
    flags_out,
    codes,
    turned,
    names,
):
    f32 = jnp.float32
    sub = lax.broadcasted_iota(jnp.int32, (8, C), 0)
    ext_out[HALO : HALO + TR, :TC] = state[...]
    ext_out[:HALO, :TC] = top[:HALO]
    ext_out[HALO + TR :, :TC] = bottom[:HALO]
    for r in range(TALL):
        ext_out[r, TC:] = jnp.where(sub < 4, right[r], left[r])
    for a in range(3):
        for b in range(3):
            high, low = split(taps[3 * a + b])
            cols = slice(b * C, (b + 1) * C)
            weights_out[a * C : (a + 1) * C, cols] = high
            weights_out[(3 + a) * C : (4 + a) * C, cols] = low
            weights_out[(6 + a) * C : (7 + a) * C, cols] = high

    for r in range(BROWS):
        names[r : r + 1] = right[r, 5:6, :]
        names[16 + r : 17 + r] = left[r, 2:3, :]
        names[32 + r : 33 + r] = right[r, 6:7, :]
        names[48 + r : 49 + r] = left[r, 1:2, :]
    lane = lax.broadcasted_iota(jnp.int32, (16, C), 1)
    wide = TC // BS

    def widen(mid, at):
        return jnp.where(
            lane < wide,
            mid,
            jnp.where(
                lane == wide,
                names[at : at + 16],
                jnp.where(lane == wide + 1, names[at + 16 : at + 32], 0.0),
            ),
        ).astype(jnp.int32)

    names[BROWS:16] = jnp.zeros((16 - BROWS, C), f32)
    names[16 + BROWS : 32] = jnp.zeros((16 - BROWS, C), f32)
    names[32 + BROWS : 48] = jnp.zeros((16 - BROWS, C), f32)
    names[48 + BROWS :] = jnp.zeros((16 - BROWS, C), f32)
    flags_out[:16] = widen(lost[...], 0)
    flags_out[16:] = jnp.zeros((16, C), jnp.int32)
    flags_out[17 : 17 + TR // BS, :wide] = erased[1]
    slots_out[...] = slots_of(widen(ids[...], 32) & 127, me[0], me[1])

    codes[...] = jnp.zeros((C, C), f32)
    codes[:TALL, :TC] = code[...]
    second = repeat_blocks(erased[1].astype(f32), TR)
    codes[TALL : TALL + TR, :TC] = jnp.where(second > 0.5, 2.0, syndromes[1].astype(f32))
    turned[...] = codes[...].T
    values, vector = table[...], lost_vector[...]
    pre_out[0] = jnp.zeros((WIDE, C), f32)
    pre_out[CONV_ROWS - 1] = jnp.zeros((WIDE, C), f32)
    for r in range(HALO - 1, HALO + TR + 1):
        column = jnp.broadcast_to(turned[:TC, r : r + 1], (TC, C))
        pre_out[r - 2, :TC] = embed(column, values, vector)
        pre_out[r - 2, TC:] = jnp.where(
            sub == 0,
            pltpu.roll(right[r], 4, 0),
            jnp.where(sub == 7, pltpu.roll(left[r], 4, 0), 0.0),
        )
    for r in range(TR):
        column = jnp.broadcast_to(turned[:TC, TALL + r : TALL + r + 1], (TC, C))
        inputs_out[r] = embed(column, values, vector)

    rows = 12

    def step(i, carry):
        start = i * rows
        pre_out[pl.ds(start, rows)] += conv_chunk(
            lambda a: ext_out[pl.ds(start + 1 + a, rows)], weights_out[...], rows
        )
        return carry

    lax.fori_loop(0, CONV_ROWS // rows, step, 0)


def group_sum(total, sub):
    near = jnp.where(sub % 2 == 0, pltpu.roll(total, 7, 0), pltpu.roll(total, 1, 0))
    total = total + near
    far = jnp.where(sub % 4 < 2, pltpu.roll(total, 6, 0), pltpu.roll(total, 2, 0))
    return total + far


def readout(sites, right, flag_a, flag_b, offset, sub):
    high, low = split(sites.reshape(32, C))
    left = jnp.concatenate(
        [jnp.concatenate([high, high], axis=1), jnp.concatenate([low, low], axis=1)],
        axis=0,
    )
    mixed = jnp.dot(left, right, preferred_element_type=jnp.float32)
    mixed = (mixed[:32] + mixed[32:]).reshape(4, 8, 2 * C)
    mixed = jnp.tanh(jnp.where(sub[None] < 4, mixed[:, :, :C], mixed[:, :, C:]))
    total = mixed[0] + mixed[1] + mixed[2] + mixed[3]
    flags = jnp.where(sub < 4, flag_a, flag_b)
    return jnp.tanh(group_sum(total, sub) * 0.0625 + flags * offset)


PIECES = (16, 8, 8, 8, 8, 8, 8) * 2


def second_kernel(
    slots, flags, me, offset, ext_hbm, pre_hbm, inputs_hbm, weights_hbm, *rest
):
    pieces = rest[:14]
    out, table, pairs, first, field, second, ext, pre, inputs, weights, sems, late = rest[14:]
    copies = [pltpu.make_async_copy(ext_hbm, ext, sems.at[14])]
    at = 0
    for i, (piece, count) in enumerate(zip(pieces, PIECES)):
        copies.append(
            pltpu.make_async_copy(piece, table.at[pl.ds(at, count)], sems.at[i])
        )
        at += count
    later = [
        pltpu.make_async_copy(pre_hbm, pre, late.at[0]),
        pltpu.make_async_copy(weights_hbm, weights, late.at[1]),
        pltpu.make_async_copy(inputs_hbm, inputs, late.at[2]),
    ]
    for copy in copies + later:
        copy.start()
    for copy in copies:
        copy.wait()
    sub = lax.broadcasted_iota(jnp.int32, (8, C), 0)
    shift = offset[...]

    def read_first(br, carry):
        for g in range(GROUPS):
            high_a, low_a = split(table[slots[br, 2 * g]])
            high_b, low_b = split(table[slots[br, 2 * g + 1]])
            right = jnp.concatenate(
                [
                    jnp.concatenate([high_a, high_b], axis=1),
                    jnp.concatenate([low_a, low_b], axis=1),
                ],
                axis=0,
            )
            pairs[br * GROUPS + g] = right
            first[br, 8 * g : 8 * g + 8] = readout(
                ext[pl.ds(br * BS, BS), 8 * g : 8 * g + 8],
                right,
                flags[br, 2 * g].astype(jnp.float32),
                flags[br, 2 * g + 1].astype(jnp.float32),
                shift,
                sub,
            )
        return carry

    lax.fori_loop(0, BROWS, read_first, 0)
    later[0].wait()

    def update(row, br):
        field[row + 1] = 0.5 * ext[row + HALO] + jnp.tanh(pre[row + 2] + first[br])

    update(-1, 0)
    update(TR, BROWS - 1)

    def update_block(br, carry):
        for r in range(BS):
            update(br * BS + r, br + 1)
        return carry

    lax.fori_loop(0, TR // BS, update_block, 0)
    field[0] = field[0] * (me[0] > 0).astype(jnp.float32)
    field[TR + 1] = field[TR + 1] * (me[0] < me[2]).astype(jnp.float32)
    edge = lax.broadcasted_iota(jnp.int32, (TR + 2, 8, C), 1)
    kept = jnp.where(
        edge < 4, (me[1] < me[3]).astype(jnp.float32), (me[1] > 0).astype(jnp.float32)
    )
    field[:, TC:] = field[:, TC:] * kept

    def read_second(br, carry):
        for g in range(TC // 8):
            second[br, 8 * g : 8 * g + 8] = readout(
                field[pl.ds(br * BS + 1, BS), 8 * g : 8 * g + 8],
                pairs[(br + 1) * GROUPS + g],
                flags[17 + br, 2 * g].astype(jnp.float32),
                flags[17 + br, 2 * g + 1].astype(jnp.float32),
                shift,
                sub,
            )
        return carry

    lax.fori_loop(0, TR // BS, read_second, 0)
    later[1].wait()
    later[2].wait()
    rows = 8

    def finish(i, carry):
        start = i * rows
        sums = conv_chunk(
            lambda a: field[pl.ds(start + a, rows)], weights[...], rows
        )[:, :TC]
        for half in range(rows // BS):
            at = start + half * BS
            out[pl.ds(at, BS)] = 0.5 * field[pl.ds(at + 1, BS), :TC] + jnp.tanh(
                sums[half * BS : (half + 1) * BS]
                + inputs[pl.ds(at, BS)]
                + second[i * (rows // BS) + half][None]
            )
        return carry

    lax.fori_loop(0, TR // rows, finish, 0)


def decode(
    state,
    syndromes,
    erased,
    readers,
    conv_weight,
    syndrome_table,
    erasure_vector,
    read_weight,
    erasure_offset,
):
    f32 = jnp.float32
    gx, gy = lax.axis_index("gx"), lax.axis_index("gy")
    gx_count, gy_count = lax.axis_size("gx"), lax.axis_size("gy")
    me = jnp.stack([gx, gy, gx_count - 1, gy_count - 1]).astype(jnp.int32)
    names = readers.reshape(1, -1)
    lost_vector, offset = erasure_vector[None], erasure_offset[None]
    vmem = pl.BlockSpec(memory_space=pltpu.VMEM)
    smem = pl.BlockSpec(memory_space=pltpu.SMEM)
    anywhere = pl.BlockSpec(memory_space=pl.ANY)

    def shape(*dims, dtype=f32):
        return jax.ShapeDtypeStruct(dims, dtype)

    up_pay, down_pay, copies = pl.pallas_call(
        rows_kernel,
        name="pack_rows",
        out_shape=(
            shape(HALO + 1, TC, C),
            shape(HALO + 1, TC, C),
            shape(16, C, C),
        ),
        in_specs=[anywhere, vmem, vmem, vmem, vmem],
        out_specs=(vmem, vmem, anywhere),
        scratch_shapes=[pltpu.SemaphoreType.DMA((2,)), pltpu.SemaphoreType.DMA((16,))],
    )(state, read_weight, syndromes, erased, names)

    up = [(i, i - 1) for i in range(1, gx_count)]
    down = [(i, i + 1) for i in range(gx_count - 1)]
    top = lax.ppermute(down_pay, "gx", down)
    bottom = lax.ppermute(up_pay, "gx", up)

    west_pay, east_pay, code, lost, ids = pl.pallas_call(
        cols_kernel,
        name="pack_cols",
        out_shape=(
            shape(TALL, 8, C),
            shape(TALL, 8, C),
            shape(TALL, TC),
            shape(16, C),
            shape(16, C),
        ),
        in_specs=[vmem] * 8,
        out_specs=(vmem,) * 5,
        scratch_shapes=[pltpu.VMEM((TALL + 32, C), f32)],
    )(state, top, bottom, syndromes, erased, names, syndrome_table, lost_vector)

    west = [(i, i - 1) for i in range(1, gy_count)]
    east = [(i, i + 1) for i in range(gy_count - 1)]
    left = lax.ppermute(east_pay, "gy", east)
    right = lax.ppermute(west_pay, "gy", west)
    pieces = gather_weights(copies)

    ext, pre, inputs, weights, slots, flags = pl.pallas_call(
        first_kernel,
        name="conv_first",
        out_shape=(
            shape(TALL, WIDE, C),
            shape(CONV_ROWS, WIDE, C),
            shape(TR, TC, C),
            shape(9 * C, 3 * C, dtype=jnp.bfloat16),
            shape(16, C, dtype=jnp.int32),
            shape(32, C, dtype=jnp.int32),
        ),
        in_specs=[smem] + [vmem] * 13,
        out_specs=(vmem,) * 6,
        scratch_shapes=[pltpu.VMEM((C, C), f32), pltpu.VMEM((C, C), f32), pltpu.VMEM((64, C), f32)],
        cost_estimate=pl.CostEstimate(
            flops=2_000_000_000, bytes_accessed=6_000_000, transcendentals=0
        ),
    )(
        me,
        state,
        top,
        bottom,
        right,
        left,
        conv_weight,
        code,
        lost,
        ids,
        syndromes,
        erased,
        syndrome_table,
        lost_vector,
    )

    return pl.pallas_call(
        second_kernel,
        name="read_and_finish",
        out_shape=shape(TR, TC, C),
        in_specs=[smem] * 3 + [vmem] + [anywhere] * 18,
        out_specs=vmem,
        scratch_shapes=[
            pltpu.VMEM((128, C, C), f32),
            pltpu.VMEM((BROWS * GROUPS, 2 * C, 2 * C), jnp.bfloat16),
            pltpu.VMEM((BROWS, WIDE, C), f32),
            pltpu.VMEM((TR + 2, WIDE, C), f32),
            pltpu.VMEM((TR // BS, TC, C), f32),
            pltpu.VMEM((TALL, WIDE, C), f32),
            pltpu.VMEM((CONV_ROWS, WIDE, C), f32),
            pltpu.VMEM((TR, TC, C), f32),
            pltpu.VMEM((9 * C, 3 * C), jnp.bfloat16),
            pltpu.SemaphoreType.DMA((15,)),
            pltpu.SemaphoreType.DMA((3,)),
        ],
        cost_estimate=pl.CostEstimate(
            flops=4_000_000_000, bytes_accessed=12_000_000, transcendentals=1_000_000
        ),
    )(slots, flags, me, offset, ext, pre, inputs, weights, *pieces)


def solution(mesh):
    placed = (
        P("gx", "gy", None),
        P(None, "gx", "gy"),
        P(None, "gx", "gy"),
        P(("gx", "gy"), None),
        P(),
        P(),
        P(),
        P(("gx", "gy"), None),
        P(),
    )
    return jax.shard_map(
        decode, mesh=mesh, in_specs=placed, out_specs=P("gx", "gy", None), check_vma=False
    )
```

```python
import jax
import jax.numpy as jnp
from jax import lax
from jax.experimental import pallas as pl
from jax.experimental.pallas import tpu as pltpu
from jax.sharding import PartitionSpec as P


BS = 4
C = 128
TR = 32
TC = 64
HALO = 4
WIDE = TC + 2 * HALO
TALL = TR + 2 * HALO
BROWS = TALL // BS
GROUPS = WIDE // 8
CONV_ROWS = TR + 4
AX = ("gx", "gy")


def flat_id(z, y, x, c):
    return ((z % 4 * 4 + y % 4) * 4 + x % 4) * 2 + c


SITES = [
    (z, y, x, c) for z in range(4) for y in range(4) for x in range(4) for c in range(2)
]


def class_groups():
    groups = {}
    for z, y, x, c in SITES:
        groups.setdefault(((x + z) % 2, (y + z) % 2, c), []).append(flat_id(z, y, x, c))
    return [groups[k] for k in sorted(groups)]


def moved(dz, dy, dx):
    return [
        (flat_id(z, y, x, c), flat_id(z + dz, y + dy, x + dx, c)) for z, y, x, c in SITES
    ]


PARTNER = [(flat_id(z, y, x, c), flat_id(z, y, x, 1 - c)) for z, y, x, c in SITES]


def gather_weights(copies):
    own = lax.all_to_all(copies, AX, 0, 0, tiled=True, axis_index_groups=class_groups())
    low, high = own[:8], own[8:]
    pieces = [own]
    for step in ((0, 0, 1), (0, 1, 0), (1, 0, 0)):
        back = tuple(-s for s in step)
        pieces.append(lax.ppermute(low, AX, moved(*step)))
        pieces.append(lax.ppermute(high, AX, moved(*back)))
    pieces += [lax.ppermute(piece, AX, PARTNER) for piece in pieces]
    return pieces


def split(value):
    high = value.astype(jnp.bfloat16)
    return high, (value - high.astype(jnp.float32)).astype(jnp.bfloat16)


def conv_chunk(read, weights, rows):
    highs, lows = [], []
    for a in range(3):
        high, low = split(read(a).reshape(rows * WIDE, C))
        highs.append(high)
        lows.append(low)
    left = jnp.concatenate(highs + lows, axis=1)
    near = jnp.dot(left, weights[:, : 4 * C], preferred_element_type=jnp.float32)
    far = jnp.dot(left[:, : 4 * C], weights[: 4 * C, 4 * C :], preferred_element_type=jnp.float32)
    sums = [
        (near[:, :C] + near[:, 3 * C :]).reshape(rows, WIDE, C),
        (near[:, C : 2 * C] + far[:, :C]).reshape(rows, WIDE, C),
        (near[:, 2 * C : 3 * C] + far[:, C:]).reshape(rows, WIDE, C),
    ]
    return pltpu.roll(sums[0], 1, 1) + sums[1] + pltpu.roll(sums[2], WIDE - 1, 1)


def rows_kernel(
    state, weight, syndromes, erased, readers, up, down, copies, rows_sem, copies_sem
):
    moves = [
        pltpu.make_async_copy(state.at[pl.ds(0, HALO)], up.at[pl.ds(0, HALO)], rows_sem.at[0]),
        pltpu.make_async_copy(
            state.at[pl.ds(TR - HALO, HALO)], down.at[pl.ds(0, HALO)], rows_sem.at[1]
        ),
    ]
    moves += [
        pltpu.make_async_copy(weight, copies.at[i], copies_sem.at[i]) for i in range(16)
    ]
    for move in moves:
        move.start()
    ids = readers[...].astype(jnp.float32)
    for pay, row, block_row in ((up, 0, 0), (down, TR - 1, TR // BS - 1)):
        pay[HALO] = jnp.zeros((TC, C), jnp.float32)
        pay[HALO, 0:1, :TC] = syndromes[0, row : row + 1, :].astype(jnp.float32)
        pay[HALO, 1:2, : TC // BS] = erased[0, block_row : block_row + 1, :].astype(
            jnp.float32
        )
        first = block_row * (TC // BS)
        pay[HALO, 2:3, :] = pltpu.roll(ids, (C - first) % C, 1)
    for move in moves:
        move.wait()


def repeat_blocks(blocks, rows):
    count = blocks.shape[0]
    row = lax.broadcasted_iota(jnp.int32, (rows, count), 0)
    tall = (row // BS == lax.broadcasted_iota(jnp.int32, (rows, count), 1)).astype(jnp.bfloat16)
    col = lax.broadcasted_iota(jnp.int32, (TC // BS, TC), 1)
    wide = (col // BS == lax.broadcasted_iota(jnp.int32, (TC // BS, TC), 0)).astype(jnp.bfloat16)
    half = jnp.dot(tall, blocks.astype(jnp.bfloat16), preferred_element_type=jnp.float32)
    return jnp.dot(half.astype(jnp.bfloat16), wide, preferred_element_type=jnp.float32)


def embed(code, table, lost_vector):
    return jnp.where(
        code > 1.5, lost_vector, jnp.where(code > 0.5, table[1:2], table[0:1])
    )


def cols_kernel(
    state,
    top,
    bottom,
    syndromes,
    erased,
    readers,
    table,
    lost_vector,
    west,
    east,
    code_out,
    lost_out,
    ids_out,
    vectors,
):
    f32 = jnp.float32
    block_rows, block_cols = TR // BS, TC // BS
    lost_out[...] = jnp.zeros((16, C), f32)
    ids_out[...] = jnp.zeros((16, C), f32)
    code_out[...] = jnp.zeros((TALL, TC), f32)
    lost_out[0:1, :block_cols] = top[HALO, 1:2, :block_cols]
    lost_out[BROWS - 1 : BROWS, :block_cols] = bottom[HALO, 1:2, :block_cols]
    lost_out[1 : 1 + block_rows, :block_cols] = erased[0].astype(f32)
    lane = lax.broadcasted_iota(jnp.int32, (1, C), 1)
    ids_out[0:1, :] = jnp.where(lane < block_cols, top[HALO, 2:3, :], 0.0)
    ids_out[BROWS - 1 : BROWS, :] = jnp.where(lane < block_cols, bottom[HALO, 2:3, :], 0.0)
    ids = readers[...].astype(f32)
    for k in range(block_rows):
        turned = pltpu.roll(ids, (C - k * block_cols) % C, 1)
        ids_out[k + 1 : k + 2, :] = jnp.where(lane < block_cols, turned, 0.0)
    code_out[HALO - 1 : HALO, :] = top[HALO, 0:1, :TC]
    code_out[HALO : HALO + TR, :] = syndromes[0].astype(f32)
    code_out[HALO + TR : HALO + TR + 1, :] = bottom[HALO, 0:1, :TC]
    sites = repeat_blocks(lost_out[:, :block_cols], TALL)
    code_out[...] = jnp.where(sites > 0.5, 2.0, code_out[...])
    sub = lax.broadcasted_iota(jnp.int32, (8, C), 0)
    for pay, edge, keep, at in ((west, 0, sub < 4, 4), (east, TC - 1, sub >= 4, 0)):
        block = edge // BS
        group = edge // 8 * 8
        code = jnp.broadcast_to(code_out[:, edge : edge + 1], (TALL, C))
        vectors[:TALL] = embed(code, table, lost_vector[...])
        vectors[TALL : TALL + 16] = jnp.broadcast_to(lost_out[:, block : block + 1], (16, C))
        vectors[TALL + 16 :] = jnp.broadcast_to(ids_out[:, block : block + 1], (16, C))
        _, second, third = (4, 5, 6) if at == 4 else (3, 2, 1)
        for r in range(TALL):
            if r < HALO:
                cells = top[r, group : group + 8]
            elif r < HALO + TR:
                cells = state[r - HALO, group : group + 8]
            else:
                cells = bottom[r - HALO - TR, group : group + 8]
            extra = jnp.broadcast_to(vectors[r : r + 1], (8, C))
            if r < BROWS:
                flag = jnp.broadcast_to(vectors[TALL + r : TALL + r + 1], (8, C))
                name = jnp.broadcast_to(vectors[TALL + 16 + r : TALL + 17 + r], (8, C))
                extra = jnp.where(sub == second, flag, jnp.where(sub == third, name, extra))
            pay[r] = jnp.where(keep, cells, extra)


def slots_of(ids, gx, gy):
    mz, my, mx, mc = gx >> 2, gx & 3, gy >> 1, gy & 1
    z, y, x, c = ids >> 5, (ids >> 3) & 3, (ids >> 1) & 3, ids & 1
    side = ((x + z + mx + mz) & 1) + 2 * ((y + z + my + mz) & 1)
    return (((c + mc) & 1) * 4 + side) * 16 + z * 4 + (y >> 1) * 2 + (x >> 1)


def first_kernel(
    me,
    state,
    top,
    bottom,
    right,
    left,
    taps,
    code,
    lost,
    ids,
    syndromes,
    erased,
    table,
    lost_vector,
    ext_out,
    pre_out,
    inputs_out,
    weights_out,
    slots_out,
    flags_out,
    codes,
    turned,
    names,
):
    f32 = jnp.float32
    sub = lax.broadcasted_iota(jnp.int32, (8, C), 0)
    ext_out[HALO : HALO + TR, :TC] = state[...]
    ext_out[:HALO, :TC] = top[:HALO]
    ext_out[HALO + TR :, :TC] = bottom[:HALO]
    for r in range(TALL):
        ext_out[r, TC:] = jnp.where(sub < 4, right[r], left[r])
    for a in range(3):
        for b in range(3):
            high, low = split(taps[3 * a + b])
            cols = slice(b * C, (b + 1) * C)
            lows = slice((3 + b) * C, (4 + b) * C)
            weights_out[a * C : (a + 1) * C, cols] = high
            weights_out[a * C : (a + 1) * C, lows] = low
            weights_out[(3 + a) * C : (4 + a) * C, cols] = high
            weights_out[(3 + a) * C : (4 + a) * C, lows] = jnp.zeros((C, C), jnp.bfloat16)

    for r in range(BROWS):
        names[r : r + 1] = right[r, 5:6, :]
        names[16 + r : 17 + r] = left[r, 2:3, :]
        names[32 + r : 33 + r] = right[r, 6:7, :]
        names[48 + r : 49 + r] = left[r, 1:2, :]
    lane = lax.broadcasted_iota(jnp.int32, (16, C), 1)
    wide = TC // BS

    def widen(mid, at):
        return jnp.where(
            lane < wide,
            mid,
            jnp.where(
                lane == wide,
                names[at : at + 16],
                jnp.where(lane == wide + 1, names[at + 16 : at + 32], 0.0),
            ),
        ).astype(jnp.int32)

    names[BROWS:16] = jnp.zeros((16 - BROWS, C), f32)
    names[16 + BROWS : 32] = jnp.zeros((16 - BROWS, C), f32)
    names[32 + BROWS : 48] = jnp.zeros((16 - BROWS, C), f32)
    names[48 + BROWS :] = jnp.zeros((16 - BROWS, C), f32)
    flags_out[:16] = widen(lost[...], 0)
    flags_out[16:] = jnp.zeros((16, C), jnp.int32)
    flags_out[17 : 17 + TR // BS, :wide] = erased[1]
    slots_out[...] = slots_of(widen(ids[...], 32) & 127, me[0], me[1])

    codes[...] = jnp.zeros((C, C), f32)
    codes[:TALL, :TC] = code[...]
    second = repeat_blocks(erased[1].astype(f32), TR)
    codes[TALL : TALL + TR, :TC] = jnp.where(second > 0.5, 2.0, syndromes[1].astype(f32))
    turned[...] = codes[...].T
    values, vector = table[...], lost_vector[...]
    pre_out[0] = jnp.zeros((WIDE, C), f32)
    pre_out[CONV_ROWS - 1] = jnp.zeros((WIDE, C), f32)
    for r in range(HALO - 1, HALO + TR + 1):
        column = jnp.broadcast_to(turned[:TC, r : r + 1], (TC, C))
        pre_out[r - 2, :TC] = embed(column, values, vector)
        pre_out[r - 2, TC:] = jnp.where(
            sub == 0,
            pltpu.roll(right[r], 4, 0),
            jnp.where(sub == 7, pltpu.roll(left[r], 4, 0), 0.0),
        )
    for r in range(TR):
        column = jnp.broadcast_to(turned[:TC, TALL + r : TALL + r + 1], (TC, C))
        inputs_out[r] = embed(column, values, vector)

    rows = 12

    def step(i, carry):
        start = i * rows
        pre_out[pl.ds(start, rows)] += conv_chunk(
            lambda a: ext_out[pl.ds(start + 1 + a, rows)], weights_out[...], rows
        )
        return carry

    lax.fori_loop(0, CONV_ROWS // rows, step, 0)


def group_sum(total, sub):
    near = jnp.where(sub % 2 == 0, pltpu.roll(total, 7, 0), pltpu.roll(total, 1, 0))
    total = total + near
    far = jnp.where(sub % 4 < 2, pltpu.roll(total, 6, 0), pltpu.roll(total, 2, 0))
    return total + far


def readout(sites, right, flag_a, flag_b, offset, sub):
    high, low = split(sites.reshape(32, C))
    left = jnp.concatenate(
        [jnp.concatenate([high, high], axis=1), jnp.concatenate([low, low], axis=1)],
        axis=0,
    )
    mixed = jnp.dot(left, right, preferred_element_type=jnp.float32)
    mixed = (mixed[:32] + mixed[32:]).reshape(4, 8, 2 * C)
    mixed = jnp.tanh(jnp.where(sub[None] < 4, mixed[:, :, :C], mixed[:, :, C:]))
    total = mixed[0] + mixed[1] + mixed[2] + mixed[3]
    flags = jnp.where(sub < 4, flag_a, flag_b)
    return jnp.tanh(group_sum(total, sub) * 0.0625 + flags * offset)


PIECES = (16, 8, 8, 8, 8, 8, 8) * 2


def second_kernel(
    slots, flags, me, offset, ext_hbm, pre_hbm, inputs_hbm, weights_hbm, *rest
):
    pieces = rest[:14]
    out, table, first, field, second, ext, pre, inputs, weights, sems = rest[14:]
    later = [
        pltpu.make_async_copy(ext_hbm, ext, sems.at[0]),
        pltpu.make_async_copy(pre_hbm, pre, sems.at[1]),
        pltpu.make_async_copy(weights_hbm, weights, sems.at[2]),
        pltpu.make_async_copy(inputs_hbm, inputs, sems.at[3]),
    ]
    for copy in later:
        copy.start()
    at = 0
    for piece, count in zip(pieces, PIECES):

        def halve(i, carry, piece=piece, at=at):
            for k in range(4):
                high, low = split(piece[4 * i + k])
                table[at + 4 * i + k, :C] = high
                table[at + 4 * i + k, C:] = low
            return carry

        lax.fori_loop(0, count // 4, halve, 0)
        at += count
    later[0].wait()
    sub = lax.broadcasted_iota(jnp.int32, (8, C), 0)
    shift = offset[...]

    def read_first(step, carry):
        for br, g in [(5 * step + k, g) for k in range(5) for g in range(GROUPS)]:
            right = jnp.concatenate(
                [table[slots[br, 2 * g]], table[slots[br, 2 * g + 1]]], axis=1
            )
            first[br, 8 * g : 8 * g + 8] = readout(
                ext[pl.ds(br * BS, BS), 8 * g : 8 * g + 8],
                right,
                flags[br, 2 * g].astype(jnp.float32),
                flags[br, 2 * g + 1].astype(jnp.float32),
                shift,
                sub,
            )
        return carry

    lax.fori_loop(0, BROWS // 5, read_first, 0)

    later[1].wait()

    def update(row, br):
        field[row + 1] = 0.5 * ext[row + HALO] + jnp.tanh(pre[row + 2] + first[br])

    update(-1, 0)
    update(TR, BROWS - 1)

    def update_block(br, carry):
        for r in range(BS):
            update(br * BS + r, br + 1)
        return carry

    lax.fori_loop(0, TR // BS, update_block, 0)
    field[0] = field[0] * (me[0] > 0).astype(jnp.float32)
    field[TR + 1] = field[TR + 1] * (me[0] < me[2]).astype(jnp.float32)
    edge = lax.broadcasted_iota(jnp.int32, (TR + 2, 8, C), 1)
    kept = jnp.where(
        edge < 4, (me[1] < me[3]).astype(jnp.float32), (me[1] > 0).astype(jnp.float32)
    )
    field[:, TC:] = field[:, TC:] * kept

    def read_second(step, carry):
        for br, g in [(4 * step + k, g) for k in range(4) for g in range(TC // 8)]:
            second[br, 8 * g : 8 * g + 8] = readout(
                field[pl.ds(br * BS + 1, BS), 8 * g : 8 * g + 8],
                jnp.concatenate(
                    [table[slots[br + 1, 2 * g]], table[slots[br + 1, 2 * g + 1]]], axis=1
                ),
                flags[17 + br, 2 * g].astype(jnp.float32),
                flags[17 + br, 2 * g + 1].astype(jnp.float32),
                shift,
                sub,
            )
        return carry

    lax.fori_loop(0, TR // BS // 4, read_second, 0)
    later[2].wait()
    later[3].wait()
    rows = 8

    def finish(i, carry):
        start = i * rows
        sums = conv_chunk(
            lambda a: field[pl.ds(start + a, rows)], weights[...], rows
        )[:, :TC]
        for half in range(rows // BS):
            at = start + half * BS
            out[pl.ds(at, BS)] = 0.5 * field[pl.ds(at + 1, BS), :TC] + jnp.tanh(
                sums[half * BS : (half + 1) * BS]
                + inputs[pl.ds(at, BS)]
                + second[i * (rows // BS) + half][None]
            )
        return carry

    lax.fori_loop(0, TR // rows, finish, 0)


def decode(
    state,
    syndromes,
    erased,
    readers,
    conv_weight,
    syndrome_table,
    erasure_vector,
    read_weight,
    erasure_offset,
):
    f32 = jnp.float32
    gx, gy = lax.axis_index("gx"), lax.axis_index("gy")
    gx_count, gy_count = lax.axis_size("gx"), lax.axis_size("gy")
    me = jnp.stack([gx, gy, gx_count - 1, gy_count - 1]).astype(jnp.int32)
    names = readers.reshape(1, -1)
    lost_vector, offset = erasure_vector[None], erasure_offset[None]
    vmem = pl.BlockSpec(memory_space=pltpu.VMEM)
    smem = pl.BlockSpec(memory_space=pltpu.SMEM)
    anywhere = pl.BlockSpec(memory_space=pl.ANY)
    hbm = pl.BlockSpec(memory_space=pltpu.HBM)

    def shape(*dims, dtype=f32):
        return jax.ShapeDtypeStruct(dims, dtype)

    up_pay, down_pay, copies = pl.pallas_call(
        rows_kernel,
        name="pack_rows",
        out_shape=(
            shape(HALO + 1, TC, C),
            shape(HALO + 1, TC, C),
            shape(16, C, C),
        ),
        in_specs=[anywhere, vmem, vmem, vmem, vmem],
        out_specs=(vmem, vmem, anywhere),
        scratch_shapes=[pltpu.SemaphoreType.DMA((2,)), pltpu.SemaphoreType.DMA((16,))],
    )(state, read_weight, syndromes, erased, names)

    up = [(i, i - 1) for i in range(1, gx_count)]
    down = [(i, i + 1) for i in range(gx_count - 1)]
    top = lax.ppermute(down_pay, "gx", down)
    bottom = lax.ppermute(up_pay, "gx", up)

    west_pay, east_pay, code, lost, ids = pl.pallas_call(
        cols_kernel,
        name="pack_cols",
        out_shape=(
            shape(TALL, 8, C),
            shape(TALL, 8, C),
            shape(TALL, TC),
            shape(16, C),
            shape(16, C),
        ),
        in_specs=[vmem] * 8,
        out_specs=(vmem,) * 5,
        scratch_shapes=[pltpu.VMEM((TALL + 32, C), f32)],
    )(state, top, bottom, syndromes, erased, names, syndrome_table, lost_vector)

    west = [(i, i - 1) for i in range(1, gy_count)]
    east = [(i, i + 1) for i in range(gy_count - 1)]
    left = lax.ppermute(east_pay, "gy", east)
    right = lax.ppermute(west_pay, "gy", west)
    pieces = gather_weights(copies)

    ext, pre, inputs, weights, slots, flags = pl.pallas_call(
        first_kernel,
        name="conv_first",
        out_shape=(
            shape(TALL, WIDE, C),
            shape(CONV_ROWS, WIDE, C),
            shape(TR, TC, C),
            shape(6 * C, 6 * C, dtype=jnp.bfloat16),
            shape(16, C, dtype=jnp.int32),
            shape(32, C, dtype=jnp.int32),
        ),
        in_specs=[smem] + [vmem] * 13,
        out_specs=(vmem,) * 6,
        scratch_shapes=[pltpu.VMEM((C, C), f32), pltpu.VMEM((C, C), f32), pltpu.VMEM((64, C), f32)],
        cost_estimate=pl.CostEstimate(
            flops=2_000_000_000, bytes_accessed=6_000_000, transcendentals=0
        ),
    )(
        me,
        state,
        top,
        bottom,
        right,
        left,
        conv_weight,
        code,
        lost,
        ids,
        syndromes,
        erased,
        syndrome_table,
        lost_vector,
    )

    return pl.pallas_call(
        second_kernel,
        name="read_and_finish",
        compiler_params=pltpu.CompilerParams(vmem_limit_bytes=47 * 2**20),
        out_shape=shape(TR, TC, C),
        in_specs=[smem] * 3 + [vmem] + [hbm] * 4 + [vmem] * 14,
        out_specs=vmem,
        scratch_shapes=[
            pltpu.VMEM((128, 2 * C, C), jnp.bfloat16),
            pltpu.VMEM((BROWS, WIDE, C), f32),
            pltpu.VMEM((TR + 2, WIDE, C), f32),
            pltpu.VMEM((TR // BS, TC, C), f32),
            pltpu.VMEM((TALL, WIDE, C), f32),
            pltpu.VMEM((CONV_ROWS, WIDE, C), f32),
            pltpu.VMEM((TR, TC, C), f32),
            pltpu.VMEM((6 * C, 6 * C), jnp.bfloat16),
            pltpu.SemaphoreType.DMA((4,)),
        ],
        cost_estimate=pl.CostEstimate(
            flops=4_000_000_000, bytes_accessed=12_000_000, transcendentals=1_000_000
        ),
    )(slots, flags, me, offset, ext, pre, inputs, weights, *pieces)


def solution(mesh):
    placed = (
        P("gx", "gy", None),
        P(None, "gx", "gy"),
        P(None, "gx", "gy"),
        P(("gx", "gy"), None),
        P(),
        P(),
        P(),
        P(("gx", "gy"), None),
        P(),
    )
    return jax.shard_map(
        decode, mesh=mesh, in_specs=placed, out_specs=P("gx", "gy", None), check_vma=False
    )
```

```python
import jax
import jax.numpy as jnp
from jax import lax
from jax.experimental import pallas as pl
from jax.experimental.pallas import tpu as pltpu
from jax.sharding import PartitionSpec as P


BS = 4
C = 128
TR = 32
TC = 64
HALO = 4
WIDE = TC + 2 * HALO
TALL = TR + 2 * HALO
BROWS = TALL // BS
GROUPS = WIDE // 8
CONV_ROWS = TR + 4
AX = ("gx", "gy")


def flat_id(z, y, x, c):
    return ((z % 4 * 4 + y % 4) * 4 + x % 4) * 2 + c


SITES = [
    (z, y, x, c) for z in range(4) for y in range(4) for x in range(4) for c in range(2)
]


def class_groups():
    groups = {}
    for z, y, x, c in SITES:
        groups.setdefault(((x + z) % 2, (y + z) % 2, c), []).append(flat_id(z, y, x, c))
    return [groups[k] for k in sorted(groups)]


def moved(dz, dy, dx):
    return [
        (flat_id(z, y, x, c), flat_id(z + dz, y + dy, x + dx, c)) for z, y, x, c in SITES
    ]


PARTNER = [(flat_id(z, y, x, c), flat_id(z, y, x, 1 - c)) for z, y, x, c in SITES]


def gather_weights(copies):
    own = lax.all_to_all(copies, AX, 0, 0, tiled=True, axis_index_groups=class_groups())
    low, high = own[:8], own[8:]
    pieces = [own]
    for step in ((0, 0, 1), (0, 1, 0), (1, 0, 0)):
        back = tuple(-s for s in step)
        pieces.append(lax.ppermute(low, AX, moved(*step)))
        pieces.append(lax.ppermute(high, AX, moved(*back)))
    pieces += [lax.ppermute(piece, AX, PARTNER) for piece in pieces]
    return pieces


def split(value):
    high = value.astype(jnp.bfloat16)
    return high, (value - high.astype(jnp.float32)).astype(jnp.bfloat16)


def conv_chunk(read, weights, rows):
    highs, lows = [], []
    for a in range(3):
        high, low = split(read(a).reshape(rows * WIDE, C))
        highs.append(high)
        lows.append(low)
    left = jnp.concatenate(highs + lows, axis=1)
    near = jnp.dot(left, weights[:, : 4 * C], preferred_element_type=jnp.float32)
    far = jnp.dot(left[:, : 4 * C], weights[: 4 * C, 4 * C :], preferred_element_type=jnp.float32)
    sums = [
        (near[:, :C] + near[:, 3 * C :]).reshape(rows, WIDE, C),
        (near[:, C : 2 * C] + far[:, :C]).reshape(rows, WIDE, C),
        (near[:, 2 * C : 3 * C] + far[:, C:]).reshape(rows, WIDE, C),
    ]
    return pltpu.roll(sums[0], 1, 1) + sums[1] + pltpu.roll(sums[2], WIDE - 1, 1)


def rows_kernel(state, syndromes, erased, readers, up, down, rows_sem):
    moves = [
        pltpu.make_async_copy(state.at[pl.ds(0, HALO)], up.at[pl.ds(0, HALO)], rows_sem.at[0]),
        pltpu.make_async_copy(
            state.at[pl.ds(TR - HALO, HALO)], down.at[pl.ds(0, HALO)], rows_sem.at[1]
        ),
    ]
    for move in moves:
        move.start()
    ids = readers[...].astype(jnp.float32)
    for pay, row, block_row in ((up, 0, 0), (down, TR - 1, TR // BS - 1)):
        pay[HALO] = jnp.zeros((TC, C), jnp.float32)
        pay[HALO, 0:1, :TC] = syndromes[0, row : row + 1, :].astype(jnp.float32)
        pay[HALO, 1:2, : TC // BS] = erased[0, block_row : block_row + 1, :].astype(
            jnp.float32
        )
        first = block_row * (TC // BS)
        pay[HALO, 2:3, :] = pltpu.roll(ids, (C - first) % C, 1)
    for move in moves:
        move.wait()


def repeat_blocks(blocks, rows):
    count = blocks.shape[0]
    row = lax.broadcasted_iota(jnp.int32, (rows, count), 0)
    tall = (row // BS == lax.broadcasted_iota(jnp.int32, (rows, count), 1)).astype(jnp.bfloat16)
    col = lax.broadcasted_iota(jnp.int32, (TC // BS, TC), 1)
    wide = (col // BS == lax.broadcasted_iota(jnp.int32, (TC // BS, TC), 0)).astype(jnp.bfloat16)
    half = jnp.dot(tall, blocks.astype(jnp.bfloat16), preferred_element_type=jnp.float32)
    return jnp.dot(half.astype(jnp.bfloat16), wide, preferred_element_type=jnp.float32)


def embed(code, table, lost_vector):
    return jnp.where(
        code > 1.5, lost_vector, jnp.where(code > 0.5, table[1:2], table[0:1])
    )


def cols_kernel(
    state,
    top,
    bottom,
    syndromes,
    erased,
    readers,
    table,
    lost_vector,
    west,
    east,
    code_out,
    lost_out,
    ids_out,
    vectors,
):
    f32 = jnp.float32
    block_rows, block_cols = TR // BS, TC // BS
    lost_out[...] = jnp.zeros((16, C), f32)
    ids_out[...] = jnp.zeros((16, C), f32)
    code_out[...] = jnp.zeros((TALL, TC), f32)
    lost_out[0:1, :block_cols] = top[HALO, 1:2, :block_cols]
    lost_out[BROWS - 1 : BROWS, :block_cols] = bottom[HALO, 1:2, :block_cols]
    lost_out[1 : 1 + block_rows, :block_cols] = erased[0].astype(f32)
    lane = lax.broadcasted_iota(jnp.int32, (1, C), 1)
    ids_out[0:1, :] = jnp.where(lane < block_cols, top[HALO, 2:3, :], 0.0)
    ids_out[BROWS - 1 : BROWS, :] = jnp.where(lane < block_cols, bottom[HALO, 2:3, :], 0.0)
    ids = readers[...].astype(f32)
    for k in range(block_rows):
        turned = pltpu.roll(ids, (C - k * block_cols) % C, 1)
        ids_out[k + 1 : k + 2, :] = jnp.where(lane < block_cols, turned, 0.0)
    code_out[HALO - 1 : HALO, :] = top[HALO, 0:1, :TC]
    code_out[HALO : HALO + TR, :] = syndromes[0].astype(f32)
    code_out[HALO + TR : HALO + TR + 1, :] = bottom[HALO, 0:1, :TC]
    sites = repeat_blocks(lost_out[:, :block_cols], TALL)
    code_out[...] = jnp.where(sites > 0.5, 2.0, code_out[...])
    sub = lax.broadcasted_iota(jnp.int32, (8, C), 0)
    for pay, edge, keep, at in ((west, 0, sub < 4, 4), (east, TC - 1, sub >= 4, 0)):
        block = edge // BS
        group = edge // 8 * 8
        code = jnp.broadcast_to(code_out[:, edge : edge + 1], (TALL, C))
        vectors[:TALL] = embed(code, table, lost_vector[...])
        vectors[TALL : TALL + 16] = jnp.broadcast_to(lost_out[:, block : block + 1], (16, C))
        vectors[TALL + 16 :] = jnp.broadcast_to(ids_out[:, block : block + 1], (16, C))
        _, second, third = (4, 5, 6) if at == 4 else (3, 2, 1)
        for r in range(TALL):
            if r < HALO:
                cells = top[r, group : group + 8]
            elif r < HALO + TR:
                cells = state[r - HALO, group : group + 8]
            else:
                cells = bottom[r - HALO - TR, group : group + 8]
            extra = jnp.broadcast_to(vectors[r : r + 1], (8, C))
            if r < BROWS:
                flag = jnp.broadcast_to(vectors[TALL + r : TALL + r + 1], (8, C))
                name = jnp.broadcast_to(vectors[TALL + 16 + r : TALL + 17 + r], (8, C))
                extra = jnp.where(sub == second, flag, jnp.where(sub == third, name, extra))
            pay[r] = jnp.where(keep, cells, extra)


def slots_of(ids, gx, gy):
    mz, my, mx, mc = gx >> 2, gx & 3, gy >> 1, gy & 1
    z, y, x, c = ids >> 5, (ids >> 3) & 3, (ids >> 1) & 3, ids & 1
    side = ((x + z + mx + mz) & 1) + 2 * ((y + z + my + mz) & 1)
    return (((c + mc) & 1) * 4 + side) * 16 + z * 4 + (y >> 1) * 2 + (x >> 1)


def first_kernel(
    me,
    state,
    top,
    bottom,
    right,
    left,
    taps,
    code,
    lost,
    ids,
    syndromes,
    erased,
    table,
    lost_vector,
    ext_out,
    pre_out,
    inputs_out,
    weights_out,
    slots_out,
    codes,
    turned,
    names,
):
    f32 = jnp.float32
    sub = lax.broadcasted_iota(jnp.int32, (8, C), 0)
    ext_out[HALO : HALO + TR, :TC] = state[...]
    ext_out[:HALO, :TC] = top[:HALO]
    ext_out[HALO + TR :, :TC] = bottom[:HALO]
    for r in range(TALL):
        ext_out[r, TC:] = jnp.where(sub < 4, right[r], left[r])
    for a in range(3):
        for b in range(3):
            high, low = split(taps[3 * a + b])
            cols = slice(b * C, (b + 1) * C)
            lows = slice((3 + b) * C, (4 + b) * C)
            weights_out[a * C : (a + 1) * C, cols] = high
            weights_out[a * C : (a + 1) * C, lows] = low
            weights_out[(3 + a) * C : (4 + a) * C, cols] = high
            weights_out[(3 + a) * C : (4 + a) * C, lows] = jnp.zeros((C, C), jnp.bfloat16)

    for r in range(BROWS):
        names[r : r + 1] = right[r, 5:6, :]
        names[16 + r : 17 + r] = left[r, 2:3, :]
        names[32 + r : 33 + r] = right[r, 6:7, :]
        names[48 + r : 49 + r] = left[r, 1:2, :]
    lane = lax.broadcasted_iota(jnp.int32, (16, C), 1)
    wide = TC // BS

    def widen(mid, at):
        return jnp.where(
            lane < wide,
            mid,
            jnp.where(
                lane == wide,
                names[at : at + 16],
                jnp.where(lane == wide + 1, names[at + 16 : at + 32], 0.0),
            ),
        ).astype(jnp.int32)

    names[BROWS:16] = jnp.zeros((16 - BROWS, C), f32)
    names[16 + BROWS : 32] = jnp.zeros((16 - BROWS, C), f32)
    names[32 + BROWS : 48] = jnp.zeros((16 - BROWS, C), f32)
    names[48 + BROWS :] = jnp.zeros((16 - BROWS, C), f32)
    slots_out[...] = slots_of(widen(ids[...], 32) & 127, me[0], me[1]) + 128 * widen(
        lost[...], 0
    )
    slots_out[1 : 1 + TR // BS, :wide] += 256 * erased[1]

    codes[...] = jnp.zeros((C, C), f32)
    codes[:TALL, :TC] = code[...]
    second = repeat_blocks(erased[1].astype(f32), TR)
    codes[TALL : TALL + TR, :TC] = jnp.where(second > 0.5, 2.0, syndromes[1].astype(f32))
    turned[...] = codes[...].T
    values, vector = table[...], lost_vector[...]
    pre_out[0] = jnp.zeros((WIDE, C), f32)
    pre_out[CONV_ROWS - 1] = jnp.zeros((WIDE, C), f32)
    for r in range(HALO - 1, HALO + TR + 1):
        column = jnp.broadcast_to(turned[:TC, r : r + 1], (TC, C))
        pre_out[r - 2, :TC] = embed(column, values, vector)
        pre_out[r - 2, TC:] = jnp.where(
            sub == 0,
            pltpu.roll(right[r], 4, 0),
            jnp.where(sub == 7, pltpu.roll(left[r], 4, 0), 0.0),
        )
    for r in range(TR):
        column = jnp.broadcast_to(turned[:TC, TALL + r : TALL + r + 1], (TC, C))
        inputs_out[r] = embed(column, values, vector)

    rows = 12

    def step(i, carry):
        start = i * rows
        pre_out[pl.ds(start, rows)] += conv_chunk(
            lambda a: ext_out[pl.ds(start + 1 + a, rows)], weights_out[...], rows
        )
        return carry

    lax.fori_loop(0, CONV_ROWS // rows, step, 0)


def group_sum(total, sub):
    near = jnp.where(sub % 2 == 0, pltpu.roll(total, 7, 0), pltpu.roll(total, 1, 0))
    total = total + near
    far = jnp.where(sub % 4 < 2, pltpu.roll(total, 6, 0), pltpu.roll(total, 2, 0))
    return total + far


def readout(sites, right, flag_a, flag_b, offset, sub):
    high, low = split(sites.reshape(32, C))
    left = jnp.concatenate(
        [jnp.concatenate([high, high], axis=1), jnp.concatenate([low, low], axis=1)],
        axis=0,
    )
    mixed = jnp.dot(left, right, preferred_element_type=jnp.float32)
    mixed = (mixed[:32] + mixed[32:]).reshape(4, 8, 2 * C)
    mixed = jnp.tanh(jnp.where(sub[None] < 4, mixed[:, :, :C], mixed[:, :, C:]))
    total = mixed[0] + mixed[1] + mixed[2] + mixed[3]
    flags = jnp.where(sub < 4, flag_a, flag_b)
    return jnp.tanh(group_sum(total, sub) * 0.0625 + flags * offset)


PIECES = (16, 8, 8, 8, 8, 8, 8) * 2


def second_kernel(
    slots, me, offset, ext_hbm, pre_hbm, inputs_hbm, weights_hbm, *rest
):
    pieces = rest[:14]
    out, table, first, field, second, ext, pre, inputs, weights, sems = rest[14:]
    later = [
        pltpu.make_async_copy(ext_hbm, ext, sems.at[0]),
        pltpu.make_async_copy(pre_hbm, pre, sems.at[1]),
        pltpu.make_async_copy(weights_hbm, weights, sems.at[2]),
        pltpu.make_async_copy(inputs_hbm, inputs, sems.at[3]),
    ]
    for copy in later:
        copy.start()
    at = 0
    for piece, count in zip(pieces, PIECES):

        def halve(i, carry, piece=piece, at=at):
            for k in range(4):
                high, low = split(piece[4 * i + k])
                table[at + 4 * i + k, :C] = high
                table[at + 4 * i + k, C:] = low
            return carry

        lax.fori_loop(0, count // 4, halve, 0)
        at += count
    later[0].wait()
    sub = lax.broadcasted_iota(jnp.int32, (8, C), 0)
    shift = offset[...]

    def read_first(step, carry):
        for br, g in [(5 * step + k, g) for k in range(5) for g in range(GROUPS)]:
            one, two = slots[br, 2 * g], slots[br, 2 * g + 1]
            first[br, 8 * g : 8 * g + 8] = readout(
                ext[pl.ds(br * BS, BS), 8 * g : 8 * g + 8],
                jnp.concatenate([table[one & 127], table[two & 127]], axis=1),
                ((one >> 7) & 1).astype(jnp.float32),
                ((two >> 7) & 1).astype(jnp.float32),
                shift,
                sub,
            )
        return carry

    lax.fori_loop(0, BROWS // 5, read_first, 0)

    later[1].wait()

    def update(row, br):
        field[row + 1] = 0.5 * ext[row + HALO] + jnp.tanh(pre[row + 2] + first[br])

    update(-1, 0)
    update(TR, BROWS - 1)

    def update_block(br, carry):
        for r in range(BS):
            update(br * BS + r, br + 1)
        return carry

    lax.fori_loop(0, TR // BS, update_block, 0)
    field[0] = field[0] * (me[0] > 0).astype(jnp.float32)
    field[TR + 1] = field[TR + 1] * (me[0] < me[2]).astype(jnp.float32)
    edge = lax.broadcasted_iota(jnp.int32, (TR + 2, 8, C), 1)
    kept = jnp.where(
        edge < 4, (me[1] < me[3]).astype(jnp.float32), (me[1] > 0).astype(jnp.float32)
    )
    field[:, TC:] = field[:, TC:] * kept

    def read_second(step, carry):
        for br, g in [(4 * step + k, g) for k in range(4) for g in range(TC // 8)]:
            one, two = slots[br + 1, 2 * g], slots[br + 1, 2 * g + 1]
            second[br, 8 * g : 8 * g + 8] = readout(
                field[pl.ds(br * BS + 1, BS), 8 * g : 8 * g + 8],
                jnp.concatenate([table[one & 127], table[two & 127]], axis=1),
                (one >> 8).astype(jnp.float32),
                (two >> 8).astype(jnp.float32),
                shift,
                sub,
            )
        return carry

    lax.fori_loop(0, TR // BS // 4, read_second, 0)
    later[2].wait()
    later[3].wait()
    rows = 8

    def finish(i, carry):
        start = i * rows
        sums = conv_chunk(
            lambda a: field[pl.ds(start + a, rows)], weights[...], rows
        )[:, :TC]
        for half in range(rows // BS):
            at = start + half * BS
            out[pl.ds(at, BS)] = 0.5 * field[pl.ds(at + 1, BS), :TC] + jnp.tanh(
                sums[half * BS : (half + 1) * BS]
                + inputs[pl.ds(at, BS)]
                + second[i * (rows // BS) + half][None]
            )
        return carry

    lax.fori_loop(0, TR // rows, finish, 0)


def decode(
    state,
    syndromes,
    erased,
    readers,
    conv_weight,
    syndrome_table,
    erasure_vector,
    read_weight,
    erasure_offset,
):
    f32 = jnp.float32
    gx, gy = lax.axis_index("gx"), lax.axis_index("gy")
    gx_count, gy_count = lax.axis_size("gx"), lax.axis_size("gy")
    me = jnp.stack([gx, gy, gx_count - 1, gy_count - 1]).astype(jnp.int32)
    names = readers.reshape(1, -1)
    lost_vector, offset = erasure_vector[None], erasure_offset[None]
    vmem = pl.BlockSpec(memory_space=pltpu.VMEM)
    smem = pl.BlockSpec(memory_space=pltpu.SMEM)
    anywhere = pl.BlockSpec(memory_space=pl.ANY)
    hbm = pl.BlockSpec(memory_space=pltpu.HBM)

    def shape(*dims, dtype=f32):
        return jax.ShapeDtypeStruct(dims, dtype)

    copies = jnp.broadcast_to(read_weight[None], (16, C, C))
    up_pay, down_pay = pl.pallas_call(
        rows_kernel,
        name="pack_rows",
        out_shape=(
            shape(HALO + 1, TC, C),
            shape(HALO + 1, TC, C),
        ),
        in_specs=[anywhere, vmem, vmem, vmem],
        out_specs=(vmem, vmem),
        scratch_shapes=[pltpu.SemaphoreType.DMA((2,))],
    )(state, syndromes, erased, names)

    up = [(i, i - 1) for i in range(1, gx_count)]
    down = [(i, i + 1) for i in range(gx_count - 1)]
    top = lax.ppermute(down_pay, "gx", down)
    bottom = lax.ppermute(up_pay, "gx", up)

    west_pay, east_pay, code, lost, ids = pl.pallas_call(
        cols_kernel,
        name="pack_cols",
        out_shape=(
            shape(TALL, 8, C),
            shape(TALL, 8, C),
            shape(TALL, TC),
            shape(16, C),
            shape(16, C),
        ),
        in_specs=[vmem] * 8,
        out_specs=(vmem,) * 5,
        scratch_shapes=[pltpu.VMEM((TALL + 32, C), f32)],
    )(state, top, bottom, syndromes, erased, names, syndrome_table, lost_vector)

    west = [(i, i - 1) for i in range(1, gy_count)]
    east = [(i, i + 1) for i in range(gy_count - 1)]
    left = lax.ppermute(east_pay, "gy", east)
    right = lax.ppermute(west_pay, "gy", west)
    pieces = gather_weights(copies)

    ext, pre, inputs, weights, slots = pl.pallas_call(
        first_kernel,
        name="conv_first",
        compiler_params=pltpu.CompilerParams(vmem_limit_bytes=16 * 2**20),
        out_shape=(
            shape(TALL, WIDE, C),
            shape(CONV_ROWS, WIDE, C),
            shape(TR, TC, C),
            shape(6 * C, 6 * C, dtype=jnp.bfloat16),
            shape(16, C, dtype=jnp.int32),
        ),
        in_specs=[smem] + [vmem] * 13,
        out_specs=(vmem,) * 5,
        scratch_shapes=[pltpu.VMEM((C, C), f32), pltpu.VMEM((C, C), f32), pltpu.VMEM((64, C), f32)],
        cost_estimate=pl.CostEstimate(
            flops=2_000_000_000, bytes_accessed=6_000_000, transcendentals=0
        ),
    )(
        me,
        state,
        top,
        bottom,
        right,
        left,
        conv_weight,
        code,
        lost,
        ids,
        syndromes,
        erased,
        syndrome_table,
        lost_vector,
    )

    return pl.pallas_call(
        second_kernel,
        name="read_and_finish",
        compiler_params=pltpu.CompilerParams(vmem_limit_bytes=44 * 2**20),
        out_shape=shape(TR, TC, C),
        in_specs=[smem] * 2 + [vmem] + [hbm] * 4 + [vmem] * 14,
        out_specs=vmem,
        scratch_shapes=[
            pltpu.VMEM((128, 2 * C, C), jnp.bfloat16),
            pltpu.VMEM((BROWS, WIDE, C), f32),
            pltpu.VMEM((TR + 2, WIDE, C), f32),
            pltpu.VMEM((TR // BS, TC, C), f32),
            pltpu.VMEM((TALL, WIDE, C), f32),
            pltpu.VMEM((CONV_ROWS, WIDE, C), f32),
            pltpu.VMEM((TR, TC, C), f32),
            pltpu.VMEM((6 * C, 6 * C), jnp.bfloat16),
            pltpu.SemaphoreType.DMA((4,)),
        ],
        cost_estimate=pl.CostEstimate(
            flops=4_000_000_000, bytes_accessed=12_000_000, transcendentals=1_000_000
        ),
    )(slots, me, offset, ext, pre, inputs, weights, *pieces)


def solution(mesh):
    placed = (
        P("gx", "gy", None),
        P(None, "gx", "gy"),
        P(None, "gx", "gy"),
        P(("gx", "gy"), None),
        P(),
        P(),
        P(),
        P(("gx", "gy"), None),
        P(),
    )
    return jax.shard_map(
        decode, mesh=mesh, in_specs=placed, out_specs=P("gx", "gy", None), check_vma=False
    )
```

```python
import jax
import jax.numpy as jnp
from jax import lax
from jax.experimental import pallas as pl
from jax.experimental.pallas import tpu as pltpu
from jax.sharding import PartitionSpec as P


BS = 4
C = 128
TR = 32
TC = 64
HALO = 4
WIDE = TC + 2 * HALO
TALL = TR + 2 * HALO
BROWS = TALL // BS
GROUPS = WIDE // 8
CONV_ROWS = TR + 4
AX = ("gx", "gy")


def flat_id(z, y, x, c):
    return ((z % 4 * 4 + y % 4) * 4 + x % 4) * 2 + c


SITES = [
    (z, y, x, c) for z in range(4) for y in range(4) for x in range(4) for c in range(2)
]


def class_groups():
    groups = {}
    for z, y, x, c in SITES:
        groups.setdefault(((x + z) % 2, (y + z) % 2, c), []).append(flat_id(z, y, x, c))
    return [groups[k] for k in sorted(groups)]


def moved(dz, dy, dx):
    return [
        (flat_id(z, y, x, c), flat_id(z + dz, y + dy, x + dx, c)) for z, y, x, c in SITES
    ]


PARTNER = [(flat_id(z, y, x, c), flat_id(z, y, x, 1 - c)) for z, y, x, c in SITES]


def gather_weights(copies):
    own = lax.all_to_all(copies, AX, 0, 0, tiled=True, axis_index_groups=class_groups())
    low, high = own[:8], own[8:]
    pieces = [own]
    for step in ((0, 0, 1), (0, 1, 0), (1, 0, 0)):
        back = tuple(-s for s in step)
        pieces.append(lax.ppermute(low, AX, moved(*step)))
        pieces.append(lax.ppermute(high, AX, moved(*back)))
    pieces += [lax.ppermute(piece, AX, PARTNER) for piece in pieces]
    return pieces


def split(value):
    high = value.astype(jnp.bfloat16)
    return high, (value - high.astype(jnp.float32)).astype(jnp.bfloat16)


def conv_chunk(read, weights, rows):
    highs, lows = [], []
    for a in range(3):
        high, low = split(read(a).reshape(rows * WIDE, C))
        highs.append(high)
        lows.append(low)
    left = jnp.concatenate(highs + lows, axis=1)
    near = jnp.dot(left, weights[:, : 4 * C], preferred_element_type=jnp.float32)
    far = jnp.dot(left[:, : 4 * C], weights[: 4 * C, 4 * C :], preferred_element_type=jnp.float32)
    sums = [
        (near[:, :C] + near[:, 3 * C :]).reshape(rows, WIDE, C),
        (near[:, C : 2 * C] + far[:, :C]).reshape(rows, WIDE, C),
        (near[:, 2 * C : 3 * C] + far[:, C:]).reshape(rows, WIDE, C),
    ]
    return pltpu.roll(sums[0], 1, 1) + sums[1] + pltpu.roll(sums[2], WIDE - 1, 1)


def rows_kernel(
    state, weight, syndromes, erased, readers, up, down, copies, rows_sem, copies_sem
):
    moves = [
        pltpu.make_async_copy(state.at[pl.ds(0, HALO)], up.at[pl.ds(0, HALO)], rows_sem.at[0]),
        pltpu.make_async_copy(
            state.at[pl.ds(TR - HALO, HALO)], down.at[pl.ds(0, HALO)], rows_sem.at[1]
        ),
    ]
    moves += [
        pltpu.make_async_copy(weight, copies.at[i], copies_sem.at[i]) for i in range(16)
    ]
    for move in moves:
        move.start()
    ids = readers[...].astype(jnp.float32)
    for pay, row, block_row in ((up, 0, 0), (down, TR - 1, TR // BS - 1)):
        pay[HALO] = jnp.zeros((TC, C), jnp.float32)
        pay[HALO, 0:1, :TC] = syndromes[0, row : row + 1, :].astype(jnp.float32)
        pay[HALO, 1:2, : TC // BS] = erased[0, block_row : block_row + 1, :].astype(
            jnp.float32
        )
        first = block_row * (TC // BS)
        pay[HALO, 2:3, :] = pltpu.roll(ids, (C - first) % C, 1)
    for move in moves:
        move.wait()


def repeat_blocks(blocks, rows):
    count = blocks.shape[0]
    row = lax.broadcasted_iota(jnp.int32, (rows, count), 0)
    tall = (row // BS == lax.broadcasted_iota(jnp.int32, (rows, count), 1)).astype(jnp.bfloat16)
    col = lax.broadcasted_iota(jnp.int32, (TC // BS, TC), 1)
    wide = (col // BS == lax.broadcasted_iota(jnp.int32, (TC // BS, TC), 0)).astype(jnp.bfloat16)
    half = jnp.dot(tall, blocks.astype(jnp.bfloat16), preferred_element_type=jnp.float32)
    return jnp.dot(half.astype(jnp.bfloat16), wide, preferred_element_type=jnp.float32)


def embed(code, table, lost_vector):
    return jnp.where(
        code > 1.5, lost_vector, jnp.where(code > 0.5, table[1:2], table[0:1])
    )


def cols_kernel(
    state,
    top,
    bottom,
    syndromes,
    erased,
    readers,
    table,
    lost_vector,
    west,
    east,
    code_out,
    lost_out,
    ids_out,
    vectors,
):
    f32 = jnp.float32
    block_rows, block_cols = TR // BS, TC // BS
    lost_out[...] = jnp.zeros((16, C), f32)
    ids_out[...] = jnp.zeros((16, C), f32)
    code_out[...] = jnp.zeros((TALL, TC), f32)
    lost_out[0:1, :block_cols] = top[HALO, 1:2, :block_cols]
    lost_out[BROWS - 1 : BROWS, :block_cols] = bottom[HALO, 1:2, :block_cols]
    lost_out[1 : 1 + block_rows, :block_cols] = erased[0].astype(f32)
    lane = lax.broadcasted_iota(jnp.int32, (1, C), 1)
    ids_out[0:1, :] = jnp.where(lane < block_cols, top[HALO, 2:3, :], 0.0)
    ids_out[BROWS - 1 : BROWS, :] = jnp.where(lane < block_cols, bottom[HALO, 2:3, :], 0.0)
    ids = readers[...].astype(f32)
    for k in range(block_rows):
        turned = pltpu.roll(ids, (C - k * block_cols) % C, 1)
        ids_out[k + 1 : k + 2, :] = jnp.where(lane < block_cols, turned, 0.0)
    code_out[HALO - 1 : HALO, :] = top[HALO, 0:1, :TC]
    code_out[HALO : HALO + TR, :] = syndromes[0].astype(f32)
    code_out[HALO + TR : HALO + TR + 1, :] = bottom[HALO, 0:1, :TC]
    sites = repeat_blocks(lost_out[:, :block_cols], TALL)
    code_out[...] = jnp.where(sites > 0.5, 2.0, code_out[...])
    sub = lax.broadcasted_iota(jnp.int32, (8, C), 0)
    for pay, edge, keep, at in ((west, 0, sub < 4, 4), (east, TC - 1, sub >= 4, 0)):
        block = edge // BS
        group = edge // 8 * 8
        code = jnp.broadcast_to(code_out[:, edge : edge + 1], (TALL, C))
        vectors[:TALL] = embed(code, table, lost_vector[...])
        vectors[TALL : TALL + 16] = jnp.broadcast_to(lost_out[:, block : block + 1], (16, C))
        vectors[TALL + 16 :] = jnp.broadcast_to(ids_out[:, block : block + 1], (16, C))
        _, second, third = (4, 5, 6) if at == 4 else (3, 2, 1)
        for r in range(TALL):
            if r < HALO:
                cells = top[r, group : group + 8]
            elif r < HALO + TR:
                cells = state[r - HALO, group : group + 8]
            else:
                cells = bottom[r - HALO - TR, group : group + 8]
            extra = jnp.broadcast_to(vectors[r : r + 1], (8, C))
            if r < BROWS:
                flag = jnp.broadcast_to(vectors[TALL + r : TALL + r + 1], (8, C))
                name = jnp.broadcast_to(vectors[TALL + 16 + r : TALL + 17 + r], (8, C))
                extra = jnp.where(sub == second, flag, jnp.where(sub == third, name, extra))
            pay[r] = jnp.where(keep, cells, extra)


def slots_of(ids, gx, gy):
    mz, my, mx, mc = gx >> 2, gx & 3, gy >> 1, gy & 1
    z, y, x, c = ids >> 5, (ids >> 3) & 3, (ids >> 1) & 3, ids & 1
    side = ((x + z + mx + mz) & 1) + 2 * ((y + z + my + mz) & 1)
    return (((c + mc) & 1) * 4 + side) * 16 + z * 4 + (y >> 1) * 2 + (x >> 1)


def first_kernel(
    me,
    state,
    top,
    bottom,
    right,
    left,
    taps,
    code,
    lost,
    ids,
    syndromes,
    erased,
    table,
    lost_vector,
    ext_out,
    pre_out,
    inputs_out,
    weights_out,
    slots_out,
    codes,
    turned,
    names,
):
    f32 = jnp.float32
    sub = lax.broadcasted_iota(jnp.int32, (8, C), 0)
    ext_out[HALO : HALO + TR, :TC] = state[...]
    ext_out[:HALO, :TC] = top[:HALO]
    ext_out[HALO + TR :, :TC] = bottom[:HALO]
    for r in range(TALL):
        ext_out[r, TC:] = jnp.where(sub < 4, right[r], left[r])
    for a in range(3):
        for b in range(3):
            high, low = split(taps[3 * a + b])
            cols = slice(b * C, (b + 1) * C)
            lows = slice((3 + b) * C, (4 + b) * C)
            weights_out[a * C : (a + 1) * C, cols] = high
            weights_out[a * C : (a + 1) * C, lows] = low
            weights_out[(3 + a) * C : (4 + a) * C, cols] = high
            weights_out[(3 + a) * C : (4 + a) * C, lows] = jnp.zeros((C, C), jnp.bfloat16)

    for r in range(BROWS):
        names[r : r + 1] = right[r, 5:6, :]
        names[16 + r : 17 + r] = left[r, 2:3, :]
        names[32 + r : 33 + r] = right[r, 6:7, :]
        names[48 + r : 49 + r] = left[r, 1:2, :]
    lane = lax.broadcasted_iota(jnp.int32, (16, C), 1)
    wide = TC // BS

    def widen(mid, at):
        return jnp.where(
            lane < wide,
            mid,
            jnp.where(
                lane == wide,
                names[at : at + 16],
                jnp.where(lane == wide + 1, names[at + 16 : at + 32], 0.0),
            ),
        ).astype(jnp.int32)

    names[BROWS:16] = jnp.zeros((16 - BROWS, C), f32)
    names[16 + BROWS : 32] = jnp.zeros((16 - BROWS, C), f32)
    names[32 + BROWS : 48] = jnp.zeros((16 - BROWS, C), f32)
    names[48 + BROWS :] = jnp.zeros((16 - BROWS, C), f32)
    slots_out[...] = slots_of(widen(ids[...], 32) & 127, me[0], me[1]) + 128 * widen(
        lost[...], 0
    )
    slots_out[1 : 1 + TR // BS, :wide] += 256 * erased[1]

    codes[...] = jnp.zeros((C, C), f32)
    codes[:TALL, :TC] = code[...]
    second = repeat_blocks(erased[1].astype(f32), TR)
    codes[TALL : TALL + TR, :TC] = jnp.where(second > 0.5, 2.0, syndromes[1].astype(f32))
    turned[...] = codes[...].T
    values, vector = table[...], lost_vector[...]
    pre_out[0] = jnp.zeros((WIDE, C), f32)
    pre_out[CONV_ROWS - 1] = jnp.zeros((WIDE, C), f32)
    for r in range(HALO - 1, HALO + TR + 1):
        column = jnp.broadcast_to(turned[:TC, r : r + 1], (TC, C))
        pre_out[r - 2, :TC] = embed(column, values, vector)
        pre_out[r - 2, TC:] = jnp.where(
            sub == 0,
            pltpu.roll(right[r], 4, 0),
            jnp.where(sub == 7, pltpu.roll(left[r], 4, 0), 0.0),
        )
    for r in range(TR):
        column = jnp.broadcast_to(turned[:TC, TALL + r : TALL + r + 1], (TC, C))
        inputs_out[r] = embed(column, values, vector)

    rows = 12

    def step(i, carry):
        start = i * rows
        pre_out[pl.ds(start, rows)] += conv_chunk(
            lambda a: ext_out[pl.ds(start + 1 + a, rows)], weights_out[...], rows
        )
        return carry

    lax.fori_loop(0, CONV_ROWS // rows, step, 0)


def group_sum(total, sub):
    near = jnp.where(sub % 2 == 0, pltpu.roll(total, 7, 0), pltpu.roll(total, 1, 0))
    total = total + near
    far = jnp.where(sub % 4 < 2, pltpu.roll(total, 6, 0), pltpu.roll(total, 2, 0))
    return total + far


def readout(sites, right, flag_a, flag_b, offset, sub):
    high, low = split(sites.reshape(32, C))
    left = jnp.concatenate(
        [jnp.concatenate([high, high], axis=1), jnp.concatenate([low, low], axis=1)],
        axis=0,
    )
    mixed = jnp.dot(left, right, preferred_element_type=jnp.float32)
    mixed = (mixed[:32] + mixed[32:]).reshape(4, 8, 2 * C)
    mixed = jnp.tanh(jnp.where(sub[None] < 4, mixed[:, :, :C], mixed[:, :, C:]))
    total = mixed[0] + mixed[1] + mixed[2] + mixed[3]
    flags = jnp.where(sub < 4, flag_a, flag_b)
    return jnp.tanh(group_sum(total, sub) * 0.0625 + flags * offset)


PIECES = (16, 8, 8, 8, 8, 8, 8) * 2


def second_kernel(
    slots, me, offset, ext_hbm, pre_hbm, inputs_hbm, weights_hbm, *rest
):
    pieces = rest[:14]
    out, table, first, field, second, ext, pre, inputs, weights, sems = rest[14:]
    later = [
        pltpu.make_async_copy(ext_hbm, ext, sems.at[0]),
        pltpu.make_async_copy(pre_hbm, pre, sems.at[1]),
        pltpu.make_async_copy(weights_hbm, weights, sems.at[2]),
        pltpu.make_async_copy(inputs_hbm, inputs, sems.at[3]),
    ]
    for copy in later:
        copy.start()
    at = 0
    for piece, count in zip(pieces, PIECES):

        def halve(i, carry, piece=piece, at=at):
            for k in range(4):
                high, low = split(piece[4 * i + k])
                table[at + 4 * i + k, :C] = high
                table[at + 4 * i + k, C:] = low
            return carry

        lax.fori_loop(0, count // 4, halve, 0)
        at += count
    later[0].wait()
    sub = lax.broadcasted_iota(jnp.int32, (8, C), 0)
    shift = offset[...]

    def read_first(step, carry):
        for br, g in [(5 * step + k, g) for k in range(5) for g in range(GROUPS)]:
            one, two = slots[br, 2 * g], slots[br, 2 * g + 1]
            first[br, 8 * g : 8 * g + 8] = readout(
                ext[pl.ds(br * BS, BS), 8 * g : 8 * g + 8],
                jnp.concatenate([table[one & 127], table[two & 127]], axis=1),
                ((one >> 7) & 1).astype(jnp.float32),
                ((two >> 7) & 1).astype(jnp.float32),
                shift,
                sub,
            )
        return carry

    lax.fori_loop(0, BROWS // 5, read_first, 0)

    later[1].wait()

    def update(row, br):
        field[row + 1] = 0.5 * ext[row + HALO] + jnp.tanh(pre[row + 2] + first[br])

    update(-1, 0)
    update(TR, BROWS - 1)

    def update_block(br, carry):
        for r in range(BS):
            update(br * BS + r, br + 1)
        return carry

    lax.fori_loop(0, TR // BS, update_block, 0)
    field[0] = field[0] * (me[0] > 0).astype(jnp.float32)
    field[TR + 1] = field[TR + 1] * (me[0] < me[2]).astype(jnp.float32)
    edge = lax.broadcasted_iota(jnp.int32, (TR + 2, 8, C), 1)
    kept = jnp.where(
        edge < 4, (me[1] < me[3]).astype(jnp.float32), (me[1] > 0).astype(jnp.float32)
    )
    field[:, TC:] = field[:, TC:] * kept

    def read_second(step, carry):
        for br, g in [(4 * step + k, g) for k in range(4) for g in range(TC // 8)]:
            one, two = slots[br + 1, 2 * g], slots[br + 1, 2 * g + 1]
            second[br, 8 * g : 8 * g + 8] = readout(
                field[pl.ds(br * BS + 1, BS), 8 * g : 8 * g + 8],
                jnp.concatenate([table[one & 127], table[two & 127]], axis=1),
                (one >> 8).astype(jnp.float32),
                (two >> 8).astype(jnp.float32),
                shift,
                sub,
            )
        return carry

    lax.fori_loop(0, TR // BS // 4, read_second, 0)
    later[2].wait()
    later[3].wait()
    rows = 8

    def finish(i, carry):
        start = i * rows
        sums = conv_chunk(
            lambda a: field[pl.ds(start + a, rows)], weights[...], rows
        )[:, :TC]
        for half in range(rows // BS):
            at = start + half * BS
            out[pl.ds(at, BS)] = 0.5 * field[pl.ds(at + 1, BS), :TC] + jnp.tanh(
                sums[half * BS : (half + 1) * BS]
                + inputs[pl.ds(at, BS)]
                + second[i * (rows // BS) + half][None]
            )
        return carry

    lax.fori_loop(0, TR // rows, finish, 0)


def decode(
    state,
    syndromes,
    erased,
    readers,
    conv_weight,
    syndrome_table,
    erasure_vector,
    read_weight,
    erasure_offset,
):
    f32 = jnp.float32
    gx, gy = lax.axis_index("gx"), lax.axis_index("gy")
    gx_count, gy_count = lax.axis_size("gx"), lax.axis_size("gy")
    me = jnp.stack([gx, gy, gx_count - 1, gy_count - 1]).astype(jnp.int32)
    names = readers.reshape(1, -1)
    lost_vector, offset = erasure_vector[None], erasure_offset[None]
    vmem = pl.BlockSpec(memory_space=pltpu.VMEM)
    smem = pl.BlockSpec(memory_space=pltpu.SMEM)
    anywhere = pl.BlockSpec(memory_space=pl.ANY)
    hbm = pl.BlockSpec(memory_space=pltpu.HBM)

    def shape(*dims, dtype=f32):
        return jax.ShapeDtypeStruct(dims, dtype)

    up_pay, down_pay, copies = pl.pallas_call(
        rows_kernel,
        name="pack_rows",
        out_shape=(
            shape(HALO + 1, TC, C),
            shape(HALO + 1, TC, C),
            shape(16, C, C),
        ),
        in_specs=[anywhere, vmem, vmem, vmem, vmem],
        out_specs=(vmem, vmem, anywhere),
        scratch_shapes=[pltpu.SemaphoreType.DMA((2,)), pltpu.SemaphoreType.DMA((16,))],
    )(state, read_weight, syndromes, erased, names)

    up = [(i, i - 1) for i in range(1, gx_count)]
    down = [(i, i + 1) for i in range(gx_count - 1)]
    top = lax.ppermute(down_pay, "gx", down)
    bottom = lax.ppermute(up_pay, "gx", up)

    west_pay, east_pay, code, lost, ids = pl.pallas_call(
        cols_kernel,
        name="pack_cols",
        out_shape=(
            shape(TALL, 8, C),
            shape(TALL, 8, C),
            shape(TALL, TC),
            shape(16, C),
            shape(16, C),
        ),
        in_specs=[vmem] * 8,
        out_specs=(vmem,) * 5,
        scratch_shapes=[pltpu.VMEM((TALL + 32, C), f32)],
    )(state, top, bottom, syndromes, erased, names, syndrome_table, lost_vector)

    west = [(i, i - 1) for i in range(1, gy_count)]
    east = [(i, i + 1) for i in range(gy_count - 1)]
    left = lax.ppermute(east_pay, "gy", east)
    right = lax.ppermute(west_pay, "gy", west)
    pieces = gather_weights(copies)

    ext, pre, inputs, weights, slots = pl.pallas_call(
        first_kernel,
        name="conv_first",
        compiler_params=pltpu.CompilerParams(vmem_limit_bytes=16 * 2**20),
        out_shape=(
            shape(TALL, WIDE, C),
            shape(CONV_ROWS, WIDE, C),
            shape(TR, TC, C),
            shape(6 * C, 6 * C, dtype=jnp.bfloat16),
            shape(16, C, dtype=jnp.int32),
        ),
        in_specs=[smem] + [vmem] * 13,
        out_specs=(vmem,) * 5,
        scratch_shapes=[pltpu.VMEM((C, C), f32), pltpu.VMEM((C, C), f32), pltpu.VMEM((64, C), f32)],
        cost_estimate=pl.CostEstimate(
            flops=2_000_000_000, bytes_accessed=6_000_000, transcendentals=0
        ),
    )(
        me,
        state,
        top,
        bottom,
        right,
        left,
        conv_weight,
        code,
        lost,
        ids,
        syndromes,
        erased,
        syndrome_table,
        lost_vector,
    )

    return pl.pallas_call(
        second_kernel,
        name="read_and_finish",
        compiler_params=pltpu.CompilerParams(vmem_limit_bytes=44 * 2**20),
        out_shape=shape(TR, TC, C),
        in_specs=[smem] * 2 + [vmem] + [hbm] * 4 + [vmem] * 14,
        out_specs=vmem,
        scratch_shapes=[
            pltpu.VMEM((128, 2 * C, C), jnp.bfloat16),
            pltpu.VMEM((BROWS, WIDE, C), f32),
            pltpu.VMEM((TR + 2, WIDE, C), f32),
            pltpu.VMEM((TR // BS, TC, C), f32),
            pltpu.VMEM((TALL, WIDE, C), f32),
            pltpu.VMEM((CONV_ROWS, WIDE, C), f32),
            pltpu.VMEM((TR, TC, C), f32),
            pltpu.VMEM((6 * C, 6 * C), jnp.bfloat16),
            pltpu.SemaphoreType.DMA((4,)),
        ],
        cost_estimate=pl.CostEstimate(
            flops=4_000_000_000, bytes_accessed=12_000_000, transcendentals=1_000_000
        ),
    )(slots, me, offset, ext, pre, inputs, weights, *pieces)


def solution(mesh):
    placed = (
        P("gx", "gy", None),
        P(None, "gx", "gy"),
        P(None, "gx", "gy"),
        P(("gx", "gy"), None),
        P(),
        P(),
        P(),
        P(("gx", "gy"), None),
        P(),
    )
    return jax.shard_map(
        decode, mesh=mesh, in_specs=placed, out_specs=P("gx", "gy", None), check_vma=False
    )
```

```python
import jax
import jax.numpy as jnp
from jax import lax
from jax.experimental import pallas as pl
from jax.experimental.pallas import tpu as pltpu
from jax.sharding import PartitionSpec as P


BS = 4
C = 128
TR = 32
TC = 64
HALO = 4
WIDE = TC + 2 * HALO
TALL = TR + 2 * HALO
BROWS = TALL // BS
GROUPS = WIDE // 8
CONV_ROWS = TR + 4
AX = ("gx", "gy")


def flat_id(z, y, x, c):
    return ((z % 4 * 4 + y % 4) * 4 + x % 4) * 2 + c


SITES = [
    (z, y, x, c) for z in range(4) for y in range(4) for x in range(4) for c in range(2)
]


def class_groups():
    groups = {}
    for z, y, x, c in SITES:
        groups.setdefault(((x + z) % 2, (y + z) % 2, c), []).append(flat_id(z, y, x, c))
    return [groups[k] for k in sorted(groups)]


def moved(dz, dy, dx):
    return [
        (flat_id(z, y, x, c), flat_id(z + dz, y + dy, x + dx, c)) for z, y, x, c in SITES
    ]


PARTNER = [(flat_id(z, y, x, c), flat_id(z, y, x, 1 - c)) for z, y, x, c in SITES]


def gather_weights(copies):
    own = lax.all_to_all(copies, AX, 0, 0, tiled=True, axis_index_groups=class_groups())
    low, high = own[:8], own[8:]
    pieces = [own]
    for step in ((0, 0, 1), (0, 1, 0), (1, 0, 0)):
        back = tuple(-s for s in step)
        pieces.append(lax.ppermute(low, AX, moved(*step)))
        pieces.append(lax.ppermute(high, AX, moved(*back)))
    pieces += [lax.ppermute(piece, AX, PARTNER) for piece in pieces]
    return pieces


def split(value):
    high = value.astype(jnp.bfloat16)
    return high, (value - high.astype(jnp.float32)).astype(jnp.bfloat16)


def conv_chunk(read, weights, rows):
    highs, lows = [], []
    for a in range(3):
        high, low = split(read(a).reshape(rows * WIDE, C))
        highs.append(high)
        lows.append(low)
    left = jnp.concatenate(highs + lows, axis=1)
    near = jnp.dot(left, weights[:, : 4 * C], preferred_element_type=jnp.float32)
    far = jnp.dot(left[:, : 4 * C], weights[: 4 * C, 4 * C :], preferred_element_type=jnp.float32)
    sums = [
        (near[:, :C] + near[:, 3 * C :]).reshape(rows, WIDE, C),
        (near[:, C : 2 * C] + far[:, :C]).reshape(rows, WIDE, C),
        (near[:, 2 * C : 3 * C] + far[:, C:]).reshape(rows, WIDE, C),
    ]
    return pltpu.roll(sums[0], 1, 1) + sums[1] + pltpu.roll(sums[2], WIDE - 1, 1)


def rows_kernel(
    state, weight, syndromes, erased, readers, up, down, copies, rows_sem, copies_sem
):
    moves = [
        pltpu.make_async_copy(state.at[pl.ds(0, HALO)], up.at[pl.ds(0, HALO)], rows_sem.at[0]),
        pltpu.make_async_copy(
            state.at[pl.ds(TR - HALO, HALO)], down.at[pl.ds(0, HALO)], rows_sem.at[1]
        ),
    ]
    moves += [
        pltpu.make_async_copy(weight, copies.at[i], copies_sem.at[i]) for i in range(16)
    ]
    for move in moves:
        move.start()
    ids = readers[...].astype(jnp.float32)
    for pay, row, block_row in ((up, 0, 0), (down, TR - 1, TR // BS - 1)):
        pay[HALO] = jnp.zeros((TC, C), jnp.float32)
        pay[HALO, 0:1, :TC] = syndromes[0, row : row + 1, :].astype(jnp.float32)
        pay[HALO, 1:2, : TC // BS] = erased[0, block_row : block_row + 1, :].astype(
            jnp.float32
        )
        first = block_row * (TC // BS)
        pay[HALO, 2:3, :] = pltpu.roll(ids, (C - first) % C, 1)
    for move in moves:
        move.wait()


def repeat_blocks(blocks, rows):
    count = blocks.shape[0]
    row = lax.broadcasted_iota(jnp.int32, (rows, count), 0)
    tall = (row // BS == lax.broadcasted_iota(jnp.int32, (rows, count), 1)).astype(jnp.bfloat16)
    col = lax.broadcasted_iota(jnp.int32, (TC // BS, TC), 1)
    wide = (col // BS == lax.broadcasted_iota(jnp.int32, (TC // BS, TC), 0)).astype(jnp.bfloat16)
    half = jnp.dot(tall, blocks.astype(jnp.bfloat16), preferred_element_type=jnp.float32)
    return jnp.dot(half.astype(jnp.bfloat16), wide, preferred_element_type=jnp.float32)


def embed(code, table, lost_vector):
    return jnp.where(
        code > 1.5, lost_vector, jnp.where(code > 0.5, table[1:2], table[0:1])
    )


def cols_kernel(
    state,
    top,
    bottom,
    syndromes,
    erased,
    readers,
    table,
    lost_vector,
    west,
    east,
    code_out,
    lost_out,
    ids_out,
    vectors,
):
    f32 = jnp.float32
    block_rows, block_cols = TR // BS, TC // BS
    lost_out[...] = jnp.zeros((16, C), f32)
    ids_out[...] = jnp.zeros((16, C), f32)
    code_out[...] = jnp.zeros((TALL, TC), f32)
    lost_out[0:1, :block_cols] = top[HALO, 1:2, :block_cols]
    lost_out[BROWS - 1 : BROWS, :block_cols] = bottom[HALO, 1:2, :block_cols]
    lost_out[1 : 1 + block_rows, :block_cols] = erased[0].astype(f32)
    lane = lax.broadcasted_iota(jnp.int32, (1, C), 1)
    ids_out[0:1, :] = jnp.where(lane < block_cols, top[HALO, 2:3, :], 0.0)
    ids_out[BROWS - 1 : BROWS, :] = jnp.where(lane < block_cols, bottom[HALO, 2:3, :], 0.0)
    ids = readers[...].astype(f32)
    for k in range(block_rows):
        turned = pltpu.roll(ids, (C - k * block_cols) % C, 1)
        ids_out[k + 1 : k + 2, :] = jnp.where(lane < block_cols, turned, 0.0)
    code_out[HALO - 1 : HALO, :] = top[HALO, 0:1, :TC]
    code_out[HALO : HALO + TR, :] = syndromes[0].astype(f32)
    code_out[HALO + TR : HALO + TR + 1, :] = bottom[HALO, 0:1, :TC]
    sites = repeat_blocks(lost_out[:, :block_cols], TALL)
    code_out[...] = jnp.where(sites > 0.5, 2.0, code_out[...])
    sub = lax.broadcasted_iota(jnp.int32, (8, C), 0)
    for pay, edge, keep, at in ((west, 0, sub < 4, 4), (east, TC - 1, sub >= 4, 0)):
        block = edge // BS
        group = edge // 8 * 8
        code = jnp.broadcast_to(code_out[:, edge : edge + 1], (TALL, C))
        vectors[:TALL] = embed(code, table, lost_vector[...])
        vectors[TALL : TALL + 16] = jnp.broadcast_to(lost_out[:, block : block + 1], (16, C))
        vectors[TALL + 16 :] = jnp.broadcast_to(ids_out[:, block : block + 1], (16, C))
        _, second, third = (4, 5, 6) if at == 4 else (3, 2, 1)
        for r in range(TALL):
            if r < HALO:
                cells = top[r, group : group + 8]
            elif r < HALO + TR:
                cells = state[r - HALO, group : group + 8]
            else:
                cells = bottom[r - HALO - TR, group : group + 8]
            extra = jnp.broadcast_to(vectors[r : r + 1], (8, C))
            if r < BROWS:
                flag = jnp.broadcast_to(vectors[TALL + r : TALL + r + 1], (8, C))
                name = jnp.broadcast_to(vectors[TALL + 16 + r : TALL + 17 + r], (8, C))
                extra = jnp.where(sub == second, flag, jnp.where(sub == third, name, extra))
            pay[r] = jnp.where(keep, cells, extra)


def slots_of(ids, gx, gy):
    mz, my, mx, mc = gx >> 2, gx & 3, gy >> 1, gy & 1
    z, y, x, c = ids >> 5, (ids >> 3) & 3, (ids >> 1) & 3, ids & 1
    side = ((x + z + mx + mz) & 1) + 2 * ((y + z + my + mz) & 1)
    return (((c + mc) & 1) * 4 + side) * 16 + z * 4 + (y >> 1) * 2 + (x >> 1)


def prepare_kernel(
    taps,
    code,
    syndromes,
    erased,
    table,
    lost_vector,
    first_out,
    second_out,
    weights_out,
    codes,
    turned,
):
    f32 = jnp.float32
    for a in range(3):
        for b in range(3):
            high, low = split(taps[3 * a + b])
            cols = slice(b * C, (b + 1) * C)
            lows = slice((3 + b) * C, (4 + b) * C)
            weights_out[a * C : (a + 1) * C, cols] = high
            weights_out[a * C : (a + 1) * C, lows] = low
            weights_out[(3 + a) * C : (4 + a) * C, cols] = high
            weights_out[(3 + a) * C : (4 + a) * C, lows] = jnp.zeros((C, C), jnp.bfloat16)
    codes[...] = jnp.zeros((C, C), f32)
    codes[:TALL, :TC] = code[...]
    second = repeat_blocks(erased[1].astype(f32), TR)
    codes[TALL : TALL + TR, :TC] = jnp.where(second > 0.5, 2.0, syndromes[1].astype(f32))
    turned[...] = codes[...].T
    values, vector = table[...], lost_vector[...]
    for r in range(HALO - 1, HALO + TR + 1):
        column = jnp.broadcast_to(turned[:TC, r : r + 1], (TC, C))
        first_out[r - HALO + 1] = embed(column, values, vector)
    for r in range(TR):
        column = jnp.broadcast_to(turned[:TC, TALL + r : TALL + r + 1], (TC, C))
        second_out[r] = embed(column, values, vector)


def first_kernel(
    me,
    state,
    top,
    bottom,
    right,
    left,
    inputs,
    weights,
    lost,
    ids,
    erased,
    ext_out,
    pre_out,
    slots_out,
    names,
):
    f32 = jnp.float32
    sub = lax.broadcasted_iota(jnp.int32, (8, C), 0)
    ext_out[HALO : HALO + TR, :TC] = state[...]
    ext_out[:HALO, :TC] = top[:HALO]
    ext_out[HALO + TR :, :TC] = bottom[:HALO]
    for r in range(TALL):
        ext_out[r, TC:] = jnp.where(sub < 4, right[r], left[r])

    names[...] = jnp.zeros((64, C), f32)
    for r in range(BROWS):
        names[r : r + 1] = right[r, 5:6, :]
        names[16 + r : 17 + r] = left[r, 2:3, :]
        names[32 + r : 33 + r] = right[r, 6:7, :]
        names[48 + r : 49 + r] = left[r, 1:2, :]
    lane = lax.broadcasted_iota(jnp.int32, (16, C), 1)
    wide = TC // BS

    def widen(mid, at):
        return jnp.where(
            lane < wide,
            mid,
            jnp.where(
                lane == wide,
                names[at : at + 16],
                jnp.where(lane == wide + 1, names[at + 16 : at + 32], 0.0),
            ),
        ).astype(jnp.int32)

    slots_out[...] = slots_of(widen(ids[...], 32) & 127, me[0], me[1]) + 128 * widen(
        lost[...], 0
    )
    slots_out[1 : 1 + TR // BS, :wide] += 256 * erased[1]

    pre_out[0] = jnp.zeros((WIDE, C), f32)
    pre_out[CONV_ROWS - 1] = jnp.zeros((WIDE, C), f32)
    pre_out[1 : CONV_ROWS - 1, :TC] = inputs[...]
    for r in range(HALO - 1, HALO + TR + 1):
        pre_out[r - 2, TC:] = jnp.where(
            sub == 0,
            pltpu.roll(right[r], 4, 0),
            jnp.where(sub == 7, pltpu.roll(left[r], 4, 0), 0.0),
        )
    rows = 12

    def step(i, carry):
        start = i * rows
        pre_out[pl.ds(start, rows)] += conv_chunk(
            lambda a: ext_out[pl.ds(start + 1 + a, rows)], weights[...], rows
        )
        return carry

    lax.fori_loop(0, CONV_ROWS // rows, step, 0)


def group_sum(total, sub):
    near = jnp.where(sub % 2 == 0, pltpu.roll(total, 7, 0), pltpu.roll(total, 1, 0))
    total = total + near
    far = jnp.where(sub % 4 < 2, pltpu.roll(total, 6, 0), pltpu.roll(total, 2, 0))
    return total + far


def readout(sites, right, flag_a, flag_b, offset, sub):
    high, low = split(sites.reshape(32, C))
    left = jnp.concatenate(
        [jnp.concatenate([high, high], axis=1), jnp.concatenate([low, low], axis=1)],
        axis=0,
    )
    mixed = jnp.dot(left, right, preferred_element_type=jnp.float32)
    mixed = (mixed[:32] + mixed[32:]).reshape(4, 8, 2 * C)
    mixed = jnp.tanh(jnp.where(sub[None] < 4, mixed[:, :, :C], mixed[:, :, C:]))
    total = mixed[0] + mixed[1] + mixed[2] + mixed[3]
    flags = jnp.where(sub < 4, flag_a, flag_b)
    return jnp.tanh(group_sum(total, sub) * 0.0625 + flags * offset)


PIECES = (16, 8, 8, 8, 8, 8, 8) * 2


def second_kernel(
    slots, me, offset, ext_hbm, pre_hbm, inputs_hbm, weights_hbm, *rest
):
    pieces = rest[:14]
    out, table, first, field, second, ext, pre, inputs, weights, sems = rest[14:]
    later = [
        pltpu.make_async_copy(ext_hbm, ext, sems.at[0]),
        pltpu.make_async_copy(pre_hbm, pre, sems.at[1]),
        pltpu.make_async_copy(weights_hbm, weights, sems.at[2]),
        pltpu.make_async_copy(inputs_hbm, inputs, sems.at[3]),
    ]
    for copy in later:
        copy.start()
    at = 0
    for piece, count in zip(pieces, PIECES):

        def halve(i, carry, piece=piece, at=at):
            for k in range(4):
                high, low = split(piece[4 * i + k])
                table[at + 4 * i + k, :C] = high
                table[at + 4 * i + k, C:] = low
            return carry

        lax.fori_loop(0, count // 4, halve, 0)
        at += count
    later[0].wait()
    sub = lax.broadcasted_iota(jnp.int32, (8, C), 0)
    shift = offset[...]

    def read_first(step, carry):
        for br, g in [(5 * step + k, g) for k in range(5) for g in range(GROUPS)]:
            one, two = slots[br, 2 * g], slots[br, 2 * g + 1]
            first[br, 8 * g : 8 * g + 8] = readout(
                ext[pl.ds(br * BS, BS), 8 * g : 8 * g + 8],
                jnp.concatenate([table[one & 127], table[two & 127]], axis=1),
                ((one >> 7) & 1).astype(jnp.float32),
                ((two >> 7) & 1).astype(jnp.float32),
                shift,
                sub,
            )
        return carry

    lax.fori_loop(0, BROWS // 5, read_first, 0)

    later[1].wait()

    def update(row, br):
        field[row + 1] = 0.5 * ext[row + HALO] + jnp.tanh(pre[row + 2] + first[br])

    update(-1, 0)
    update(TR, BROWS - 1)

    def update_block(br, carry):
        for r in range(BS):
            update(br * BS + r, br + 1)
        return carry

    lax.fori_loop(0, TR // BS, update_block, 0)
    field[0] = field[0] * (me[0] > 0).astype(jnp.float32)
    field[TR + 1] = field[TR + 1] * (me[0] < me[2]).astype(jnp.float32)
    edge = lax.broadcasted_iota(jnp.int32, (TR + 2, 8, C), 1)
    kept = jnp.where(
        edge < 4, (me[1] < me[3]).astype(jnp.float32), (me[1] > 0).astype(jnp.float32)
    )
    field[:, TC:] = field[:, TC:] * kept

    def read_second(step, carry):
        for br, g in [(4 * step + k, g) for k in range(4) for g in range(TC // 8)]:
            one, two = slots[br + 1, 2 * g], slots[br + 1, 2 * g + 1]
            second[br, 8 * g : 8 * g + 8] = readout(
                field[pl.ds(br * BS + 1, BS), 8 * g : 8 * g + 8],
                jnp.concatenate([table[one & 127], table[two & 127]], axis=1),
                (one >> 8).astype(jnp.float32),
                (two >> 8).astype(jnp.float32),
                shift,
                sub,
            )
        return carry

    lax.fori_loop(0, TR // BS // 4, read_second, 0)
    later[2].wait()
    later[3].wait()
    rows = 8

    def finish(i, carry):
        start = i * rows
        sums = conv_chunk(
            lambda a: field[pl.ds(start + a, rows)], weights[...], rows
        )[:, :TC]
        for half in range(rows // BS):
            at = start + half * BS
            out[pl.ds(at, BS)] = 0.5 * field[pl.ds(at + 1, BS), :TC] + jnp.tanh(
                sums[half * BS : (half + 1) * BS]
                + inputs[pl.ds(at, BS)]
                + second[i * (rows // BS) + half][None]
            )
        return carry

    lax.fori_loop(0, TR // rows, finish, 0)


def decode(
    state,
    syndromes,
    erased,
    readers,
    conv_weight,
    syndrome_table,
    erasure_vector,
    read_weight,
    erasure_offset,
):
    f32 = jnp.float32
    gx, gy = lax.axis_index("gx"), lax.axis_index("gy")
    gx_count, gy_count = lax.axis_size("gx"), lax.axis_size("gy")
    me = jnp.stack([gx, gy, gx_count - 1, gy_count - 1]).astype(jnp.int32)
    names = readers.reshape(1, -1)
    lost_vector, offset = erasure_vector[None], erasure_offset[None]
    vmem = pl.BlockSpec(memory_space=pltpu.VMEM)
    smem = pl.BlockSpec(memory_space=pltpu.SMEM)
    anywhere = pl.BlockSpec(memory_space=pl.ANY)
    hbm = pl.BlockSpec(memory_space=pltpu.HBM)

    def shape(*dims, dtype=f32):
        return jax.ShapeDtypeStruct(dims, dtype)

    up_pay, down_pay, copies = pl.pallas_call(
        rows_kernel,
        name="pack_rows",
        out_shape=(
            shape(HALO + 1, TC, C),
            shape(HALO + 1, TC, C),
            shape(16, C, C),
        ),
        in_specs=[anywhere, vmem, vmem, vmem, vmem],
        out_specs=(vmem, vmem, anywhere),
        scratch_shapes=[pltpu.SemaphoreType.DMA((2,)), pltpu.SemaphoreType.DMA((16,))],
    )(state, read_weight, syndromes, erased, names)

    up = [(i, i - 1) for i in range(1, gx_count)]
    down = [(i, i + 1) for i in range(gx_count - 1)]
    top = lax.ppermute(down_pay, "gx", down)
    bottom = lax.ppermute(up_pay, "gx", up)

    west_pay, east_pay, code, lost, ids = pl.pallas_call(
        cols_kernel,
        name="pack_cols",
        out_shape=(
            shape(TALL, 8, C),
            shape(TALL, 8, C),
            shape(TALL, TC),
            shape(16, C),
            shape(16, C),
        ),
        in_specs=[vmem] * 8,
        out_specs=(vmem,) * 5,
        scratch_shapes=[pltpu.VMEM((TALL + 32, C), f32)],
    )(state, top, bottom, syndromes, erased, names, syndrome_table, lost_vector)

    west = [(i, i - 1) for i in range(1, gy_count)]
    east = [(i, i + 1) for i in range(gy_count - 1)]
    left = lax.ppermute(east_pay, "gy", east)
    right = lax.ppermute(west_pay, "gy", west)
    pieces = gather_weights(copies)

    inputs_first, inputs, weights = pl.pallas_call(
        prepare_kernel,
        name="prepare",
        compiler_params=pltpu.CompilerParams(vmem_limit_bytes=60 * 2**20),
        out_shape=(shape(TR + 2, TC, C), shape(TR, TC, C), shape(6 * C, 6 * C, dtype=jnp.bfloat16)),
        in_specs=[vmem] * 6,
        out_specs=(vmem,) * 3,
        scratch_shapes=[pltpu.VMEM((C, C), f32), pltpu.VMEM((C, C), f32)],
    )(conv_weight, code, syndromes, erased, syndrome_table, lost_vector)

    ext, pre, slots = pl.pallas_call(
        first_kernel,
        name="conv_first",
        compiler_params=pltpu.CompilerParams(vmem_limit_bytes=60 * 2**20),
        out_shape=(shape(TALL, WIDE, C), shape(CONV_ROWS, WIDE, C), shape(16, C, dtype=jnp.int32)),
        in_specs=[smem] + [vmem] * 10,
        out_specs=(vmem,) * 3,
        scratch_shapes=[pltpu.VMEM((64, C), f32)],
        cost_estimate=pl.CostEstimate(
            flops=2_000_000_000, bytes_accessed=6_000_000, transcendentals=0
        ),
    )(me, state, top, bottom, right, left, inputs_first, weights, lost, ids, erased)

    return pl.pallas_call(
        second_kernel,
        name="read_and_finish",
        compiler_params=pltpu.CompilerParams(vmem_limit_bytes=44 * 2**20),
        out_shape=shape(TR, TC, C),
        in_specs=[smem] * 2 + [vmem] + [hbm] * 4 + [vmem] * 14,
        out_specs=vmem,
        scratch_shapes=[
            pltpu.VMEM((128, 2 * C, C), jnp.bfloat16),
            pltpu.VMEM((BROWS, WIDE, C), f32),
            pltpu.VMEM((TR + 2, WIDE, C), f32),
            pltpu.VMEM((TR // BS, TC, C), f32),
            pltpu.VMEM((TALL, WIDE, C), f32),
            pltpu.VMEM((CONV_ROWS, WIDE, C), f32),
            pltpu.VMEM((TR, TC, C), f32),
            pltpu.VMEM((6 * C, 6 * C), jnp.bfloat16),
            pltpu.SemaphoreType.DMA((4,)),
        ],
        cost_estimate=pl.CostEstimate(
            flops=4_000_000_000, bytes_accessed=12_000_000, transcendentals=1_000_000
        ),
    )(slots, me, offset, ext, pre, inputs, weights, *pieces)


def solution(mesh):
    placed = (
        P("gx", "gy", None),
        P(None, "gx", "gy"),
        P(None, "gx", "gy"),
        P(("gx", "gy"), None),
        P(),
        P(),
        P(),
        P(("gx", "gy"), None),
        P(),
    )
    return jax.shard_map(
        decode, mesh=mesh, in_specs=placed, out_specs=P("gx", "gy", None), check_vma=False
    )
```

```python
import jax
import jax.numpy as jnp
from jax import lax
from jax.experimental import pallas as pl
from jax.experimental.pallas import tpu as pltpu
from jax.sharding import PartitionSpec as P


BS = 4
C = 128
TR = 32
TC = 64
HALO = 4
WIDE = TC + 2 * HALO
TALL = TR + 2 * HALO
BROWS = TALL // BS
GROUPS = WIDE // 8
CONV_ROWS = TR + 4
AX = ("gx", "gy")


def flat_id(z, y, x, c):
    return ((z % 4 * 4 + y % 4) * 4 + x % 4) * 2 + c


SITES = [
    (z, y, x, c) for z in range(4) for y in range(4) for x in range(4) for c in range(2)
]


def class_groups():
    groups = {}
    for z, y, x, c in SITES:
        groups.setdefault(((x + z) % 2, (y + z) % 2, c), []).append(flat_id(z, y, x, c))
    return [groups[k] for k in sorted(groups)]


def moved(dz, dy, dx):
    return [
        (flat_id(z, y, x, c), flat_id(z + dz, y + dy, x + dx, c)) for z, y, x, c in SITES
    ]


PARTNER = [(flat_id(z, y, x, c), flat_id(z, y, x, 1 - c)) for z, y, x, c in SITES]


def gather_weights(copies):
    own = lax.all_to_all(copies, AX, 0, 0, tiled=True, axis_index_groups=class_groups())
    low, high = own[:8], own[8:]
    pieces = [own]
    for step in ((0, 0, 1), (0, 1, 0), (1, 0, 0)):
        back = tuple(-s for s in step)
        pieces.append(lax.ppermute(low, AX, moved(*step)))
        pieces.append(lax.ppermute(high, AX, moved(*back)))
    pieces += [lax.ppermute(piece, AX, PARTNER) for piece in pieces]
    return pieces


def split(value):
    high = value.astype(jnp.bfloat16)
    return high, (value - high.astype(jnp.float32)).astype(jnp.bfloat16)


def conv_chunk(cells, weights, rows):
    half = rows // 2
    paired = cells.reshape(half + 1, 2, WIDE, C)
    d0, d1, d2, d3 = paired[:half, 0], paired[:half, 1], paired[1:, 0], paired[1:, 1]
    parts = []
    for q, plane in enumerate((d0 - d2, d1 + d2, d2 - d1, d1 - d3)):
        left = jnp.concatenate(split(plane.reshape(half * WIDE, C)), axis=1)
        sums = jnp.dot(
            left, weights[q * 2 * C : (q + 1) * 2 * C], preferred_element_type=jnp.float32
        )
        parts.append((sums[:, : 3 * C] + sums[:, 3 * C :]).reshape(half, WIDE, 3 * C))
    m1, m2, m3, m4 = parts

    def join(sums):
        return (
            pltpu.roll(sums[:, :, :C], 1, 1)
            + sums[:, :, C : 2 * C]
            + pltpu.roll(sums[:, :, 2 * C :], WIDE - 1, 1)
        )

    pair = [join(m1 + m2 + m3)[:, None], join(m2 - m3 - m4)[:, None]]
    return jnp.concatenate(pair, axis=1).reshape(rows, WIDE, C)


def rows_kernel(
    state, weight, syndromes, erased, readers, up, down, copies, rows_sem, copies_sem
):
    moves = [
        pltpu.make_async_copy(state.at[pl.ds(0, HALO)], up.at[pl.ds(0, HALO)], rows_sem.at[0]),
        pltpu.make_async_copy(
            state.at[pl.ds(TR - HALO, HALO)], down.at[pl.ds(0, HALO)], rows_sem.at[1]
        ),
    ]
    moves += [
        pltpu.make_async_copy(weight, copies.at[i], copies_sem.at[i]) for i in range(16)
    ]
    for move in moves:
        move.start()
    ids = readers[...].astype(jnp.float32)
    for pay, row, block_row in ((up, 0, 0), (down, TR - 1, TR // BS - 1)):
        pay[HALO] = jnp.zeros((TC, C), jnp.float32)
        pay[HALO, 0:1, :TC] = syndromes[0, row : row + 1, :].astype(jnp.float32)
        pay[HALO, 1:2, : TC // BS] = erased[0, block_row : block_row + 1, :].astype(
            jnp.float32
        )
        first = block_row * (TC // BS)
        pay[HALO, 2:3, :] = pltpu.roll(ids, (C - first) % C, 1)
    for move in moves:
        move.wait()


def repeat_blocks(blocks, rows):
    count = blocks.shape[0]
    row = lax.broadcasted_iota(jnp.int32, (rows, count), 0)
    tall = (row // BS == lax.broadcasted_iota(jnp.int32, (rows, count), 1)).astype(jnp.bfloat16)
    col = lax.broadcasted_iota(jnp.int32, (TC // BS, TC), 1)
    wide = (col // BS == lax.broadcasted_iota(jnp.int32, (TC // BS, TC), 0)).astype(jnp.bfloat16)
    half = jnp.dot(tall, blocks.astype(jnp.bfloat16), preferred_element_type=jnp.float32)
    return jnp.dot(half.astype(jnp.bfloat16), wide, preferred_element_type=jnp.float32)


def embed(code, table, lost_vector):
    return jnp.where(
        code > 1.5, lost_vector, jnp.where(code > 0.5, table[1:2], table[0:1])
    )


def cols_kernel(
    state,
    top,
    bottom,
    syndromes,
    erased,
    readers,
    table,
    lost_vector,
    west,
    east,
    code_out,
    lost_out,
    ids_out,
    vectors,
):
    f32 = jnp.float32
    block_rows, block_cols = TR // BS, TC // BS
    lost_out[...] = jnp.zeros((16, C), f32)
    ids_out[...] = jnp.zeros((16, C), f32)
    code_out[...] = jnp.zeros((TALL, TC), f32)
    lost_out[0:1, :block_cols] = top[HALO, 1:2, :block_cols]
    lost_out[BROWS - 1 : BROWS, :block_cols] = bottom[HALO, 1:2, :block_cols]
    lost_out[1 : 1 + block_rows, :block_cols] = erased[0].astype(f32)
    lane = lax.broadcasted_iota(jnp.int32, (1, C), 1)
    ids_out[0:1, :] = jnp.where(lane < block_cols, top[HALO, 2:3, :], 0.0)
    ids_out[BROWS - 1 : BROWS, :] = jnp.where(lane < block_cols, bottom[HALO, 2:3, :], 0.0)
    ids = readers[...].astype(f32)
    for k in range(block_rows):
        turned = pltpu.roll(ids, (C - k * block_cols) % C, 1)
        ids_out[k + 1 : k + 2, :] = jnp.where(lane < block_cols, turned, 0.0)
    code_out[HALO - 1 : HALO, :] = top[HALO, 0:1, :TC]
    code_out[HALO : HALO + TR, :] = syndromes[0].astype(f32)
    code_out[HALO + TR : HALO + TR + 1, :] = bottom[HALO, 0:1, :TC]
    sites = repeat_blocks(lost_out[:, :block_cols], TALL)
    code_out[...] = jnp.where(sites > 0.5, 2.0, code_out[...])
    sub = lax.broadcasted_iota(jnp.int32, (8, C), 0)
    for pay, edge, keep, at in ((west, 0, sub < 4, 4), (east, TC - 1, sub >= 4, 0)):
        block = edge // BS
        group = edge // 8 * 8
        code = jnp.broadcast_to(code_out[:, edge : edge + 1], (TALL, C))
        vectors[:TALL] = embed(code, table, lost_vector[...])
        vectors[TALL : TALL + 16] = jnp.broadcast_to(lost_out[:, block : block + 1], (16, C))
        vectors[TALL + 16 :] = jnp.broadcast_to(ids_out[:, block : block + 1], (16, C))
        _, second, third = (4, 5, 6) if at == 4 else (3, 2, 1)
        for r in range(TALL):
            if r < HALO:
                cells = top[r, group : group + 8]
            elif r < HALO + TR:
                cells = state[r - HALO, group : group + 8]
            else:
                cells = bottom[r - HALO - TR, group : group + 8]
            extra = jnp.broadcast_to(vectors[r : r + 1], (8, C))
            if r < BROWS:
                flag = jnp.broadcast_to(vectors[TALL + r : TALL + r + 1], (8, C))
                name = jnp.broadcast_to(vectors[TALL + 16 + r : TALL + 17 + r], (8, C))
                extra = jnp.where(sub == second, flag, jnp.where(sub == third, name, extra))
            pay[r] = jnp.where(keep, cells, extra)


def slots_of(ids, gx, gy):
    mz, my, mx, mc = gx >> 2, gx & 3, gy >> 1, gy & 1
    z, y, x, c = ids >> 5, (ids >> 3) & 3, (ids >> 1) & 3, ids & 1
    side = ((x + z + mx + mz) & 1) + 2 * ((y + z + my + mz) & 1)
    return (((c + mc) & 1) * 4 + side) * 16 + z * 4 + (y >> 1) * 2 + (x >> 1)


def prepare_kernel(
    me,
    taps,
    code,
    syndromes,
    erased,
    table,
    lost_vector,
    first_out,
    second_out,
    weights_out,
    codes,
    turned,
):
    f32 = jnp.float32
    for b in range(3):
        g0, g1, g2 = taps[b], taps[3 + b], taps[6 + b]
        mixed = (g0, (g0 + g1 + g2) * 0.5, (g0 - g1 + g2) * 0.5, g2)
        for q in range(4):
            high, low = split(mixed[q])
            top, mid, end = 2 * q * C, (2 * q + 1) * C, (2 * q + 2) * C
            cols = slice(b * C, (b + 1) * C)
            lows = slice((3 + b) * C, (4 + b) * C)
            weights_out[top:mid, cols] = high
            weights_out[top:mid, lows] = low
            weights_out[mid:end, cols] = high
            weights_out[mid:end, lows] = jnp.zeros((C, C), jnp.bfloat16)
    codes[...] = jnp.zeros((C, C), f32)
    codes[:TALL, :TC] = code[...]
    second = repeat_blocks(erased[1].astype(f32), TR)
    codes[TALL : TALL + TR, :TC] = jnp.where(second > 0.5, 2.0, syndromes[1].astype(f32))
    turned[...] = codes[...].T
    values, vector = table[...], lost_vector[...]
    for r in range(HALO - 1, HALO + TR + 1):
        column = jnp.broadcast_to(turned[:TC, r : r + 1], (TC, C))
        first_out[r - HALO + 1] = embed(column, values, vector)
    for r in range(TR):
        column = jnp.broadcast_to(turned[:TC, TALL + r : TALL + r + 1], (TC, C))
        second_out[r] = embed(column, values, vector)


def first_kernel(
    me,
    state,
    top,
    bottom,
    right,
    left,
    inputs,
    weights,
    lost,
    ids,
    erased,
    ext_out,
    pre_out,
    slots_out,
    names,
):
    f32 = jnp.float32
    sub = lax.broadcasted_iota(jnp.int32, (8, C), 0)
    ext_out[HALO : HALO + TR, :TC] = state[...]
    ext_out[:HALO, :TC] = top[:HALO]
    ext_out[HALO + TR :, :TC] = bottom[:HALO]
    for r in range(TALL):
        ext_out[r, TC:] = jnp.where(sub < 4, right[r], left[r])

    names[...] = jnp.zeros((64, C), f32)
    for r in range(BROWS):
        names[r : r + 1] = right[r, 5:6, :]
        names[16 + r : 17 + r] = left[r, 2:3, :]
        names[32 + r : 33 + r] = right[r, 6:7, :]
        names[48 + r : 49 + r] = left[r, 1:2, :]
    lane = lax.broadcasted_iota(jnp.int32, (16, C), 1)
    wide = TC // BS

    def widen(mid, at):
        return jnp.where(
            lane < wide,
            mid,
            jnp.where(
                lane == wide,
                names[at : at + 16],
                jnp.where(lane == wide + 1, names[at + 16 : at + 32], 0.0),
            ),
        ).astype(jnp.int32)

    slots_out[...] = slots_of(widen(ids[...], 32) & 127, me[0], me[1]) + 128 * widen(
        lost[...], 0
    )
    slots_out[1 : 1 + TR // BS, :wide] += 256 * erased[1]

    pre_out[0] = jnp.zeros((WIDE, C), f32)
    pre_out[CONV_ROWS - 1] = jnp.zeros((WIDE, C), f32)
    pre_out[1 : CONV_ROWS - 1, :TC] = inputs[...]
    for r in range(HALO - 1, HALO + TR + 1):
        pre_out[r - 2, TC:] = jnp.where(
            sub == 0,
            pltpu.roll(right[r], 4, 0),
            jnp.where(sub == 7, pltpu.roll(left[r], 4, 0), 0.0),
        )
    rows = 12

    def step(i, carry):
        start = i * rows
        pre_out[pl.ds(start, rows)] += conv_chunk(
            ext_out[pl.ds(start + 1, rows + 2)], weights, rows
        )
        return carry

    lax.fori_loop(0, CONV_ROWS // rows, step, 0)


def group_sum(total, sub):
    near = jnp.where(sub % 2 == 0, pltpu.roll(total, 7, 0), pltpu.roll(total, 1, 0))
    total = total + near
    far = jnp.where(sub % 4 < 2, pltpu.roll(total, 6, 0), pltpu.roll(total, 2, 0))
    return total + far


def readout(sites, right, flag_a, flag_b, offset, sub):
    high, low = split(sites.reshape(32, C))
    left = jnp.concatenate(
        [jnp.concatenate([high, high], axis=1), jnp.concatenate([low, low], axis=1)],
        axis=0,
    )
    mixed = jnp.dot(left, right, preferred_element_type=jnp.float32)
    mixed = (mixed[:32] + mixed[32:]).reshape(4, 8, 2 * C)
    mixed = jnp.tanh(jnp.where(sub[None] < 4, mixed[:, :, :C], mixed[:, :, C:]))
    total = mixed[0] + mixed[1] + mixed[2] + mixed[3]
    flags = jnp.where(sub < 4, flag_a, flag_b)
    return jnp.tanh(group_sum(total, sub) * 0.0625 + flags * offset)


PIECES = (16, 8, 8, 8, 8, 8, 8) * 2


def second_kernel(
    slots, me, offset, ext_hbm, pre_hbm, inputs_hbm, weights_hbm, *rest
):
    pieces = rest[:14]
    out, table, first, field, second, ext, pre, inputs, weights, sems = rest[14:]
    later = [
        pltpu.make_async_copy(ext_hbm, ext, sems.at[0]),
        pltpu.make_async_copy(pre_hbm, pre, sems.at[1]),
        pltpu.make_async_copy(weights_hbm, weights, sems.at[2]),
        pltpu.make_async_copy(inputs_hbm, inputs, sems.at[3]),
    ]
    for copy in later:
        copy.start()
    at = 0
    for piece, count in zip(pieces, PIECES):

        def halve(i, carry, piece=piece, at=at):
            for k in range(4):
                high, low = split(piece[4 * i + k])
                table[at + 4 * i + k, :C] = high
                table[at + 4 * i + k, C:] = low
            return carry

        lax.fori_loop(0, count // 4, halve, 0)
        at += count
    later[0].wait()
    sub = lax.broadcasted_iota(jnp.int32, (8, C), 0)
    shift = offset[...]

    def read_first(step, carry):
        for br, g in [(5 * step + k, g) for k in range(5) for g in range(GROUPS)]:
            one, two = slots[br, 2 * g], slots[br, 2 * g + 1]
            first[br, 8 * g : 8 * g + 8] = readout(
                ext[pl.ds(br * BS, BS), 8 * g : 8 * g + 8],
                jnp.concatenate([table[one & 127], table[two & 127]], axis=1),
                ((one >> 7) & 1).astype(jnp.float32),
                ((two >> 7) & 1).astype(jnp.float32),
                shift,
                sub,
            )
        return carry

    lax.fori_loop(0, BROWS // 5, read_first, 0)

    later[1].wait()

    def update(row, br):
        field[row + 1] = 0.5 * ext[row + HALO] + jnp.tanh(pre[row + 2] + first[br])

    update(-1, 0)
    update(TR, BROWS - 1)

    def update_block(br, carry):
        for r in range(BS):
            update(br * BS + r, br + 1)
        return carry

    lax.fori_loop(0, TR // BS, update_block, 0)
    field[0] = field[0] * (me[0] > 0).astype(jnp.float32)
    field[TR + 1] = field[TR + 1] * (me[0] < me[2]).astype(jnp.float32)
    edge = lax.broadcasted_iota(jnp.int32, (TR + 2, 8, C), 1)
    kept = jnp.where(
        edge < 4, (me[1] < me[3]).astype(jnp.float32), (me[1] > 0).astype(jnp.float32)
    )
    field[:, TC:] = field[:, TC:] * kept

    def read_second(step, carry):
        for br, g in [(4 * step + k, g) for k in range(4) for g in range(TC // 8)]:
            one, two = slots[br + 1, 2 * g], slots[br + 1, 2 * g + 1]
            second[br, 8 * g : 8 * g + 8] = readout(
                field[pl.ds(br * BS + 1, BS), 8 * g : 8 * g + 8],
                jnp.concatenate([table[one & 127], table[two & 127]], axis=1),
                (one >> 8).astype(jnp.float32),
                (two >> 8).astype(jnp.float32),
                shift,
                sub,
            )
        return carry

    lax.fori_loop(0, TR // BS // 4, read_second, 0)
    later[2].wait()
    later[3].wait()
    rows = 16

    def finish(i, carry):
        start = i * rows
        sums = conv_chunk(field[pl.ds(start, rows + 2)], weights, rows)[:, :TC]
        for half in range(rows // BS):
            at = start + half * BS
            out[pl.ds(at, BS)] = 0.5 * field[pl.ds(at + 1, BS), :TC] + jnp.tanh(
                sums[half * BS : (half + 1) * BS]
                + inputs[pl.ds(at, BS)]
                + second[i * (rows // BS) + half][None]
            )
        return carry

    lax.fori_loop(0, TR // rows, finish, 0)


def decode(
    state,
    syndromes,
    erased,
    readers,
    conv_weight,
    syndrome_table,
    erasure_vector,
    read_weight,
    erasure_offset,
):
    f32 = jnp.float32
    gx, gy = lax.axis_index("gx"), lax.axis_index("gy")
    gx_count, gy_count = lax.axis_size("gx"), lax.axis_size("gy")
    me = jnp.stack([gx, gy, gx_count - 1, gy_count - 1]).astype(jnp.int32)
    names = readers.reshape(1, -1)
    lost_vector, offset = erasure_vector[None], erasure_offset[None]
    vmem = pl.BlockSpec(memory_space=pltpu.VMEM)
    smem = pl.BlockSpec(memory_space=pltpu.SMEM)
    anywhere = pl.BlockSpec(memory_space=pl.ANY)
    hbm = pl.BlockSpec(memory_space=pltpu.HBM)

    def shape(*dims, dtype=f32):
        return jax.ShapeDtypeStruct(dims, dtype)

    up_pay, down_pay, copies = pl.pallas_call(
        rows_kernel,
        name="pack_rows",
        out_shape=(
            shape(HALO + 1, TC, C),
            shape(HALO + 1, TC, C),
            shape(16, C, C),
        ),
        in_specs=[anywhere, vmem, vmem, vmem, vmem],
        out_specs=(vmem, vmem, anywhere),
        scratch_shapes=[pltpu.SemaphoreType.DMA((2,)), pltpu.SemaphoreType.DMA((16,))],
    )(state, read_weight, syndromes, erased, names)

    up = [(i, i - 1) for i in range(1, gx_count)]
    down = [(i, i + 1) for i in range(gx_count - 1)]
    top = lax.ppermute(down_pay, "gx", down)
    bottom = lax.ppermute(up_pay, "gx", up)

    west_pay, east_pay, code, lost, ids = pl.pallas_call(
        cols_kernel,
        name="pack_cols",
        out_shape=(
            shape(TALL, 8, C),
            shape(TALL, 8, C),
            shape(TALL, TC),
            shape(16, C),
            shape(16, C),
        ),
        in_specs=[vmem] * 8,
        out_specs=(vmem,) * 5,
        scratch_shapes=[pltpu.VMEM((TALL + 32, C), f32)],
    )(state, top, bottom, syndromes, erased, names, syndrome_table, lost_vector)

    west = [(i, i - 1) for i in range(1, gy_count)]
    east = [(i, i + 1) for i in range(gy_count - 1)]
    left = lax.ppermute(east_pay, "gy", east)
    right = lax.ppermute(west_pay, "gy", west)
    pieces = gather_weights(copies)

    inputs_first, inputs, weights = pl.pallas_call(
        prepare_kernel,
        name="prepare",
        compiler_params=pltpu.CompilerParams(vmem_limit_bytes=60 * 2**20),
        out_shape=(shape(TR + 2, TC, C), shape(TR, TC, C), shape(8 * C, 6 * C, dtype=jnp.bfloat16)),
        in_specs=[smem] + [vmem] * 6,
        out_specs=(vmem,) * 3,
        scratch_shapes=[pltpu.VMEM((C, C), f32), pltpu.VMEM((C, C), f32)],
    )(me, conv_weight, code, syndromes, erased, syndrome_table, lost_vector)

    ext, pre, slots = pl.pallas_call(
        first_kernel,
        name="conv_first",
        compiler_params=pltpu.CompilerParams(vmem_limit_bytes=60 * 2**20),
        out_shape=(shape(TALL, WIDE, C), shape(CONV_ROWS, WIDE, C), shape(16, C, dtype=jnp.int32)),
        in_specs=[smem] + [vmem] * 10,
        out_specs=(vmem,) * 3,
        scratch_shapes=[pltpu.VMEM((64, C), f32)],
        cost_estimate=pl.CostEstimate(
            flops=2_000_000_000, bytes_accessed=6_000_000, transcendentals=0
        ),
    )(me, state, top, bottom, right, left, inputs_first, weights, lost, ids, erased)

    return pl.pallas_call(
        second_kernel,
        name="read_and_finish",
        compiler_params=pltpu.CompilerParams(vmem_limit_bytes=44 * 2**20),
        out_shape=shape(TR, TC, C),
        in_specs=[smem] * 2 + [vmem] + [hbm] * 4 + [vmem] * 14,
        out_specs=vmem,
        scratch_shapes=[
            pltpu.VMEM((128, 2 * C, C), jnp.bfloat16),
            pltpu.VMEM((BROWS, WIDE, C), f32),
            pltpu.VMEM((TR + 2, WIDE, C), f32),
            pltpu.VMEM((TR // BS, TC, C), f32),
            pltpu.VMEM((TALL, WIDE, C), f32),
            pltpu.VMEM((CONV_ROWS, WIDE, C), f32),
            pltpu.VMEM((TR, TC, C), f32),
            pltpu.VMEM((8 * C, 6 * C), jnp.bfloat16),
            pltpu.SemaphoreType.DMA((4,)),
        ],
        cost_estimate=pl.CostEstimate(
            flops=4_000_000_000, bytes_accessed=12_000_000, transcendentals=1_000_000
        ),
    )(slots, me, offset, ext, pre, inputs, weights, *pieces)


def solution(mesh):
    placed = (
        P("gx", "gy", None),
        P(None, "gx", "gy"),
        P(None, "gx", "gy"),
        P(("gx", "gy"), None),
        P(),
        P(),
        P(),
        P(("gx", "gy"), None),
        P(),
    )
    return jax.shard_map(
        decode, mesh=mesh, in_specs=placed, out_specs=P("gx", "gy", None), check_vma=False
    )
```

```python
import jax
import jax.numpy as jnp
from jax import lax
from jax.experimental import pallas as pl
from jax.experimental.pallas import tpu as pltpu
from jax.sharding import PartitionSpec as P


BS = 4
C = 128
TR = 32
TC = 64
HALO = 4
WIDE = TC + 2 * HALO
TALL = TR + 2 * HALO
BROWS = TALL // BS
GROUPS = WIDE // 8
CONV_ROWS = TR + 4
AX = ("gx", "gy")


def flat_id(z, y, x, c):
    return ((z % 4 * 4 + y % 4) * 4 + x % 4) * 2 + c


SITES = [
    (z, y, x, c) for z in range(4) for y in range(4) for x in range(4) for c in range(2)
]


def class_groups():
    groups = {}
    for z, y, x, c in SITES:
        groups.setdefault(((x + z) % 2, (y + z) % 2, c), []).append(flat_id(z, y, x, c))
    return [groups[k] for k in sorted(groups)]


def moved(dz, dy, dx):
    return [
        (flat_id(z, y, x, c), flat_id(z + dz, y + dy, x + dx, c)) for z, y, x, c in SITES
    ]


PARTNER = [(flat_id(z, y, x, c), flat_id(z, y, x, 1 - c)) for z, y, x, c in SITES]


def gather_weights(copies):
    own = lax.all_to_all(copies, AX, 0, 0, tiled=True, axis_index_groups=class_groups())
    low, high = own[:8], own[8:]
    pieces = [own]
    for step in ((0, 0, 1), (0, 1, 0), (1, 0, 0)):
        back = tuple(-s for s in step)
        pieces.append(lax.ppermute(low, AX, moved(*step)))
        pieces.append(lax.ppermute(high, AX, moved(*back)))
    pieces += [lax.ppermute(piece, AX, PARTNER) for piece in pieces]
    return pieces


def split(value):
    high = value.astype(jnp.bfloat16)
    return high, (value - high.astype(jnp.float32)).astype(jnp.bfloat16)


def conv_chunk(cells, weights, rows):
    half = rows // 2
    paired = cells.reshape(half + 1, 2, WIDE, C)
    d0, d1, d2, d3 = paired[:half, 0], paired[:half, 1], paired[1:, 0], paired[1:, 1]
    parts = []
    for q, plane in enumerate((d0 - d2, d1 + d2, d2 - d1, d1 - d3)):
        left = jnp.concatenate(split(plane.reshape(half * WIDE, C)), axis=1)
        sums = jnp.dot(
            left, weights[q * 2 * C : (q + 1) * 2 * C], preferred_element_type=jnp.float32
        )
        parts.append((sums[:, : 3 * C] + sums[:, 3 * C :]).reshape(half, WIDE, 3 * C))
    m1, m2, m3, m4 = parts

    def join(sums):
        return (
            pltpu.roll(sums[:, :, :C], 1, 1)
            + sums[:, :, C : 2 * C]
            + pltpu.roll(sums[:, :, 2 * C :], WIDE - 1, 1)
        )

    pair = [join(m1 + m2 + m3)[:, None], join(m2 - m3 - m4)[:, None]]
    return jnp.concatenate(pair, axis=1).reshape(rows, WIDE, C)


def rows_kernel(
    state, weight, syndromes, erased, readers, up, down, copies, rows_sem, copies_sem
):
    moves = [
        pltpu.make_async_copy(state.at[pl.ds(0, HALO)], up.at[pl.ds(0, HALO)], rows_sem.at[0]),
        pltpu.make_async_copy(
            state.at[pl.ds(TR - HALO, HALO)], down.at[pl.ds(0, HALO)], rows_sem.at[1]
        ),
    ]
    moves += [
        pltpu.make_async_copy(weight, copies.at[i], copies_sem.at[i]) for i in range(16)
    ]
    for move in moves:
        move.start()
    ids = readers[...].astype(jnp.float32)
    for pay, row, block_row in ((up, 0, 0), (down, TR - 1, TR // BS - 1)):
        pay[HALO] = jnp.zeros((TC, C), jnp.float32)
        pay[HALO, 0:1, :TC] = syndromes[0, row : row + 1, :].astype(jnp.float32)
        pay[HALO, 1:2, : TC // BS] = erased[0, block_row : block_row + 1, :].astype(
            jnp.float32
        )
        first = block_row * (TC // BS)
        pay[HALO, 2:3, :] = pltpu.roll(ids, (C - first) % C, 1)
    for move in moves:
        move.wait()


def repeat_blocks(blocks, rows):
    count = blocks.shape[0]
    row = lax.broadcasted_iota(jnp.int32, (rows, count), 0)
    tall = (row // BS == lax.broadcasted_iota(jnp.int32, (rows, count), 1)).astype(jnp.bfloat16)
    col = lax.broadcasted_iota(jnp.int32, (TC // BS, TC), 1)
    wide = (col // BS == lax.broadcasted_iota(jnp.int32, (TC // BS, TC), 0)).astype(jnp.bfloat16)
    half = jnp.dot(tall, blocks.astype(jnp.bfloat16), preferred_element_type=jnp.float32)
    return jnp.dot(half.astype(jnp.bfloat16), wide, preferred_element_type=jnp.float32)


def embed(code, table, lost_vector):
    return jnp.where(
        code > 1.5, lost_vector, jnp.where(code > 0.5, table[1:2], table[0:1])
    )


def cols_kernel(
    state,
    top,
    bottom,
    syndromes,
    erased,
    readers,
    table,
    lost_vector,
    west,
    east,
    code_out,
    lost_out,
    ids_out,
    vectors,
):
    f32 = jnp.float32
    block_rows, block_cols = TR // BS, TC // BS
    lost_out[...] = jnp.zeros((16, C), f32)
    ids_out[...] = jnp.zeros((16, C), f32)
    code_out[...] = jnp.zeros((TALL, TC), f32)
    lost_out[0:1, :block_cols] = top[HALO, 1:2, :block_cols]
    lost_out[BROWS - 1 : BROWS, :block_cols] = bottom[HALO, 1:2, :block_cols]
    lost_out[1 : 1 + block_rows, :block_cols] = erased[0].astype(f32)
    lane = lax.broadcasted_iota(jnp.int32, (1, C), 1)
    ids_out[0:1, :] = jnp.where(lane < block_cols, top[HALO, 2:3, :], 0.0)
    ids_out[BROWS - 1 : BROWS, :] = jnp.where(lane < block_cols, bottom[HALO, 2:3, :], 0.0)
    ids = readers[...].astype(f32)
    for k in range(block_rows):
        turned = pltpu.roll(ids, (C - k * block_cols) % C, 1)
        ids_out[k + 1 : k + 2, :] = jnp.where(lane < block_cols, turned, 0.0)
    code_out[HALO - 1 : HALO, :] = top[HALO, 0:1, :TC]
    code_out[HALO : HALO + TR, :] = syndromes[0].astype(f32)
    code_out[HALO + TR : HALO + TR + 1, :] = bottom[HALO, 0:1, :TC]
    sites = repeat_blocks(lost_out[:, :block_cols], TALL)
    code_out[...] = jnp.where(sites > 0.5, 2.0, code_out[...])
    sub = lax.broadcasted_iota(jnp.int32, (8, C), 0)
    for pay, edge, keep, at in ((west, 0, sub < 4, 4), (east, TC - 1, sub >= 4, 0)):
        block = edge // BS
        group = edge // 8 * 8
        code = jnp.broadcast_to(code_out[:, edge : edge + 1], (TALL, C))
        vectors[:TALL] = embed(code, table, lost_vector[...])
        vectors[TALL : TALL + 16] = jnp.broadcast_to(lost_out[:, block : block + 1], (16, C))
        vectors[TALL + 16 :] = jnp.broadcast_to(ids_out[:, block : block + 1], (16, C))
        _, second, third = (4, 5, 6) if at == 4 else (3, 2, 1)
        for r in range(TALL):
            if r < HALO:
                cells = top[r, group : group + 8]
            elif r < HALO + TR:
                cells = state[r - HALO, group : group + 8]
            else:
                cells = bottom[r - HALO - TR, group : group + 8]
            extra = jnp.broadcast_to(vectors[r : r + 1], (8, C))
            if r < BROWS:
                flag = jnp.broadcast_to(vectors[TALL + r : TALL + r + 1], (8, C))
                name = jnp.broadcast_to(vectors[TALL + 16 + r : TALL + 17 + r], (8, C))
                extra = jnp.where(sub == second, flag, jnp.where(sub == third, name, extra))
            pay[r] = jnp.where(keep, cells, extra)


def slots_of(ids, gx, gy):
    mz, my, mx, mc = gx >> 2, gx & 3, gy >> 1, gy & 1
    z, y, x, c = ids >> 5, (ids >> 3) & 3, (ids >> 1) & 3, ids & 1
    side = ((x + z + mx + mz) & 1) + 2 * ((y + z + my + mz) & 1)
    return (((c + mc) & 1) * 4 + side) * 16 + z * 4 + (y >> 1) * 2 + (x >> 1)


def prepare_kernel(
    me,
    taps,
    code,
    syndromes,
    erased,
    table,
    lost_vector,
    first_out,
    second_out,
    weights_out,
    codes,
    turned,
):
    f32 = jnp.float32
    for b in range(3):
        g0, g1, g2 = taps[b], taps[3 + b], taps[6 + b]
        mixed = (g0, (g0 + g1 + g2) * 0.5, (g0 - g1 + g2) * 0.5, g2)
        for q in range(4):
            high, low = split(mixed[q])
            top, mid, end = 2 * q * C, (2 * q + 1) * C, (2 * q + 2) * C
            cols = slice(b * C, (b + 1) * C)
            lows = slice((3 + b) * C, (4 + b) * C)
            weights_out[top:mid, cols] = high
            weights_out[top:mid, lows] = low
            weights_out[mid:end, cols] = high
            weights_out[mid:end, lows] = jnp.zeros((C, C), jnp.bfloat16)
    codes[...] = jnp.zeros((C, C), f32)
    codes[:TALL, :TC] = code[...]
    second = repeat_blocks(erased[1].astype(f32), TR)
    codes[TALL : TALL + TR, :TC] = jnp.where(second > 0.5, 2.0, syndromes[1].astype(f32))
    turned[...] = codes[...].T
    values, vector = table[...], lost_vector[...]
    for r in range(HALO - 1, HALO + TR + 1):
        column = jnp.broadcast_to(turned[:TC, r : r + 1], (TC, C))
        first_out[r - HALO + 1] = embed(column, values, vector)
    for r in range(TR):
        column = jnp.broadcast_to(turned[:TC, TALL + r : TALL + r + 1], (TC, C))
        second_out[r] = embed(column, values, vector)


def first_kernel(
    me,
    state,
    top,
    bottom,
    right,
    left,
    inputs,
    weights,
    lost,
    ids,
    erased,
    ext_out,
    pre_out,
    slots_out,
    names,
):
    f32 = jnp.float32
    sub = lax.broadcasted_iota(jnp.int32, (8, C), 0)
    ext_out[HALO : HALO + TR, :TC] = state[...]
    ext_out[:HALO, :TC] = top[:HALO]
    ext_out[HALO + TR :, :TC] = bottom[:HALO]
    for r in range(TALL):
        ext_out[r, TC:] = jnp.where(sub < 4, right[r], left[r])

    names[...] = jnp.zeros((64, C), f32)
    for r in range(BROWS):
        names[r : r + 1] = right[r, 5:6, :]
        names[16 + r : 17 + r] = left[r, 2:3, :]
        names[32 + r : 33 + r] = right[r, 6:7, :]
        names[48 + r : 49 + r] = left[r, 1:2, :]
    lane = lax.broadcasted_iota(jnp.int32, (16, C), 1)
    wide = TC // BS

    def widen(mid, at):
        return jnp.where(
            lane < wide,
            mid,
            jnp.where(
                lane == wide,
                names[at : at + 16],
                jnp.where(lane == wide + 1, names[at + 16 : at + 32], 0.0),
            ),
        ).astype(jnp.int32)

    slots_out[...] = slots_of(widen(ids[...], 32) & 127, me[0], me[1]) + 128 * widen(
        lost[...], 0
    )
    slots_out[1 : 1 + TR // BS, :wide] += 256 * erased[1]

    pre_out[0] = jnp.zeros((WIDE, C), f32)
    pre_out[CONV_ROWS - 1] = jnp.zeros((WIDE, C), f32)
    pre_out[1 : CONV_ROWS - 1, :TC] = inputs[...]
    for r in range(HALO - 1, HALO + TR + 1):
        pre_out[r - 2, TC:] = jnp.where(
            sub == 0,
            pltpu.roll(right[r], 4, 0),
            jnp.where(sub == 7, pltpu.roll(left[r], 4, 0), 0.0),
        )
    rows = CONV_ROWS

    def step(i, carry):
        start = i * rows
        pre_out[pl.ds(start, rows)] += conv_chunk(
            ext_out[pl.ds(start + 1, rows + 2)], weights, rows
        )
        return carry

    lax.fori_loop(0, CONV_ROWS // rows, step, 0)


def group_sum(total, sub):
    near = jnp.where(sub % 2 == 0, pltpu.roll(total, 7, 0), pltpu.roll(total, 1, 0))
    total = total + near
    far = jnp.where(sub % 4 < 2, pltpu.roll(total, 6, 0), pltpu.roll(total, 2, 0))
    return total + far


def readout(sites, right, flag_a, flag_b, offset, sub):
    high, low = split(sites.reshape(32, C))
    left = jnp.concatenate(
        [jnp.concatenate([high, high], axis=1), jnp.concatenate([low, low], axis=1)],
        axis=0,
    )
    mixed = jnp.dot(left, right, preferred_element_type=jnp.float32)
    mixed = (mixed[:32] + mixed[32:]).reshape(4, 8, 2 * C)
    mixed = jnp.tanh(jnp.where(sub[None] < 4, mixed[:, :, :C], mixed[:, :, C:]))
    total = mixed[0] + mixed[1] + mixed[2] + mixed[3]
    flags = jnp.where(sub < 4, flag_a, flag_b)
    return jnp.tanh(group_sum(total, sub) * 0.0625 + flags * offset)


PIECES = (16, 8, 8, 8, 8, 8, 8) * 2


def second_kernel(
    slots, me, offset, ext_hbm, pre_hbm, inputs_hbm, weights_hbm, *rest
):
    pieces = rest[:14]
    out, table, first, field, second, ext, pre, inputs, weights, sems = rest[14:]
    later = [
        pltpu.make_async_copy(ext_hbm, ext, sems.at[0]),
        pltpu.make_async_copy(pre_hbm, pre, sems.at[1]),
        pltpu.make_async_copy(weights_hbm, weights, sems.at[2]),
        pltpu.make_async_copy(inputs_hbm, inputs, sems.at[3]),
    ]
    for copy in later:
        copy.start()
    at = 0
    for piece, count in zip(pieces, PIECES):

        def halve(i, carry, piece=piece, at=at):
            for k in range(4):
                high, low = split(piece[4 * i + k])
                table[at + 4 * i + k, :C] = high
                table[at + 4 * i + k, C:] = low
            return carry

        lax.fori_loop(0, count // 4, halve, 0)
        at += count
    later[0].wait()
    sub = lax.broadcasted_iota(jnp.int32, (8, C), 0)
    shift = offset[...]

    def read_first(step, carry):
        for br, g in [(10 * step + k, g) for k in range(10) for g in range(GROUPS)]:
            one, two = slots[br, 2 * g], slots[br, 2 * g + 1]
            first[br, 8 * g : 8 * g + 8] = readout(
                ext[pl.ds(br * BS, BS), 8 * g : 8 * g + 8],
                jnp.concatenate([table[one & 127], table[two & 127]], axis=1),
                ((one >> 7) & 1).astype(jnp.float32),
                ((two >> 7) & 1).astype(jnp.float32),
                shift,
                sub,
            )
        return carry

    read_first(0, 0)

    later[1].wait()

    def update(row, br):
        field[row + 1] = 0.5 * ext[row + HALO] + jnp.tanh(pre[row + 2] + first[br])

    update(-1, 0)
    update(TR, BROWS - 1)

    def update_block(br, carry):
        for r in range(BS):
            update(br * BS + r, br + 1)
        return carry

    lax.fori_loop(0, TR // BS, update_block, 0)
    field[0] = field[0] * (me[0] > 0).astype(jnp.float32)
    field[TR + 1] = field[TR + 1] * (me[0] < me[2]).astype(jnp.float32)
    edge = lax.broadcasted_iota(jnp.int32, (TR + 2, 8, C), 1)
    kept = jnp.where(
        edge < 4, (me[1] < me[3]).astype(jnp.float32), (me[1] > 0).astype(jnp.float32)
    )
    field[:, TC:] = field[:, TC:] * kept

    def read_second(step, carry):
        for br, g in [(8 * step + k, g) for k in range(8) for g in range(TC // 8)]:
            one, two = slots[br + 1, 2 * g], slots[br + 1, 2 * g + 1]
            second[br, 8 * g : 8 * g + 8] = readout(
                field[pl.ds(br * BS + 1, BS), 8 * g : 8 * g + 8],
                jnp.concatenate([table[one & 127], table[two & 127]], axis=1),
                (one >> 8).astype(jnp.float32),
                (two >> 8).astype(jnp.float32),
                shift,
                sub,
            )
        return carry

    read_second(0, 0)
    later[2].wait()
    later[3].wait()
    rows = TR

    def finish(i, carry):
        start = i * rows
        sums = conv_chunk(field[pl.ds(start, rows + 2)], weights, rows)[:, :TC]
        for half in range(rows // BS):
            at = start + half * BS
            out[pl.ds(at, BS)] = 0.5 * field[pl.ds(at + 1, BS), :TC] + jnp.tanh(
                sums[half * BS : (half + 1) * BS]
                + inputs[pl.ds(at, BS)]
                + second[i * (rows // BS) + half][None]
            )
        return carry

    lax.fori_loop(0, TR // rows, finish, 0)


def decode(
    state,
    syndromes,
    erased,
    readers,
    conv_weight,
    syndrome_table,
    erasure_vector,
    read_weight,
    erasure_offset,
):
    f32 = jnp.float32
    gx, gy = lax.axis_index("gx"), lax.axis_index("gy")
    gx_count, gy_count = lax.axis_size("gx"), lax.axis_size("gy")
    me = jnp.stack([gx, gy, gx_count - 1, gy_count - 1]).astype(jnp.int32)
    names = readers.reshape(1, -1)
    lost_vector, offset = erasure_vector[None], erasure_offset[None]
    vmem = pl.BlockSpec(memory_space=pltpu.VMEM)
    smem = pl.BlockSpec(memory_space=pltpu.SMEM)
    anywhere = pl.BlockSpec(memory_space=pl.ANY)
    hbm = pl.BlockSpec(memory_space=pltpu.HBM)

    def shape(*dims, dtype=f32):
        return jax.ShapeDtypeStruct(dims, dtype)

    up_pay, down_pay, copies = pl.pallas_call(
        rows_kernel,
        name="pack_rows",
        out_shape=(
            shape(HALO + 1, TC, C),
            shape(HALO + 1, TC, C),
            shape(16, C, C),
        ),
        in_specs=[anywhere, vmem, vmem, vmem, vmem],
        out_specs=(vmem, vmem, anywhere),
        scratch_shapes=[pltpu.SemaphoreType.DMA((2,)), pltpu.SemaphoreType.DMA((16,))],
    )(state, read_weight, syndromes, erased, names)

    up = [(i, i - 1) for i in range(1, gx_count)]
    down = [(i, i + 1) for i in range(gx_count - 1)]
    top = lax.ppermute(down_pay, "gx", down)
    bottom = lax.ppermute(up_pay, "gx", up)

    west_pay, east_pay, code, lost, ids = pl.pallas_call(
        cols_kernel,
        name="pack_cols",
        out_shape=(
            shape(TALL, 8, C),
            shape(TALL, 8, C),
            shape(TALL, TC),
            shape(16, C),
            shape(16, C),
        ),
        in_specs=[vmem] * 8,
        out_specs=(vmem,) * 5,
        scratch_shapes=[pltpu.VMEM((TALL + 32, C), f32)],
    )(state, top, bottom, syndromes, erased, names, syndrome_table, lost_vector)

    west = [(i, i - 1) for i in range(1, gy_count)]
    east = [(i, i + 1) for i in range(gy_count - 1)]
    left = lax.ppermute(east_pay, "gy", east)
    right = lax.ppermute(west_pay, "gy", west)
    pieces = gather_weights(copies)

    inputs_first, inputs, weights = pl.pallas_call(
        prepare_kernel,
        name="prepare",
        compiler_params=pltpu.CompilerParams(vmem_limit_bytes=60 * 2**20),
        out_shape=(shape(TR + 2, TC, C), shape(TR, TC, C), shape(8 * C, 6 * C, dtype=jnp.bfloat16)),
        in_specs=[smem] + [vmem] * 6,
        out_specs=(vmem,) * 3,
        scratch_shapes=[pltpu.VMEM((C, C), f32), pltpu.VMEM((C, C), f32)],
    )(me, conv_weight, code, syndromes, erased, syndrome_table, lost_vector)

    ext, pre, slots = pl.pallas_call(
        first_kernel,
        name="conv_first",
        compiler_params=pltpu.CompilerParams(vmem_limit_bytes=60 * 2**20),
        out_shape=(shape(TALL, WIDE, C), shape(CONV_ROWS, WIDE, C), shape(16, C, dtype=jnp.int32)),
        in_specs=[smem] + [vmem] * 10,
        out_specs=(vmem,) * 3,
        scratch_shapes=[pltpu.VMEM((64, C), f32)],
        cost_estimate=pl.CostEstimate(
            flops=2_000_000_000, bytes_accessed=6_000_000, transcendentals=0
        ),
    )(me, state, top, bottom, right, left, inputs_first, weights, lost, ids, erased)

    return pl.pallas_call(
        second_kernel,
        name="read_and_finish",
        compiler_params=pltpu.CompilerParams(vmem_limit_bytes=44 * 2**20),
        out_shape=shape(TR, TC, C),
        in_specs=[smem] * 2 + [vmem] + [hbm] * 4 + [vmem] * 14,
        out_specs=vmem,
        scratch_shapes=[
            pltpu.VMEM((128, 2 * C, C), jnp.bfloat16),
            pltpu.VMEM((BROWS, WIDE, C), f32),
            pltpu.VMEM((TR + 2, WIDE, C), f32),
            pltpu.VMEM((TR // BS, TC, C), f32),
            pltpu.VMEM((TALL, WIDE, C), f32),
            pltpu.VMEM((CONV_ROWS, WIDE, C), f32),
            pltpu.VMEM((TR, TC, C), f32),
            pltpu.VMEM((8 * C, 6 * C), jnp.bfloat16),
            pltpu.SemaphoreType.DMA((4,)),
        ],
        cost_estimate=pl.CostEstimate(
            flops=4_000_000_000, bytes_accessed=12_000_000, transcendentals=1_000_000
        ),
    )(slots, me, offset, ext, pre, inputs, weights, *pieces)


def solution(mesh):
    placed = (
        P("gx", "gy", None),
        P(None, "gx", "gy"),
        P(None, "gx", "gy"),
        P(("gx", "gy"), None),
        P(),
        P(),
        P(),
        P(("gx", "gy"), None),
        P(),
    )
    return jax.shard_map(
        decode, mesh=mesh, in_specs=placed, out_specs=P("gx", "gy", None), check_vma=False
    )
```

```python
import jax
import jax.numpy as jnp
from jax import lax
from jax.experimental import pallas as pl
from jax.experimental.pallas import tpu as pltpu
from jax.sharding import PartitionSpec as P


BS = 4
C = 128
TR = 32
TC = 64
HALO = 4
WIDE = TC + 2 * HALO
TALL = TR + 2 * HALO
BROWS = TALL // BS
GROUPS = WIDE // 8
CONV_ROWS = TR + 4
AX = ("gx", "gy")


def flat_id(z, y, x, c):
    return ((z % 4 * 4 + y % 4) * 4 + x % 4) * 2 + c


SITES = [
    (z, y, x, c) for z in range(4) for y in range(4) for x in range(4) for c in range(2)
]


def class_groups():
    groups = {}
    for z, y, x, c in SITES:
        groups.setdefault(((x + z) % 2, (y + z) % 2, c), []).append(flat_id(z, y, x, c))
    return [groups[k] for k in sorted(groups)]


def moved(dz, dy, dx):
    return [
        (flat_id(z, y, x, c), flat_id(z + dz, y + dy, x + dx, c)) for z, y, x, c in SITES
    ]


PARTNER = [(flat_id(z, y, x, c), flat_id(z, y, x, 1 - c)) for z, y, x, c in SITES]


def gather_weights(copies):
    own = lax.all_to_all(copies, AX, 0, 0, tiled=True, axis_index_groups=class_groups())
    low, high = own[:8], own[8:]
    pieces = [own]
    for step in ((0, 0, 1), (0, 1, 0), (1, 0, 0)):
        back = tuple(-s for s in step)
        pieces.append(lax.ppermute(low, AX, moved(*step)))
        pieces.append(lax.ppermute(high, AX, moved(*back)))
    swapped = [lax.ppermute(own, AX, PARTNER)]
    swapped += [lax.ppermute(piece, AX, PARTNER) for piece in pieces[1:]]
    return pieces + swapped


def split(value):
    high = value.astype(jnp.bfloat16)
    return high, (value - high.astype(jnp.float32)).astype(jnp.bfloat16)


def conv_chunk(cells, weights, rows):
    half = rows // 2
    paired = cells.reshape(half + 1, 2, WIDE, C)
    d0, d1, d2, d3 = paired[:half, 0], paired[:half, 1], paired[1:, 0], paired[1:, 1]
    parts = []
    for q, plane in enumerate((d0 - d2, d1 + d2, d2 - d1, d1 - d3)):
        left = jnp.concatenate(split(plane.reshape(half * WIDE, C)), axis=1)
        sums = jnp.dot(
            left, weights[q * 2 * C : (q + 1) * 2 * C], preferred_element_type=jnp.float32
        )
        parts.append((sums[:, : 3 * C] + sums[:, 3 * C :]).reshape(half, WIDE, 3 * C))
    m1, m2, m3, m4 = parts

    def join(sums):
        return (
            pltpu.roll(sums[:, :, :C], 1, 1)
            + sums[:, :, C : 2 * C]
            + pltpu.roll(sums[:, :, 2 * C :], WIDE - 1, 1)
        )

    pair = [join(m1 + m2 + m3)[:, None], join(m2 - m3 - m4)[:, None]]
    return jnp.concatenate(pair, axis=1).reshape(rows, WIDE, C)


def rows_kernel(
    state, weight, syndromes, erased, readers, up, down, copies, rows_sem, copies_sem
):
    moves = [
        pltpu.make_async_copy(state.at[pl.ds(0, HALO)], up.at[pl.ds(0, HALO)], rows_sem.at[0]),
        pltpu.make_async_copy(
            state.at[pl.ds(TR - HALO, HALO)], down.at[pl.ds(0, HALO)], rows_sem.at[1]
        ),
    ]
    moves += [
        pltpu.make_async_copy(weight, copies.at[i], copies_sem.at[i]) for i in range(16)
    ]
    for move in moves:
        move.start()
    ids = readers[...].astype(jnp.float32)
    for pay, row, block_row in ((up, 0, 0), (down, TR - 1, TR // BS - 1)):
        pay[HALO] = jnp.zeros((TC, C), jnp.float32)
        pay[HALO, 0:1, :TC] = syndromes[0, row : row + 1, :].astype(jnp.float32)
        pay[HALO, 1:2, : TC // BS] = erased[0, block_row : block_row + 1, :].astype(
            jnp.float32
        )
        first = block_row * (TC // BS)
        pay[HALO, 2:3, :] = pltpu.roll(ids, (C - first) % C, 1)
    for move in moves:
        move.wait()


def repeat_blocks(blocks, rows):
    count = blocks.shape[0]
    row = lax.broadcasted_iota(jnp.int32, (rows, count), 0)
    tall = (row // BS == lax.broadcasted_iota(jnp.int32, (rows, count), 1)).astype(jnp.bfloat16)
    col = lax.broadcasted_iota(jnp.int32, (TC // BS, TC), 1)
    wide = (col // BS == lax.broadcasted_iota(jnp.int32, (TC // BS, TC), 0)).astype(jnp.bfloat16)
    half = jnp.dot(tall, blocks.astype(jnp.bfloat16), preferred_element_type=jnp.float32)
    return jnp.dot(half.astype(jnp.bfloat16), wide, preferred_element_type=jnp.float32)


def embed(code, table, lost_vector):
    return jnp.where(
        code > 1.5, lost_vector, jnp.where(code > 0.5, table[1:2], table[0:1])
    )


def cols_kernel(
    state,
    top,
    bottom,
    syndromes,
    erased,
    readers,
    table,
    lost_vector,
    west,
    east,
    code_out,
    lost_out,
    ids_out,
    vectors,
):
    f32 = jnp.float32
    block_rows, block_cols = TR // BS, TC // BS
    lost_out[...] = jnp.zeros((16, C), f32)
    ids_out[...] = jnp.zeros((16, C), f32)
    code_out[...] = jnp.zeros((TALL, TC), f32)
    lost_out[0:1, :block_cols] = top[HALO, 1:2, :block_cols]
    lost_out[BROWS - 1 : BROWS, :block_cols] = bottom[HALO, 1:2, :block_cols]
    lost_out[1 : 1 + block_rows, :block_cols] = erased[0].astype(f32)
    lane = lax.broadcasted_iota(jnp.int32, (1, C), 1)
    ids_out[0:1, :] = jnp.where(lane < block_cols, top[HALO, 2:3, :], 0.0)
    ids_out[BROWS - 1 : BROWS, :] = jnp.where(lane < block_cols, bottom[HALO, 2:3, :], 0.0)
    ids = readers[...].astype(f32)
    for k in range(block_rows):
        turned = pltpu.roll(ids, (C - k * block_cols) % C, 1)
        ids_out[k + 1 : k + 2, :] = jnp.where(lane < block_cols, turned, 0.0)
    code_out[HALO - 1 : HALO, :] = top[HALO, 0:1, :TC]
    code_out[HALO : HALO + TR, :] = syndromes[0].astype(f32)
    code_out[HALO + TR : HALO + TR + 1, :] = bottom[HALO, 0:1, :TC]
    sites = repeat_blocks(lost_out[:, :block_cols], TALL)
    code_out[...] = jnp.where(sites > 0.5, 2.0, code_out[...])
    sub = lax.broadcasted_iota(jnp.int32, (8, C), 0)
    for pay, edge, keep, at in ((west, 0, sub < 4, 4), (east, TC - 1, sub >= 4, 0)):
        block = edge // BS
        group = edge // 8 * 8
        code = jnp.broadcast_to(code_out[:, edge : edge + 1], (TALL, C))
        vectors[:TALL] = embed(code, table, lost_vector[...])
        vectors[TALL : TALL + 16] = jnp.broadcast_to(lost_out[:, block : block + 1], (16, C))
        vectors[TALL + 16 :] = jnp.broadcast_to(ids_out[:, block : block + 1], (16, C))
        _, second, third = (4, 5, 6) if at == 4 else (3, 2, 1)
        for r in range(TALL):
            if r < HALO:
                cells = top[r, group : group + 8]
            elif r < HALO + TR:
                cells = state[r - HALO, group : group + 8]
            else:
                cells = bottom[r - HALO - TR, group : group + 8]
            extra = jnp.broadcast_to(vectors[r : r + 1], (8, C))
            if r < BROWS:
                flag = jnp.broadcast_to(vectors[TALL + r : TALL + r + 1], (8, C))
                name = jnp.broadcast_to(vectors[TALL + 16 + r : TALL + 17 + r], (8, C))
                extra = jnp.where(sub == second, flag, jnp.where(sub == third, name, extra))
            pay[r] = jnp.where(keep, cells, extra)


def slots_of(ids, gx, gy):
    mz, my, mx, mc = gx >> 2, gx & 3, gy >> 1, gy & 1
    z, y, x, c = ids >> 5, (ids >> 3) & 3, (ids >> 1) & 3, ids & 1
    side = ((x + z + mx + mz) & 1) + 2 * ((y + z + my + mz) & 1)
    return (((c + mc) & 1) * 4 + side) * 16 + z * 4 + (y >> 1) * 2 + (x >> 1)


def prepare_kernel(
    me,
    taps,
    code,
    syndromes,
    erased,
    table,
    lost_vector,
    first_out,
    second_out,
    weights_out,
    codes,
    turned,
):
    f32 = jnp.float32
    for b in range(3):
        g0, g1, g2 = taps[b], taps[3 + b], taps[6 + b]
        mixed = (g0, (g0 + g1 + g2) * 0.5, (g0 - g1 + g2) * 0.5, g2)
        for q in range(4):
            high, low = split(mixed[q])
            top, mid, end = 2 * q * C, (2 * q + 1) * C, (2 * q + 2) * C
            cols = slice(b * C, (b + 1) * C)
            lows = slice((3 + b) * C, (4 + b) * C)
            weights_out[top:mid, cols] = high
            weights_out[top:mid, lows] = low
            weights_out[mid:end, cols] = high
            weights_out[mid:end, lows] = jnp.zeros((C, C), jnp.bfloat16)
    codes[...] = jnp.zeros((C, C), f32)
    codes[:TALL, :TC] = code[...]
    second = repeat_blocks(erased[1].astype(f32), TR)
    codes[TALL : TALL + TR, :TC] = jnp.where(second > 0.5, 2.0, syndromes[1].astype(f32))
    turned[...] = codes[...].T
    values, vector = table[...], lost_vector[...]
    for r in range(HALO - 1, HALO + TR + 1):
        column = jnp.broadcast_to(turned[:TC, r : r + 1], (TC, C))
        first_out[r - HALO + 1] = embed(column, values, vector)
    for r in range(TR):
        column = jnp.broadcast_to(turned[:TC, TALL + r : TALL + r + 1], (TC, C))
        second_out[r] = embed(column, values, vector)


def first_kernel(
    me,
    state,
    top,
    bottom,
    right,
    left,
    inputs,
    weights,
    lost,
    ids,
    erased,
    ext_out,
    pre_out,
    slots_out,
    names,
):
    f32 = jnp.float32
    sub = lax.broadcasted_iota(jnp.int32, (8, C), 0)
    ext_out[HALO : HALO + TR, :TC] = state[...]
    ext_out[:HALO, :TC] = top[:HALO]
    ext_out[HALO + TR :, :TC] = bottom[:HALO]
    for r in range(TALL):
        ext_out[r, TC:] = jnp.where(sub < 4, right[r], left[r])

    names[...] = jnp.zeros((64, C), f32)
    for r in range(BROWS):
        names[r : r + 1] = right[r, 5:6, :]
        names[16 + r : 17 + r] = left[r, 2:3, :]
        names[32 + r : 33 + r] = right[r, 6:7, :]
        names[48 + r : 49 + r] = left[r, 1:2, :]
    lane = lax.broadcasted_iota(jnp.int32, (16, C), 1)
    wide = TC // BS

    def widen(mid, at):
        return jnp.where(
            lane < wide,
            mid,
            jnp.where(
                lane == wide,
                names[at : at + 16],
                jnp.where(lane == wide + 1, names[at + 16 : at + 32], 0.0),
            ),
        ).astype(jnp.int32)

    slots_out[...] = slots_of(widen(ids[...], 32) & 127, me[0], me[1]) + 128 * widen(
        lost[...], 0
    )
    slots_out[1 : 1 + TR // BS, :wide] += 256 * erased[1]

    pre_out[0] = jnp.zeros((WIDE, C), f32)
    pre_out[CONV_ROWS - 1] = jnp.zeros((WIDE, C), f32)
    pre_out[1 : CONV_ROWS - 1, :TC] = inputs[...]
    for r in range(HALO - 1, HALO + TR + 1):
        pre_out[r - 2, TC:] = jnp.where(
            sub == 0,
            pltpu.roll(right[r], 4, 0),
            jnp.where(sub == 7, pltpu.roll(left[r], 4, 0), 0.0),
        )
    rows = CONV_ROWS

    def step(i, carry):
        start = i * rows
        pre_out[pl.ds(start, rows)] += conv_chunk(
            ext_out[pl.ds(start + 1, rows + 2)], weights, rows
        )
        return carry

    lax.fori_loop(0, CONV_ROWS // rows, step, 0)


def group_sum(total, sub):
    near = jnp.where(sub % 2 == 0, pltpu.roll(total, 7, 0), pltpu.roll(total, 1, 0))
    total = total + near
    far = jnp.where(sub % 4 < 2, pltpu.roll(total, 6, 0), pltpu.roll(total, 2, 0))
    return total + far


def readout(sites, right, flag_a, flag_b, offset, sub):
    high, low = split(sites.reshape(32, C))
    left = jnp.concatenate(
        [jnp.concatenate([high, high], axis=1), jnp.concatenate([low, low], axis=1)],
        axis=0,
    )
    mixed = jnp.dot(left, right, preferred_element_type=jnp.float32)
    mixed = (mixed[:32] + mixed[32:]).reshape(4, 8, 2 * C)
    mixed = jnp.tanh(jnp.where(sub[None] < 4, mixed[:, :, :C], mixed[:, :, C:]))
    total = mixed[0] + mixed[1] + mixed[2] + mixed[3]
    flags = jnp.where(sub < 4, flag_a, flag_b)
    return jnp.tanh(group_sum(total, sub) * 0.0625 + flags * offset)


PIECES = (16, 8, 8, 8, 8, 8, 8) * 2


def second_kernel(
    slots, me, offset, ext_hbm, pre_hbm, inputs_hbm, weights_hbm, *rest
):
    pieces = rest[:14]
    out, table, first, field, second, ext, pre, inputs, weights, sems = rest[14:]
    later = [
        pltpu.make_async_copy(ext_hbm, ext, sems.at[0]),
        pltpu.make_async_copy(pre_hbm, pre, sems.at[1]),
        pltpu.make_async_copy(weights_hbm, weights, sems.at[2]),
        pltpu.make_async_copy(inputs_hbm, inputs, sems.at[3]),
    ]
    for copy in later:
        copy.start()
    at = 0
    for piece, count in zip(pieces, PIECES):

        def halve(i, carry, piece=piece, at=at):
            for k in range(4):
                high, low = split(piece[4 * i + k])
                table[at + 4 * i + k, :C] = high
                table[at + 4 * i + k, C:] = low
            return carry

        lax.fori_loop(0, count // 4, halve, 0)
        at += count
    later[0].wait()
    sub = lax.broadcasted_iota(jnp.int32, (8, C), 0)
    shift = offset[...]

    def read_first(step, carry):
        for br, g in [(10 * step + k, g) for k in range(10) for g in range(GROUPS)]:
            one, two = slots[br, 2 * g], slots[br, 2 * g + 1]
            first[br, 8 * g : 8 * g + 8] = readout(
                ext[pl.ds(br * BS, BS), 8 * g : 8 * g + 8],
                jnp.concatenate([table[one & 127], table[two & 127]], axis=1),
                ((one >> 7) & 1).astype(jnp.float32),
                ((two >> 7) & 1).astype(jnp.float32),
                shift,
                sub,
            )
        return carry

    read_first(0, 0)

    later[1].wait()

    def update(row, br):
        field[row + 1] = 0.5 * ext[row + HALO] + jnp.tanh(pre[row + 2] + first[br])

    update(-1, 0)
    update(TR, BROWS - 1)

    def update_block(br, carry):
        for r in range(BS):
            update(br * BS + r, br + 1)
        return carry

    lax.fori_loop(0, TR // BS, update_block, 0)
    field[0] = field[0] * (me[0] > 0).astype(jnp.float32)
    field[TR + 1] = field[TR + 1] * (me[0] < me[2]).astype(jnp.float32)
    edge = lax.broadcasted_iota(jnp.int32, (TR + 2, 8, C), 1)
    kept = jnp.where(
        edge < 4, (me[1] < me[3]).astype(jnp.float32), (me[1] > 0).astype(jnp.float32)
    )
    field[:, TC:] = field[:, TC:] * kept

    def read_second(step, carry):
        for br, g in [(8 * step + k, g) for k in range(8) for g in range(TC // 8)]:
            one, two = slots[br + 1, 2 * g], slots[br + 1, 2 * g + 1]
            second[br, 8 * g : 8 * g + 8] = readout(
                field[pl.ds(br * BS + 1, BS), 8 * g : 8 * g + 8],
                jnp.concatenate([table[one & 127], table[two & 127]], axis=1),
                (one >> 8).astype(jnp.float32),
                (two >> 8).astype(jnp.float32),
                shift,
                sub,
            )
        return carry

    read_second(0, 0)
    later[2].wait()
    later[3].wait()
    rows = TR

    def finish(i, carry):
        start = i * rows
        sums = conv_chunk(field[pl.ds(start, rows + 2)], weights, rows)[:, :TC]
        for half in range(rows // BS):
            at = start + half * BS
            out[pl.ds(at, BS)] = 0.5 * field[pl.ds(at + 1, BS), :TC] + jnp.tanh(
                sums[half * BS : (half + 1) * BS]
                + inputs[pl.ds(at, BS)]
                + second[i * (rows // BS) + half][None]
            )
        return carry

    lax.fori_loop(0, TR // rows, finish, 0)


def decode(
    state,
    syndromes,
    erased,
    readers,
    conv_weight,
    syndrome_table,
    erasure_vector,
    read_weight,
    erasure_offset,
):
    f32 = jnp.float32
    gx, gy = lax.axis_index("gx"), lax.axis_index("gy")
    gx_count, gy_count = lax.axis_size("gx"), lax.axis_size("gy")
    me = jnp.stack([gx, gy, gx_count - 1, gy_count - 1]).astype(jnp.int32)
    names = readers.reshape(1, -1)
    lost_vector, offset = erasure_vector[None], erasure_offset[None]
    vmem = pl.BlockSpec(memory_space=pltpu.VMEM)
    smem = pl.BlockSpec(memory_space=pltpu.SMEM)
    anywhere = pl.BlockSpec(memory_space=pl.ANY)
    hbm = pl.BlockSpec(memory_space=pltpu.HBM)

    def shape(*dims, dtype=f32):
        return jax.ShapeDtypeStruct(dims, dtype)

    up_pay, down_pay, copies = pl.pallas_call(
        rows_kernel,
        name="pack_rows",
        out_shape=(
            shape(HALO + 1, TC, C),
            shape(HALO + 1, TC, C),
            shape(16, C, C),
        ),
        in_specs=[anywhere, vmem, vmem, vmem, vmem],
        out_specs=(vmem, vmem, anywhere),
        scratch_shapes=[pltpu.SemaphoreType.DMA((2,)), pltpu.SemaphoreType.DMA((16,))],
    )(state, read_weight, syndromes, erased, names)

    up = [(i, i - 1) for i in range(1, gx_count)]
    down = [(i, i + 1) for i in range(gx_count - 1)]
    top = lax.ppermute(down_pay, "gx", down)
    bottom = lax.ppermute(up_pay, "gx", up)

    west_pay, east_pay, code, lost, ids = pl.pallas_call(
        cols_kernel,
        name="pack_cols",
        out_shape=(
            shape(TALL, 8, C),
            shape(TALL, 8, C),
            shape(TALL, TC),
            shape(16, C),
            shape(16, C),
        ),
        in_specs=[vmem] * 8,
        out_specs=(vmem,) * 5,
        scratch_shapes=[pltpu.VMEM((TALL + 32, C), f32)],
    )(state, top, bottom, syndromes, erased, names, syndrome_table, lost_vector)

    west = [(i, i - 1) for i in range(1, gy_count)]
    east = [(i, i + 1) for i in range(gy_count - 1)]
    left = lax.ppermute(east_pay, "gy", east)
    right = lax.ppermute(west_pay, "gy", west)
    pieces = gather_weights(copies)

    inputs_first, inputs, weights = pl.pallas_call(
        prepare_kernel,
        name="prepare",
        compiler_params=pltpu.CompilerParams(vmem_limit_bytes=60 * 2**20),
        out_shape=(shape(TR + 2, TC, C), shape(TR, TC, C), shape(8 * C, 6 * C, dtype=jnp.bfloat16)),
        in_specs=[smem] + [vmem] * 6,
        out_specs=(vmem,) * 3,
        scratch_shapes=[pltpu.VMEM((C, C), f32), pltpu.VMEM((C, C), f32)],
    )(me, conv_weight, code, syndromes, erased, syndrome_table, lost_vector)

    ext, pre, slots = pl.pallas_call(
        first_kernel,
        name="conv_first",
        compiler_params=pltpu.CompilerParams(vmem_limit_bytes=60 * 2**20),
        out_shape=(shape(TALL, WIDE, C), shape(CONV_ROWS, WIDE, C), shape(16, C, dtype=jnp.int32)),
        in_specs=[smem] + [vmem] * 10,
        out_specs=(vmem,) * 3,
        scratch_shapes=[pltpu.VMEM((64, C), f32)],
        cost_estimate=pl.CostEstimate(
            flops=2_000_000_000, bytes_accessed=6_000_000, transcendentals=0
        ),
    )(me, state, top, bottom, right, left, inputs_first, weights, lost, ids, erased)

    return pl.pallas_call(
        second_kernel,
        name="read_and_finish",
        compiler_params=pltpu.CompilerParams(vmem_limit_bytes=44 * 2**20),
        out_shape=shape(TR, TC, C),
        in_specs=[smem] * 2 + [vmem] + [hbm] * 4 + [vmem] * 14,
        out_specs=vmem,
        scratch_shapes=[
            pltpu.VMEM((128, 2 * C, C), jnp.bfloat16),
            pltpu.VMEM((BROWS, WIDE, C), f32),
            pltpu.VMEM((TR + 2, WIDE, C), f32),
            pltpu.VMEM((TR // BS, TC, C), f32),
            pltpu.VMEM((TALL, WIDE, C), f32),
            pltpu.VMEM((CONV_ROWS, WIDE, C), f32),
            pltpu.VMEM((TR, TC, C), f32),
            pltpu.VMEM((8 * C, 6 * C), jnp.bfloat16),
            pltpu.SemaphoreType.DMA((4,)),
        ],
        cost_estimate=pl.CostEstimate(
            flops=4_000_000_000, bytes_accessed=12_000_000, transcendentals=1_000_000
        ),
    )(slots, me, offset, ext, pre, inputs, weights, *pieces)


def solution(mesh):
    placed = (
        P("gx", "gy", None),
        P(None, "gx", "gy"),
        P(None, "gx", "gy"),
        P(("gx", "gy"), None),
        P(),
        P(),
        P(),
        P(("gx", "gy"), None),
        P(),
    )
    return jax.shard_map(
        decode, mesh=mesh, in_specs=placed, out_specs=P("gx", "gy", None), check_vma=False
    )
```
